32 devices in a mesh: seq: 4 (over x, core), head: 8 (over z, y).
Axes of the slice: x: 2, y: 2, z: 4, core: 2. Of those that a mesh axis runs over, the one named last changes fastest.
Arguments:
- inner_input: bfloat16 [2048, 16384], P('seq', 'head'), may hold values from -6 to 6
- gate_input: bfloat16 [2048, 16384], P('seq', 'head'), may hold values from -48 to 48
- bc_input: bfloat16 [2048, 4096], P('seq'), may hold values from -6 to 6
- dt_input: float32 [256, 2048], P('head', 'seq'), may hold values from -11.5 to 0
- log_rate: float32 [256], P('head'), may hold values from -1.2 to 0
- skip_weight: float32 [256], P('head'), may hold values from 0.5 to 1.5
- conv_weight_x: float32 [4, 16384], P(None, 'head'), may hold values from -3 to 3
- conv_bias_x: float32 [16384], P('head'), may hold values from -3 to 3
- conv_weight_bc: float32 [4, 4096], replicated, may hold values from -3 to 3
- conv_bias_bc: float32 [4096], replicated, may hold values from -3 to 3
- conv_tail_x: bfloat16 [3, 16384], P(None, 'head'), may hold values from -6 to 6
- conv_tail_bc: bfloat16 [3, 4096], replicated, may hold values from -6 to 6
- init_state: float32 [256, 64, 256], P('head'), may hold values from -0.6 to 0.6
- norm_gain: float32 [16384], P('head'), may hold values from 0.5 to 1.5
- out_weight: bfloat16 [16384, 8192], P('head', 'seq'), may hold values from -0.046875 to 0.046875
Outputs:
- layer_out: bfloat16 [2048, 8192], P(('seq', 'head'))
- boundary_states: float32 [4, 256, 64, 256], P('seq', 'head')
The draws below stay inside these ranges and needn't reach their ends.
All inputs are finite; a program needn't handle non-finite values.
Results may differ from the reference program's by a relative error of at most 0.015.
Values may be sent and summed in bfloat16 or wider, within the bound.
A program may use at most 192 MiB of HBM per device.

```python
import jax
import jax.numpy as jnp
from jax import lax

D = 8192
MIXER_HEADS = 256
HEADDIM = 64
STATE = 256
GROUPS = 8
KERNEL = 4
SPAN = 128
TOK_SEQ = 512
DINNER = 16384
TOKEN_COUNT = 2048
N_SEQ = 4
N_HEAD = 8


def draw_dt_input(key, part):
    random_keys = jax.random.split(key, 4)
    gradual_span = jax.random.randint(random_keys[0], (MIXER_HEADS, 1), 0, 10) < 5
    rough = jnp.exp(jax.random.uniform(random_keys[1], (MIXER_HEADS, TOKEN_COUNT), minval=-0.5, maxval=0.5))
    gradual_step = 0.5 / TOKEN_COUNT * rough
    rapid_step = 0.04 * rough
    locations = jax.random.randint(random_keys[2], (3,), 0, TOKEN_COUNT)
    quick_span = jnp.any(jnp.arange(TOKEN_COUNT)[:, None] == locations[None, :], axis=1)
    quick_span_step = jax.random.uniform(random_keys[3], (MIXER_HEADS, TOKEN_COUNT), minval=0.25, maxval=0.6)
    stride_length = jnp.where(quick_span[None, :], quick_span_step, jnp.where(gradual_span, gradual_step, rapid_step))
    return jnp.log(jnp.expm1(stride_length)).astype(jnp.float32)


def draw_gate_input(key, part):
    random_keys = jax.random.split(key, 3)
    trend = jnp.exp(jnp.log(3.0) * jnp.arange(DINNER) / DINNER)[None, :]
    column_scale = jnp.exp(jax.random.uniform(random_keys[0], (1, DINNER), minval=-1.15, maxval=1.15)) * trend
    row_scale = jnp.exp(jax.random.uniform(random_keys[1], (TOKEN_COUNT, 1), minval=-1.15, maxval=1.15))
    base = jnp.clip(jax.random.normal(random_keys[2], (TOKEN_COUNT, DINNER)), -4.0, 4.0)
    return (0.25 * base * column_scale * row_scale).astype(jnp.bfloat16)


def steps_of(key, dims, cuts, smallest, high):
    level = 1.0
    for position, parts in cuts:
        steps = jax.random.uniform(jax.random.fold_in(jax.random.fold_in(key, 6), position), (parts,), jnp.float32, smallest / len(cuts), high / len(cuts))
        level = level * jnp.repeat(jnp.exp(steps), dims[position] // parts).reshape((-1,) + (1,) * (len(dims) - 1 - position))
    return level


def noise(own_key, dims, deviation, bound, pieces=(), kind=jnp.bfloat16):
    level = steps_of(own_key, dims, pieces, -0.22, 0.18) if pieces else 1.0
    result = jax.random.normal(own_key, dims, jnp.float32) * deviation * level
    return jnp.minimum(jnp.maximum(result, -bound), bound).astype(kind)


def setup_inputs(seed: int = 0) -> dict:
    keys = jax.random.split(jax.random.key(seed), 16)
    inner_input = noise(keys[0], (TOKEN_COUNT, DINNER), 1.0, 6.0, ((0, 4), (1, 8)))
    gate_input = draw_gate_input(jax.random.fold_in(keys[15], 71), 0)
    bc_input = noise(keys[2], (TOKEN_COUNT, 2 * GROUPS * STATE), 1.0, 6.0, ((0, 4),))
    dt_input = draw_dt_input(jax.random.fold_in(keys[15], 71), 0)
    log_rate = jnp.clip(-1.2 + 1.2 * jax.random.uniform(keys[4], (MIXER_HEADS,), jnp.float32) ** steps_of(keys[4], (MIXER_HEADS,), ((0, 8),), -0.2, 0.2), -1.2, 0.0)
    skip_weight = jnp.clip(0.5 + 1.0 * jax.random.uniform(keys[5], (MIXER_HEADS,), jnp.float32) ** steps_of(keys[5], (MIXER_HEADS,), ((0, 8),), -0.2, 0.2), 0.5, 1.5)
    conv_weight_x = noise(keys[6], (KERNEL, DINNER), 0.5, 3.0, ((1, 8),), jnp.float32)
    conv_bias_x = noise(keys[7], (DINNER,), 0.5, 3.0, ((0, 8),), jnp.float32)
    conv_weight_bc = noise(keys[8], (KERNEL, 2 * GROUPS * STATE), 0.5, 3.0, (), jnp.float32)
    conv_bias_bc = noise(keys[9], (2 * GROUPS * STATE,), 0.5, 3.0, (), jnp.float32)
    conv_tail_x = noise(keys[10], (KERNEL - 1, DINNER), 1.0, 6.0, ((1, 8),))
    conv_tail_bc = noise(keys[11], (KERNEL - 1, 2 * GROUPS * STATE), 1.0, 6.0)
    init_state = noise(keys[12], (MIXER_HEADS, HEADDIM, STATE), 0.1, 0.6, ((0, 8),), jnp.float32)
    norm_gain = jnp.clip(1.0 + 0.1 * jax.random.normal(keys[13], (DINNER,), jnp.float32), 0.5, 1.5)
    out_weight = noise(keys[14], (DINNER, D), DINNER ** -0.5, 0.046875, ((0, 8), (1, 4)))
    return dict(inner_input=inner_input, gate_input=gate_input, bc_input=bc_input, dt_input=dt_input, log_rate=log_rate, skip_weight=skip_weight, conv_weight_x=conv_weight_x, conv_bias_x=conv_bias_x, conv_weight_bc=conv_weight_bc, conv_bias_bc=conv_bias_bc, conv_tail_x=conv_tail_x, conv_tail_bc=conv_tail_bc, init_state=init_state, norm_gain=norm_gain, out_weight=out_weight)


highest = lax.Precision.HIGHEST
norm_eps = 1e-05

def causal_conv(values, previous, kernel_weight, kernel_bias):
    extended = jnp.concatenate([previous, values], axis=0)
    length = values.shape[0]
    running = jnp.zeros_like(values) + kernel_bias[None, :]
    for offset in range(KERNEL):
        running = running + kernel_weight[offset][None, :] * extended[offset:offset + length]
    return running

def ssd_block(span_x, span_b, span_c, span_step, span_log, state):
    cumul = jnp.cumsum(span_log, axis=1)
    length = span_x.shape[0]
    causal = (jnp.arange(length)[:, None] >= jnp.arange(length)[None, :])[None]
    spread = jnp.where(causal, cumul[:, :, None] - cumul[:, None, :], 0.0)
    decays = jnp.where(causal, jnp.exp(spread), 0.0)
    scores = jnp.einsum('thn,shn->hts', span_c, span_b, precision=highest)
    mixer = scores * decays * span_step[:, None, :]
    output = jnp.einsum('hts,shp->thp', mixer, span_x, precision=highest)
    carried = jnp.einsum('thn,hpn->thp', span_c, state, precision=highest)
    output = output + jnp.exp(cumul).T[:, :, None] * carried
    weights = jnp.exp(cumul[:, -1:] - cumul) * span_step
    written = jnp.einsum('hs,shp,shn->hpn', weights, span_x, span_b, precision=highest)
    new_state = jnp.exp(cumul[:, -1])[:, None, None] * state + written
    return (output, new_state)

def reference(inner_input, gate_input, bc_input, dt_input, log_rate, skip_weight, conv_weight_x, conv_bias_x, conv_weight_bc, conv_bias_bc, conv_tail_x, conv_tail_bc, init_state, norm_gain, out_weight):
    conv_x = jax.nn.silu(causal_conv(inner_input.astype(jnp.float32), conv_tail_x.astype(jnp.float32), conv_weight_x, conv_bias_x)).astype(jnp.bfloat16)
    conv_bc = jax.nn.silu(causal_conv(bc_input.astype(jnp.float32), conv_tail_bc.astype(jnp.float32), conv_weight_bc, conv_bias_bc)).astype(jnp.bfloat16)
    stride_length = jax.nn.softplus(dt_input)
    decay_log = -jnp.exp(log_rate)[:, None] * stride_length
    per_group = MIXER_HEADS // GROUPS
    spans_group = TOK_SEQ // SPAN

    def span_body(state, span_index):
        first_row = (span_index * SPAN).astype(jnp.int32)
        span_x = lax.dynamic_slice_in_dim(conv_x, first_row, SPAN, 0).astype(jnp.float32).reshape(SPAN, MIXER_HEADS, HEADDIM)
        span_bc = lax.dynamic_slice_in_dim(conv_bc, first_row, SPAN, 0).astype(jnp.float32)
        span_b = jnp.repeat(span_bc[:, :GROUPS * STATE].reshape(SPAN, GROUPS, STATE), per_group, axis=1)
        span_c = jnp.repeat(span_bc[:, GROUPS * STATE:].reshape(SPAN, GROUPS, STATE), per_group, axis=1)
        span_step = lax.dynamic_slice_in_dim(stride_length, first_row, SPAN, 1)
        span_log = lax.dynamic_slice_in_dim(decay_log, first_row, SPAN, 1)
        output, new_state = ssd_block(span_x, span_b, span_c, span_step, span_log, state)
        output = output + skip_weight[None, :, None] * span_x
        return (new_state, output)

    def group_body(state, group_index):
        indices = group_index * spans_group + jnp.arange(spans_group, dtype=jnp.int32)
        state, outputs = lax.scan(span_body, state, indices)
        return (state, (state, outputs))
    final_state, (boundary_states, outputs) = lax.scan(group_body, init_state, jnp.arange(N_SEQ, dtype=jnp.int32))
    mixed = outputs.reshape(TOKEN_COUNT, DINNER) * jax.nn.silu(gate_input.astype(jnp.float32))
    grouped = mixed.reshape(TOKEN_COUNT, GROUPS, DINNER // GROUPS)
    mean_square = lax.optimization_barrier(jnp.mean(grouped * grouped, axis=2, keepdims=True))
    normed = ((grouped * lax.rsqrt(mean_square + norm_eps)).reshape(TOKEN_COUNT, DINNER) * norm_gain[None, :]).astype(jnp.bfloat16)
    block_width = DINNER // N_HEAD

    def add_block(counter, running):
        offset = (counter * block_width).astype(jnp.int32)
        block_rows = lax.dynamic_slice_in_dim(normed, offset, block_width, 1)
        block_weight = lax.dynamic_slice_in_dim(out_weight, offset, block_width, 0)
        partial_sum = jnp.dot(block_rows, block_weight, preferred_element_type=jnp.float32).astype(jnp.bfloat16)
        return running + lax.optimization_barrier(partial_sum).astype(jnp.float32)
    layer_out = lax.fori_loop(0, N_HEAD, add_block, jnp.zeros((TOKEN_COUNT, D), jnp.float32)).astype(jnp.bfloat16)
    return (layer_out, boundary_states)
```

```python
import functools

import jax
import jax.numpy as jnp
from jax import lax
from jax.experimental import pallas as pl
from jax.experimental.pallas import tpu as pltpu
from jax.sharding import PartitionSpec as P

MIXER_HEADS = 256
HEADDIM = 64
STATE = 256
GROUPS = 8
KERNEL = 4
SPAN = 128
DINNER = 16384
EXTRA = 16
VMEM_LIMIT = 48 * 1024 * 1024

highest = lax.Precision.HIGHEST
norm_eps = 1e-05
f32 = jnp.float32
bf16 = jnp.bfloat16
MESH = pl.DeviceIdType.MESH


def silu(v):
    return v * (1.0 / (1.0 + jnp.exp(-v)))


def shifted(cur, prev8, by):
    moved = pltpu.roll(cur, by, 0)
    before = pltpu.roll(prev8, by, 0)
    row = lax.broadcasted_iota(jnp.int32, before.shape, 0)
    first = jnp.where(row < by, before, moved[:8])
    return jnp.concatenate([first, moved[8:]], axis=0)


def conv_block(in_ref, prev_ref, w_ref, b_ref, out_ref, chunk):
    width = in_ref.shape[1]
    rows = in_ref.shape[0]
    for c in range(0, width, chunk):
        cols = slice(c, c + chunk)
        cur = in_ref[:, cols].astype(f32)
        prev8 = prev_ref[:, cols]
        total = b_ref[:, cols] + w_ref[KERNEL - 1 : KERNEL, cols] * cur
        for by in range(1, KERNEL):
            k = KERNEL - 1 - by
            total = total + w_ref[k : k + 1, cols] * shifted(cur, prev8, by)
        prev_ref[:, cols] = cur[rows - 8 :]
        out_ref[:, cols] = silu(total).astype(bf16)


def spread_matrix(heads):
    h = lax.broadcasted_iota(jnp.int32, (heads, heads * HEADDIM), 0)
    c = lax.broadcasted_iota(jnp.int32, (heads, heads * HEADDIM), 1)
    return jnp.where(c // HEADDIM == h, 1.0, 0.0).astype(f32)


def spread(values, matrix):
    return jnp.dot(values, matrix, precision=highest, preferred_element_type=f32)


def softplus(v):
    e = jnp.exp(-jnp.abs(v))
    u = 1.0 + e
    series = e * (1.0 - e * (0.5 - e * (1.0 / 3.0 - 0.25 * e)))
    return jnp.maximum(v, 0.0) + jnp.where(e < 0.015625, series, jnp.log(u))


def transposed_dot(lhs, rhs):
    return lax.dot_general(
        lhs, rhs, (((1,), (1,)), ((), ())), precision=highest, preferred_element_type=f32
    )


def decay_terms(dt_ref, rate_ref):
    step = softplus(dt_ref[...])
    log = -jnp.exp(rate_ref[...]) * step
    t = lax.broadcasted_iota(jnp.int32, (SPAN, SPAN), 0)
    s = lax.broadcasted_iota(jnp.int32, (SPAN, SPAN), 1)
    lower = jnp.where(t >= s, 1.0, 0.0).astype(f32)
    eye = jnp.where(t == s, 1.0, 0.0).astype(f32)
    cumul_row = transposed_dot(log, lower)
    cumul_col = transposed_dot(lower, log)
    step_col = transposed_dot(eye, step)
    return step, step_col, cumul_row, cumul_col, t >= s


def state_kernel(
    g_ref, inner, bin_, cin, dt, rate, wx, bx, wb, wc, bb, bc, halo_x, halo_b, halo_c,
    x_out, b_out, c_out, enter_out, send_out, local_out,
    prev_x, prev_b, prev_c, state, total,
):
    i = pl.program_id(0)
    heads = dt.shape[0]

    @pl.when(i == 0)
    def _():
        prev_x[...] = halo_x[...].astype(f32)
        prev_b[...] = halo_b[...].astype(f32)
        prev_c[...] = halo_c[...].astype(f32)
        state[...] = jnp.zeros_like(state)
        total[...] = jnp.zeros_like(total)

    conv_block(inner, prev_x, wx, bx, x_out, 256)
    conv_block(bin_, prev_b, wb, bb, b_out, 256)
    conv_block(cin, prev_c, wc, bc, c_out, 256)
    step, step_col, cumul_row, cumul_col, causal = decay_terms(dt, rate)
    last = cumul_col[SPAN - 1 :]
    matrix = spread_matrix(heads)
    weights = spread(jnp.exp(last - cumul_col) * step_col, matrix)
    last8 = spread(jnp.broadcast_to(last, (8, heads)), matrix)
    enter_out[0] = state[...].astype(bf16)
    weighted = (x_out[...].astype(f32) * weights).astype(bf16)
    b_t = b_out[...].astype(f32).T.astype(bf16)
    written = jnp.dot(b_t, weighted, preferred_element_type=f32)
    state[...] = jnp.exp(last8[:1]) * state[...] + written
    total[...] += last8

    @pl.when(i == pl.num_programs(0) - 1)
    def _():
        local_out[...] = state[...]
        send_out[:STATE] = state[...].astype(bf16)
        tl = total[:1]
        high = tl.astype(bf16).astype(f32)
        row = lax.broadcasted_iota(jnp.int32, (EXTRA, tl.shape[1]), 0)
        send_out[STATE:] = jnp.where(row == 0, high, jnp.where(row == 1, tl - high, 0.0)).astype(bf16)


PARTS = 4


def chain_kernel(
    x, b, c, dt, rate, skip, enter, local, sent, y_out, prior_out,
    land, hop, send_sem, recv_sem,
):
    i = pl.program_id(0)
    seq = lax.axis_index("seq")
    last = 3
    wide = land.shape[2]

    def copy(k):
        return pltpu.make_async_remote_copy(
            src_ref=hop.at[k], dst_ref=land.at[k],
            send_sem=send_sem.at[k], recv_sem=recv_sem.at[k],
            device_id={"seq": (seq + 1) % 4}, device_id_type=MESH,
        )

    def joined(k):
        cols = slice(k * wide, (k + 1) * wide)
        own = sent[STATE : STATE + 1, cols].astype(f32) + sent[STATE + 1 : STATE + 2, cols].astype(f32)
        tail = land[k, STATE:].astype(f32)
        hop[k, :STATE] = (
            jnp.exp(own) * land[k, :STATE].astype(f32) + local[:, cols]
        ).astype(bf16)
        log = tail[0:1] + tail[1:2] + own
        high = log.astype(bf16).astype(f32)
        row = lax.broadcasted_iota(jnp.int32, (EXTRA, wide), 0)
        hop[k, STATE:] = jnp.where(row == 0, high, jnp.where(row == 1, log - high, 0.0)).astype(bf16)

    @pl.when(i == 0)
    def _():
        barrier = pltpu.get_barrier_semaphore()

        for by in (1, 3):
            pl.semaphore_signal(
                barrier, inc=1, device_id={"seq": (seq + by) % 4}, device_id_type=MESH
            )
        pl.semaphore_wait(barrier, 2)

        @pl.when(seq == 0)
        def _():
            for k in range(PARTS):
                hop[k] = sent[:, k * wide : (k + 1) * wide]
                copy(k).start()

        @pl.when(seq == 1)
        def _():
            for k in range(PARTS):
                copy(k).wait_recv()
                joined(k)
                copy(k).start()

    local_kernel(x, b, c, dt, rate, skip, enter, y_out)

    @pl.when(i == pl.num_programs(0) - 1)
    def _():
        @pl.when(seq == 2)
        def _():
            for k in range(PARTS):
                copy(k).wait_recv()
                joined(k)
                copy(k).start()

        @pl.when(seq == 3)
        def _():
            for k in range(PARTS):
                copy(k).wait_recv()

        @pl.when(seq > 0)
        def _():
            for k in range(PARTS):
                prior_out[:, k * wide : (k + 1) * wide] = land[k]

        @pl.when(seq == 0)
        def _():
            prior_out[...] = jnp.zeros_like(prior_out)

        @pl.when(seq < last)
        def _():
            for k in range(PARTS):
                copy(k).wait_send()


def local_kernel(x, b, c, dt, rate, skip, enter, y_out):
    heads = dt.shape[0]
    step, step_col, cumul_row, cumul_col, causal = decay_terms(dt, rate)
    matrix = spread_matrix(heads)
    scores = lax.dot_general(
        c[...], b[...], (((1,), (1,)), ((), ())), preferred_element_type=f32
    )
    row_term = jnp.log(step) - cumul_row
    growth = spread(jnp.exp(cumul_col), matrix)
    skip_row = spread(jnp.broadcast_to(skip[...], (8, heads)), matrix)[:1]
    lane = lax.broadcasted_iota(jnp.int32, (SPAN, 2 * HEADDIM), 1)
    zero = jnp.zeros((SPAN, 2 * HEADDIM), bf16)
    for pair in range(heads // 2):
        cols = slice(pair * 2 * HEADDIM, (pair + 1) * 2 * HEADDIM)
        mixers = []
        for h in (2 * pair, 2 * pair + 1):
            power = jnp.where(causal, cumul_col[:, h : h + 1] + row_term[h : h + 1], -1e30)
            mixers.append((scores * jnp.exp(power)).astype(bf16))
        xp = x[:, cols]
        both = jnp.concatenate(
            [jnp.where(lane < HEADDIM, xp, zero), jnp.where(lane >= HEADDIM, xp, zero)], axis=0
        )
        inside = jnp.dot(
            jnp.concatenate(mixers, axis=1), both, preferred_element_type=f32
        )
        carried = jnp.dot(c[...], enter[0, :, cols], preferred_element_type=f32)
        y_out[:, cols] = (
            inside + growth[:, cols] * carried + skip_row[:, cols] * xp.astype(f32)
        )


def output_kernel(
    meta, y, c, gate, dt, rate, gain, gathered, own_tail, init, local, normed_out, boundary_out,
    incoming, entering, mixed, offset, *, block, halves, whole_group, chained,
):
    i = pl.program_id(0)
    heads = dt.shape[0]
    width = y.shape[1]
    count = gathered.shape[0]

    @pl.when(i == 0)
    def _():
        place = meta[0]
        rate_sum = jnp.zeros((1, width), f32)
        incoming[...] = jnp.zeros_like(incoming)
        if chained:
            tail = gathered[0, STATE:].astype(f32)
            incoming[...] = gathered[0, :STATE].astype(f32)
            rate_sum = tail[0:1] + tail[1:2]
        for k in range(-1 if chained else count - 2, -1, -1):
            live = k < place
            tail = gathered[k, STATE:].astype(f32)
            factor = jnp.where(live, jnp.exp(rate_sum), 0.0)
            incoming[...] += factor * gathered[k, :STATE].astype(f32)
            rate_sum = rate_sum + jnp.where(live, tail[0:1] + tail[1:2], 0.0)
        tail = (own_tail[...] if chained else gathered[place, STATE:]).astype(f32)
        own = jnp.exp(tail[0:1] + tail[1:2])
        for k in range(0, width, 256):
            cols = slice(k, k + 256)
            value = incoming[:, cols] + jnp.exp(rate_sum[:, cols]) * init[cols, :].T
            entering[:, cols] = value.astype(bf16)
            boundary_out[cols, :] = (own[:, cols] * value + local[:, cols]).T
        offset[...] = jnp.zeros_like(offset)

    step, step_col, cumul_row, cumul_col, causal = decay_terms(dt, rate)
    cumul_col = cumul_col + offset[:1]
    offset[...] = jnp.broadcast_to(cumul_col[SPAN - 1 :], offset.shape)
    growth = spread(jnp.exp(cumul_col), spread_matrix(heads))
    squares = jnp.zeros((SPAN, 1), f32)
    for k in range(0, width, 256):
        cols = slice(k, k + 256)
        carried = jnp.dot(c[...], entering[:, cols], preferred_element_type=f32)
        value = (y[:, cols] + growth[:, cols] * carried) * silu(gate[:, cols].astype(f32))
        mixed[:, cols] = value
        squares = squares + jnp.sum(value * value, axis=1, keepdims=True)
    if whole_group:
        inverse = lax.rsqrt(squares / width + norm_eps)
    piece = block // halves
    for q in range(SPAN // piece):
        rows = slice(q * piece, (q + 1) * piece)
        first = meta[1 + i * (SPAN // block) + q // halves]
        first = first + (q % halves) * (normed_out.shape[0] // halves)
        value = mixed[rows, :]
        if whole_group:
            value = value * inverse[rows] * gain[...]
        normed_out[pl.ds(pl.multiple_of(first, piece), piece), :] = value.astype(normed_out.dtype)


def partner_of(place, bit):
    size = 1 << bit
    return place + (1 - 2 * ((place // size) % 2)) * size


HALVES = 2
GROUP = 4
MULTIPLY, FIRST, SECOND, THIRD, ARRIVED, LOADED = range(6)
FIRST_Z = (0, 3, 8, 12)
ORDER = (
    82, 6, 83, 3, 81, 1, 22, 80, 0, 2, 17, 4, 18, 16, 33, 64, 38, 9, 20, 32,
    8, 7, 34, 54, 11, 36, 5, 23, 25, 27, 39, 65, 15, 12, 24, 43, 14, 41, 21, 10,
    40, 52, 28, 31, 37, 30, 57, 13, 47, 26, 44, 49, 59, 56, 55, 42, 29, 46, 50, 58,
    63, 60, 19, 45, 53, 48, 62, 35, 61, 51,
)


def project_kernel(
    act, w_own, w_other, out,
    w, acts, keep, y_send, y_recv, a_send, a_recv, b_send, b_recv, x_send, x_recv,
    w_sem, own_sem, act_send_sem, act_recv_sem, send_sem, recv_sem, x_send_sem, x_recv_sem,
):
    seq = lax.axis_index("seq")
    head = lax.axis_index("head")
    wide = w.shape[2]
    per = w_own.shape[1] // wide
    count = keep.shape[0]
    part = count // 2
    piece = out.shape[0] // HALVES
    rows = acts.shape[3]
    other_chip = (seq + 2) % 4
    near = [partner_of(head, bit) for bit in range(3)]
    across = [{"head": place} for place in near]
    over_x = {"seq": other_chip}

    def turned(t):
        value = 0
        for k in FIRST_Z:
            value = value + jnp.where(t == k, 1, 0)
        return value

    def target_of(stage, t):
        if stage == 2:
            return across[2]
        return {"head": near[stage] + turned(t) * (near[1 - stage] - near[stage])}

    def reorder(place, half):
        for slot, first in enumerate((0, 4, 2, 6)):
            acts[place, 1, half, slot * 2 * piece : (slot + 1) * 2 * piece] = acts[
                place, 0, half, first * piece : (first + 2) * piece
            ]

    def load(k):
        source = w_own if k < per else w_other
        first = (k % per) * wide
        return pltpu.make_async_copy(source.at[:, first : first + wide], w.at[k], w_sem.at[k])

    def own_copy(half):
        return pltpu.make_async_copy(
            act.at[half * rows : (half + 1) * rows], acts.at[0, 0, half], own_sem.at[half]
        )

    def act_copy(half):
        return pltpu.make_async_remote_copy(
            src_ref=acts.at[0, 0, half], dst_ref=acts.at[1, 0, half],
            send_sem=act_send_sem.at[half], recv_sem=act_recv_sem.at[half],
            device_id=over_x, device_id_type=MESH,
        )

    def head_copy(stage, t):
        source, target = ((y_send, y_recv), (a_send, a_recv), (b_send, b_recv))[stage]
        return pltpu.make_async_remote_copy(
            src_ref=source.at[t], dst_ref=target.at[t],
            send_sem=send_sem.at[stage, t], recv_sem=recv_sem.at[stage, t],
            device_id=target_of(stage, t), device_id_type=MESH,
        )

    def chip_copy(k):
        return pltpu.make_async_remote_copy(
            src_ref=x_send.at[k], dst_ref=x_recv.at[k],
            send_sem=x_send_sem.at[k], recv_sem=x_recv_sem.at[k],
            device_id=over_x, device_id_type=MESH,
        )

    for half in range(HALVES):
        own_copy(half).start()
    for k in range(GROUP):
        load(k).start()

    barrier = pltpu.get_barrier_semaphore()
    for target in across + [over_x]:
        pl.semaphore_signal(barrier, inc=1, device_id=target, device_id_type=MESH)
    pl.semaphore_wait(barrier, 4)

    for half in range(HALVES):
        own_copy(half).wait()
        act_copy(half).start()
        reorder(0, half)

    def multiply(t):
        place, half, group = t // part, (t % part) // GROUP, t % GROUP
        product = jnp.dot(
            acts[place, turned(t), half], w[group], preferred_element_type=f32
        )
        y_send[t] = product[rows // 2 :].astype(bf16)
        keep[t] = product[: rows // 2]
        head_copy(0, t).start()

    def first_stage(t):
        head_copy(0, t).wait_recv()
        a_send[t] = (keep[t, 2 * piece :] + y_recv[t, 2 * piece :].astype(f32)).astype(bf16)
        head_copy(1, t).start()
        keep[t, : 2 * piece] = keep[t, : 2 * piece] + y_recv[t, : 2 * piece].astype(f32)

    def second_stage(t):
        head_copy(1, t).wait_recv()
        b_send[t] = (keep[t, piece : 2 * piece] + a_recv[t, piece:].astype(f32)).astype(bf16)
        head_copy(2, t).start()
        keep[t, :piece] = keep[t, :piece] + a_recv[t, :piece].astype(f32)

    def place_out(t, home, value):
        group = t % GROUP
        core = (home % 2 + group // per) % 2
        column = ((home // 2) * 2 + core) * (per * wide) + (group % per) * wide
        first = ((t % part) // GROUP) * piece
        out[
            pl.ds(pl.multiple_of(first, piece), piece), pl.ds(pl.multiple_of(column, wide), wide)
        ] = value

    def third_stage(t):
        head_copy(2, t).wait_recv()
        value = (keep[t, :piece] + b_recv[t].astype(f32)).astype(bf16)

        @pl.when(t < part)
        def _():
            place_out(t, seq, value)

        @pl.when(t >= part)
        def _():
            x_send[t - part] = value
            chip_copy(t - part).start()

    def step(i, carry):
        code = 0
        for k, event in enumerate(ORDER):
            code = code + jnp.where(i == k, event, 0)
        kind, t = code // 16, code % 16

        @pl.when(kind == MULTIPLY)
        def _():
            multiply(t)

        @pl.when(kind == FIRST)
        def _():
            first_stage(t)

        @pl.when(kind == SECOND)
        def _():
            second_stage(t)

        @pl.when(kind == THIRD)
        def _():
            third_stage(t)

        for half in range(HALVES):
            @pl.when((kind == ARRIVED) & (t == half))
            def _():
                act_copy(half).wait_recv()
                reorder(1, half)

        for group in range(GROUP):
            @pl.when((kind == LOADED) & (t == group))
            def _():
                load(group).wait()

        return carry

    lax.fori_loop(0, len(ORDER), step, 0)

    def collect(k, carry):
        chip_copy(k).wait_recv()
        place_out(k, other_chip, x_recv[k])
        chip_copy(k).wait_send()
        return carry

    def drain(t, carry):
        for stage in range(3):
            head_copy(stage, t).wait_send()
        return carry

    lax.fori_loop(0, part, collect, 0)
    for half in range(HALVES):
        act_copy(half).wait_send()
    lax.fori_loop(0, count, drain, 0)


def project(normed, own, other):
    rows, width = normed.shape
    columns = own.shape[1]
    block = rows // 8
    piece = block // HALVES
    wide = 2 * columns // GROUP
    part = HALVES * GROUP
    count = 2 * part
    return pl.pallas_call(
        project_kernel,
        in_specs=[
            pl.BlockSpec(memory_space=pl.ANY),
            pl.BlockSpec(memory_space=pl.ANY),
            pl.BlockSpec(memory_space=pl.ANY),
        ],
        out_specs=pl.BlockSpec(memory_space=pltpu.VMEM),
        out_shape=jax.ShapeDtypeStruct((block, 4 * columns), bf16),
        scratch_shapes=[
            pltpu.VMEM((GROUP, width, wide), bf16),
            pltpu.VMEM((2, 2, HALVES, rows // HALVES, width), bf16),
            pltpu.VMEM((count, 4 * piece, wide), f32),
            pltpu.VMEM((count, 4 * piece, wide), bf16),
            pltpu.VMEM((count, 4 * piece, wide), bf16),
            pltpu.VMEM((count, 2 * piece, wide), bf16),
            pltpu.VMEM((count, 2 * piece, wide), bf16),
            pltpu.VMEM((count, piece, wide), bf16),
            pltpu.VMEM((count, piece, wide), bf16),
            pltpu.VMEM((part, piece, wide), bf16),
            pltpu.VMEM((part, piece, wide), bf16),
            pltpu.SemaphoreType.DMA((GROUP,)),
            pltpu.SemaphoreType.DMA((HALVES,)),
            pltpu.SemaphoreType.DMA((HALVES,)),
            pltpu.SemaphoreType.DMA((HALVES,)),
            pltpu.SemaphoreType.DMA((3, count)),
            pltpu.SemaphoreType.DMA((3, count)),
            pltpu.SemaphoreType.DMA((part,)),
            pltpu.SemaphoreType.DMA((part,)),
        ],
        compiler_params=pltpu.CompilerParams(
            vmem_limit_bytes=56 * 1024 * 1024, collective_id=0, has_side_effects=True
        ),
        name="project_and_sum",
    )(normed, own, other)


def params():
    return pltpu.CompilerParams(vmem_limit_bytes=VMEM_LIMIT)


def body(
    inner_input,
    gate_input,
    bc_input,
    dt_input,
    log_rate,
    skip_weight,
    conv_weight_x,
    conv_bias_x,
    conv_weight_bc,
    conv_bias_bc,
    conv_tail_x,
    conv_tail_bc,
    init_state,
    norm_gain,
    out_weight,
):
    seq_count = lax.axis_size("seq")
    head_count = lax.axis_size("head")
    seq_index = lax.axis_index("seq")
    head_index = lax.axis_index("head")
    rows, width = inner_input.shape
    heads = dt_input.shape[0]
    per_group = MIXER_HEADS // GROUPS
    group = (head_index * heads // per_group).astype(jnp.int32)
    spans = rows // SPAN
    block = rows // head_count
    group_width = DINNER // GROUPS
    whole_group = width == group_width

    other_core = lax.ppermute(out_weight, "seq", [(i, i ^ 1) for i in range(seq_count)])

    def pair_columns(table, axis):
        return [
            lax.dynamic_slice_in_dim(table, (g + group) * STATE, STATE, axis) for g in (0, GROUPS)
        ]

    tail_rows = rows - KERNEL + 1
    last_rows = jnp.concatenate(
        [inner_input[tail_rows:]] + pair_columns(bc_input[tail_rows:], 1), axis=1
    )
    arrived = lax.ppermute(last_rows, "seq", [(i, i + 1) for i in range(seq_count - 1)])
    first_rows = jnp.concatenate([conv_tail_x] + pair_columns(conv_tail_bc, 1), axis=1)
    halo = jnp.where(seq_index == 0, first_rows, arrived)
    halo = jnp.pad(halo, ((8 - KERNEL + 1, 0), (0, 0)))
    rate = log_rate[:, None]

    def const(shape, *index):
        return pl.BlockSpec(shape, lambda i, *_: index)

    span_x = pl.BlockSpec((SPAN, width), lambda i, *_: (i, 0))
    span_bc = pl.BlockSpec((SPAN, STATE), lambda i, *_: (i, 0))
    span_dt = pl.BlockSpec((heads, SPAN), lambda i, *_: (0, i))

    conv_x, conv_b, conv_c, enter, sent, local = pl.pallas_call(
        state_kernel,
        grid_spec=pltpu.PrefetchScalarGridSpec(
            num_scalar_prefetch=1,
            grid=(spans,),
            in_specs=[
                span_x,
                pl.BlockSpec((SPAN, STATE), lambda i, g: (i, g[0])),
                pl.BlockSpec((SPAN, STATE), lambda i, g: (i, g[0] + GROUPS)),
                span_dt,
                const((heads, 1), 0, 0),
                const((KERNEL, width), 0, 0),
                const((1, width), 0, 0),
                pl.BlockSpec((KERNEL, STATE), lambda i, g: (0, g[0])),
                pl.BlockSpec((KERNEL, STATE), lambda i, g: (0, g[0] + GROUPS)),
                pl.BlockSpec((1, STATE), lambda i, g: (0, g[0])),
                pl.BlockSpec((1, STATE), lambda i, g: (0, g[0] + GROUPS)),
                const((8, width), 0, 0),
                const((8, STATE), 0, width // STATE),
                const((8, STATE), 0, width // STATE + 1),
            ],
            out_specs=[
                span_x,
                span_bc,
                span_bc,
                pl.BlockSpec((1, STATE, width), lambda i, *_: (i, 0, 0)),
                const((STATE + EXTRA, width), 0, 0),
                const((STATE, width), 0, 0),
            ],
            scratch_shapes=[
                pltpu.VMEM((8, width), f32),
                pltpu.VMEM((8, STATE), f32),
                pltpu.VMEM((8, STATE), f32),
                pltpu.VMEM((STATE, width), f32),
                pltpu.VMEM((8, width), f32),
            ],
        ),
        out_shape=[
            jax.ShapeDtypeStruct((rows, width), bf16),
            jax.ShapeDtypeStruct((rows, STATE), bf16),
            jax.ShapeDtypeStruct((rows, STATE), bf16),
            jax.ShapeDtypeStruct((spans, STATE, width), bf16),
            jax.ShapeDtypeStruct((STATE + EXTRA, width), bf16),
            jax.ShapeDtypeStruct((STATE, width), f32),
        ],
        compiler_params=params(),
        name="conv_and_states",
    )(
        group[None],
        inner_input, bc_input, bc_input, dt_input, rate,
        conv_weight_x, conv_bias_x[None], conv_weight_bc, conv_weight_bc,
        conv_bias_bc[None], conv_bias_bc[None], halo, halo, halo,
    )

    chained = seq_count == 4 and width % (PARTS * 128) == 0
    local_specs = [
        span_x,
        span_bc,
        span_bc,
        span_dt,
        const((heads, 1), 0, 0),
        const((1, heads), 0, 0),
        pl.BlockSpec((1, STATE, width), lambda i: (i, 0, 0)),
    ]
    local_args = (conv_x, conv_b, conv_c, dt_input, rate, skip_weight[None], enter)
    y_shape = jax.ShapeDtypeStruct((rows, width), f32)
    if chained:
        slots = (PARTS, STATE + EXTRA, width // PARTS)
        y_local, prior = pl.pallas_call(
            chain_kernel,
            grid=(spans,),
            in_specs=local_specs
            + [const((STATE, width), 0, 0), const((STATE + EXTRA, width), 0, 0)],
            out_specs=[span_x, const((STATE + EXTRA, width), 0, 0)],
            out_shape=[y_shape, jax.ShapeDtypeStruct((STATE + EXTRA, width), bf16)],
            scratch_shapes=[
                pltpu.VMEM(slots, bf16),
                pltpu.VMEM(slots, bf16),
                pltpu.SemaphoreType.DMA((PARTS,)),
                pltpu.SemaphoreType.DMA((PARTS,)),
            ],
            compiler_params=pltpu.CompilerParams(
                vmem_limit_bytes=VMEM_LIMIT, collective_id=1, has_side_effects=True
            ),
            name="local_outputs_and_chain",
        )(*local_args, local, sent)
        gathered = prior[None]
    else:
        gathered = lax.all_gather(sent, "seq")
        y_local = pl.pallas_call(
            local_kernel,
            grid=(spans,),
            in_specs=local_specs,
            out_specs=span_x,
            out_shape=y_shape,
            compiler_params=params(),
            name="local_outputs",
        )(*local_args)

    projected = (
        seq_count == 4 and head_count == 8 and whole_group and rows == 512
        and out_weight.shape[1] % 512 == 0
    )
    halves = HALVES if projected else 1
    bits = head_count.bit_length() - 1
    distance = jnp.arange(head_count, dtype=jnp.int32) ^ head_index
    slot = jnp.zeros_like(distance)
    for bit in range(bits):
        slot = slot + ((distance >> bit) & 1) * (head_count >> (bit + 1))
    meta = jnp.concatenate([seq_index[None].astype(jnp.int32), slot.astype(jnp.int32) * (block // halves)])

    normed, boundary = pl.pallas_call(
        functools.partial(
            output_kernel, block=block, halves=halves, whole_group=whole_group, chained=chained
        ),
        grid_spec=pltpu.PrefetchScalarGridSpec(
            num_scalar_prefetch=1,
            grid=(spans,),
            in_specs=[
                span_x,
                span_bc,
                span_x,
                span_dt,
                const((heads, 1), 0, 0),
                const((1, width), 0, 0),
                const((gathered.shape[0], STATE + EXTRA, width), 0, 0, 0),
                const((EXTRA, width), STATE // EXTRA, 0),
                const((width, STATE), 0, 0),
                const((STATE, width), 0, 0),
            ],
            out_specs=[const((rows, width), 0, 0), const((width, STATE), 0, 0)],
            scratch_shapes=[
                pltpu.VMEM((STATE, width), f32),
                pltpu.VMEM((STATE, width), bf16),
                pltpu.VMEM((SPAN, width), f32),
                pltpu.VMEM((8, heads), f32),
            ],
        ),
        out_shape=[
            jax.ShapeDtypeStruct((rows, width), bf16 if whole_group else f32),
            jax.ShapeDtypeStruct((width, STATE), f32),
        ],
        compiler_params=params(),
        name="gated_outputs",
    )(
        meta,
        y_local, conv_c, gate_input, dt_input, rate, norm_gain[None], gathered, sent,
        init_state.reshape(width, STATE), local,
    )
    boundary = boundary.reshape(1, heads, HEADDIM, STATE)

    if not whole_group:
        piece = min(width, group_width)
        pieces = normed.reshape(rows, width // piece, piece)
        squares = jnp.sum(pieces * pieces, axis=2).T
        blocks = squares.reshape(squares.shape[0], head_count, block)
        ordered = jnp.take(blocks, slot, axis=1).reshape(squares.shape)
        own = (head_index * (width // piece) + jnp.arange(width // piece)) * piece // group_width
        member = (own[:, None] == jnp.arange(GROUPS)[None, :]).astype(f32)
        totals = lax.psum(jnp.dot(member.T, ordered, precision=highest), "head")
        sums = jnp.dot(member, totals, precision=highest)
        inverse = lax.rsqrt(sums / group_width + norm_eps)
        back = jnp.zeros_like(slot).at[slot].set(jnp.arange(head_count, dtype=slot.dtype))
        inverse = jnp.take(inverse.reshape(blocks.shape), back, axis=1).reshape(squares.shape).T
        normed = (
            (pieces * inverse[:, :, None]).reshape(rows, width) * norm_gain[None, :]
        ).astype(bf16)

    if projected:
        return (project(normed, out_weight, other_core), boundary)

    chips = seq_count // 2

    def around(value, by):
        if by % chips == 0:
            return value
        return lax.ppermute(
            value, "seq", [(i, (i + 2 * by) % seq_count) for i in range(seq_count)]
        )

    def across(value, bit):
        return lax.ppermute(
            value, "head", [(i, i ^ (1 << bit)) for i in range(head_count)]
        )

    def reduced(act, weight):
        half = rows // 2
        give = jnp.dot(act[half:], weight, preferred_element_type=f32).astype(bf16)
        keep = jnp.dot(act[:half], weight, preferred_element_type=f32)
        keep = keep + across(give, 0).astype(f32)
        for bit in range(1, bits):
            half = half // 2
            got = across(keep[half:].astype(bf16), bit)
            keep = keep[:half] + got.astype(f32)
        return keep.astype(bf16)

    core = seq_index % 2
    columns = out_weight.shape[1]
    layer_out = jnp.zeros((block, seq_count, columns), bf16)
    acts = [around(normed, by) for by in range(chips)]
    done = [[reduced(act, w) for w in (out_weight, other_core)] for act in acts]
    for by in range(chips):
        mine, other = [around(d, -by) for d in done[by]]
        chip = (seq_index // 2 + by) % chips
        layer_out = lax.dynamic_update_slice(
            layer_out, mine[:, None], (0, chip * 2 + core, 0)
        )
        layer_out = lax.dynamic_update_slice(
            layer_out, other[:, None], (0, chip * 2 + 1 - core, 0)
        )
    return (layer_out.reshape(block, seq_count * columns), boundary)


def solution(mesh):
    in_specs = (
        P("seq", "head"),
        P("seq", "head"),
        P("seq", None),
        P("head", "seq"),
        P("head"),
        P("head"),
        P(None, "head"),
        P("head"),
        P(),
        P(),
        P(None, "head"),
        P(),
        P("head", None, None),
        P("head"),
        P("head", "seq"),
    )
    out_specs = (P(("seq", "head"), None), P("seq", "head", None, None))
    return jax.shard_map(body, mesh=mesh, in_specs=in_specs, out_specs=out_specs, check_vma=False)
```

```python
import functools

import jax
import jax.numpy as jnp
from jax import lax
from jax.experimental import pallas as pl
from jax.experimental.pallas import tpu as pltpu
from jax.sharding import PartitionSpec as P

MIXER_HEADS = 256
HEADDIM = 64
STATE = 256
GROUPS = 8
KERNEL = 4
SPAN = 128
DINNER = 16384
EXTRA = 16
VMEM_LIMIT = 48 * 1024 * 1024
FRONT_LIMIT = 60 * 1024 * 1024

highest = lax.Precision.HIGHEST
norm_eps = 1e-05
f32 = jnp.float32
bf16 = jnp.bfloat16
MESH = pl.DeviceIdType.MESH


def silu(v):
    return v * (1.0 / (1.0 + jnp.exp(-v)))


def shifted(cur, prev8, by):
    moved = pltpu.roll(cur, by, 0)
    before = pltpu.roll(prev8, by, 0)
    row = lax.broadcasted_iota(jnp.int32, before.shape, 0)
    first = jnp.where(row < by, before, moved[:8])
    return jnp.concatenate([first, moved[8:]], axis=0)


def conv_block(in_ref, prev_ref, w_ref, b_ref, out_ref, chunk):
    width = in_ref.shape[1]
    rows = in_ref.shape[0]
    for c in range(0, width, chunk):
        cols = slice(c, c + chunk)
        cur = in_ref[:, cols].astype(f32)
        prev8 = prev_ref[:, cols]
        total = b_ref[:, cols] + w_ref[KERNEL - 1 : KERNEL, cols] * cur
        for by in range(1, KERNEL):
            k = KERNEL - 1 - by
            total = total + w_ref[k : k + 1, cols] * shifted(cur, prev8, by)
        prev_ref[:, cols] = cur[rows - 8 :]
        out_ref[:, cols] = silu(total).astype(bf16)


def spread_matrix(heads):
    h = lax.broadcasted_iota(jnp.int32, (heads, heads * HEADDIM), 0)
    c = lax.broadcasted_iota(jnp.int32, (heads, heads * HEADDIM), 1)
    return jnp.where(c // HEADDIM == h, 1.0, 0.0).astype(f32)


def spread(values, matrix):
    return jnp.dot(values, matrix, precision=highest, preferred_element_type=f32)


def softplus(v):
    e = jnp.exp(-jnp.abs(v))
    u = 1.0 + e
    series = e * (1.0 - e * (0.5 - e * (1.0 / 3.0 - 0.25 * e)))
    return jnp.maximum(v, 0.0) + jnp.where(e < 0.015625, series, jnp.log(u))


def transposed_dot(lhs, rhs):
    return lax.dot_general(
        lhs, rhs, (((1,), (1,)), ((), ())), precision=highest, preferred_element_type=f32
    )


def decay_terms(dt_ref, rate_ref):
    step = softplus(dt_ref[...])
    log = -jnp.exp(rate_ref[...]) * step
    t = lax.broadcasted_iota(jnp.int32, (SPAN, SPAN), 0)
    s = lax.broadcasted_iota(jnp.int32, (SPAN, SPAN), 1)
    lower = jnp.where(t >= s, 1.0, 0.0).astype(f32)
    eye = jnp.where(t == s, 1.0, 0.0).astype(f32)
    cumul_row = transposed_dot(log, lower)
    cumul_col = transposed_dot(lower, log)
    step_col = transposed_dot(eye, step)
    return step, step_col, cumul_row, cumul_col, t >= s


def state_kernel(
    g_ref, inner, bin_, cin, dt, rate, wx, bx, wb, wc, bb, bc, halo_x, halo_b, halo_c,
    x_out, b_out, c_out, enter_out, send_out, local_out,
    prev_x, prev_b, prev_c, state, total,
):
    i = pl.program_id(0)
    heads = dt.shape[0]

    @pl.when(i == 0)
    def _():
        prev_x[...] = halo_x[...].astype(f32)
        prev_b[...] = halo_b[...].astype(f32)
        prev_c[...] = halo_c[...].astype(f32)
        state[...] = jnp.zeros_like(state)
        total[...] = jnp.zeros_like(total)

    conv_block(inner, prev_x, wx, bx, x_out, 256)
    conv_block(bin_, prev_b, wb, bb, b_out, 256)
    conv_block(cin, prev_c, wc, bc, c_out, 256)
    step, step_col, cumul_row, cumul_col, causal = decay_terms(dt, rate)
    last = cumul_col[SPAN - 1 :]
    matrix = spread_matrix(heads)
    weights = spread(jnp.exp(last - cumul_col) * step_col, matrix)
    last8 = spread(jnp.broadcast_to(last, (8, heads)), matrix)
    enter_out[0] = state[...].astype(bf16)
    weighted = (x_out[...].astype(f32) * weights).astype(bf16)
    b_t = b_out[...].astype(f32).T.astype(bf16)
    written = jnp.dot(b_t, weighted, preferred_element_type=f32)
    state[...] = jnp.exp(last8[:1]) * state[...] + written
    total[...] += last8

    @pl.when(i == pl.num_programs(0) - 1)
    def _():
        local_out[...] = state[...]
        send_out[:STATE] = state[...].astype(bf16)
        tl = total[:1]
        high = tl.astype(bf16).astype(f32)
        row = lax.broadcasted_iota(jnp.int32, (EXTRA, tl.shape[1]), 0)
        send_out[STATE:] = jnp.where(row == 0, high, jnp.where(row == 1, tl - high, 0.0)).astype(bf16)


PARTS = 4


def chain_kernel(
    x, b, c, dt, rate, skip, enter, local, sent, y_out, prior_out,
    land, hop, send_sem, recv_sem,
):
    i = pl.program_id(0)
    seq = lax.axis_index("seq")
    last = 3
    wide = land.shape[2]

    def copy(k):
        return pltpu.make_async_remote_copy(
            src_ref=hop.at[k], dst_ref=land.at[k],
            send_sem=send_sem.at[k], recv_sem=recv_sem.at[k],
            device_id={"seq": (seq + 1) % 4}, device_id_type=MESH,
        )

    def joined(k):
        cols = slice(k * wide, (k + 1) * wide)
        own = sent[STATE : STATE + 1, cols].astype(f32) + sent[STATE + 1 : STATE + 2, cols].astype(f32)
        tail = land[k, STATE:].astype(f32)
        hop[k, :STATE] = (
            jnp.exp(own) * land[k, :STATE].astype(f32) + local[:, cols]
        ).astype(bf16)
        log = tail[0:1] + tail[1:2] + own
        high = log.astype(bf16).astype(f32)
        row = lax.broadcasted_iota(jnp.int32, (EXTRA, wide), 0)
        hop[k, STATE:] = jnp.where(row == 0, high, jnp.where(row == 1, log - high, 0.0)).astype(bf16)

    @pl.when(i == 0)
    def _():
        barrier = pltpu.get_barrier_semaphore()

        for by in (1, 3):
            pl.semaphore_signal(
                barrier, inc=1, device_id={"seq": (seq + by) % 4}, device_id_type=MESH
            )
        pl.semaphore_wait(barrier, 2)

        @pl.when(seq == 0)
        def _():
            for k in range(PARTS):
                hop[k] = sent[:, k * wide : (k + 1) * wide]
                copy(k).start()

        @pl.when(seq == 1)
        def _():
            for k in range(PARTS):
                copy(k).wait_recv()
                joined(k)
                copy(k).start()

    local_kernel(x, b, c, dt, rate, skip, enter, y_out)

    @pl.when(i == pl.num_programs(0) - 1)
    def _():
        @pl.when(seq == 2)
        def _():
            for k in range(PARTS):
                copy(k).wait_recv()
                joined(k)
                copy(k).start()

        @pl.when(seq == 3)
        def _():
            for k in range(PARTS):
                copy(k).wait_recv()

        @pl.when(seq > 0)
        def _():
            for k in range(PARTS):
                prior_out[:, k * wide : (k + 1) * wide] = land[k]

        @pl.when(seq == 0)
        def _():
            prior_out[...] = jnp.zeros_like(prior_out)

        @pl.when(seq < last)
        def _():
            for k in range(PARTS):
                copy(k).wait_send()


def local_kernel(x, b, c, dt, rate, skip, enter, y_out):
    heads = dt.shape[0]
    step, step_col, cumul_row, cumul_col, causal = decay_terms(dt, rate)
    matrix = spread_matrix(heads)
    scores = lax.dot_general(
        c[...], b[...], (((1,), (1,)), ((), ())), preferred_element_type=f32
    )
    row_term = jnp.log(step) - cumul_row
    growth = spread(jnp.exp(cumul_col), matrix)
    skip_row = spread(jnp.broadcast_to(skip[...], (8, heads)), matrix)[:1]
    lane = lax.broadcasted_iota(jnp.int32, (SPAN, 2 * HEADDIM), 1)
    zero = jnp.zeros((SPAN, 2 * HEADDIM), bf16)
    for pair in range(heads // 2):
        cols = slice(pair * 2 * HEADDIM, (pair + 1) * 2 * HEADDIM)
        mixers = []
        for h in (2 * pair, 2 * pair + 1):
            power = jnp.where(causal, cumul_col[:, h : h + 1] + row_term[h : h + 1], -1e30)
            mixers.append((scores * jnp.exp(power)).astype(bf16))
        xp = x[:, cols]
        both = jnp.concatenate(
            [jnp.where(lane < HEADDIM, xp, zero), jnp.where(lane >= HEADDIM, xp, zero)], axis=0
        )
        inside = jnp.dot(
            jnp.concatenate(mixers, axis=1), both, preferred_element_type=f32
        )
        carried = jnp.dot(c[...], enter[0, :, cols], preferred_element_type=f32)
        y_out[:, cols] = (
            inside + growth[:, cols] * carried + skip_row[:, cols] * xp.astype(f32)
        )


def output_kernel(
    meta, y, c, gate, dt, rate, gain, gathered, own_tail, init, local, normed_out, boundary_out,
    incoming, entering, mixed, offset, *, block, halves, whole_group, chained,
):
    i = pl.program_id(0)
    heads = dt.shape[0]
    width = y.shape[1]
    count = gathered.shape[0]

    @pl.when(i == 0)
    def _():
        place = meta[0]
        rate_sum = jnp.zeros((1, width), f32)
        incoming[...] = jnp.zeros_like(incoming)
        if chained:
            tail = gathered[0, STATE:].astype(f32)
            incoming[...] = gathered[0, :STATE].astype(f32)
            rate_sum = tail[0:1] + tail[1:2]
        for k in range(-1 if chained else count - 2, -1, -1):
            live = k < place
            tail = gathered[k, STATE:].astype(f32)
            factor = jnp.where(live, jnp.exp(rate_sum), 0.0)
            incoming[...] += factor * gathered[k, :STATE].astype(f32)
            rate_sum = rate_sum + jnp.where(live, tail[0:1] + tail[1:2], 0.0)
        tail = (own_tail[...] if chained else gathered[place, STATE:]).astype(f32)
        own = jnp.exp(tail[0:1] + tail[1:2])
        for k in range(0, width, 256):
            cols = slice(k, k + 256)
            value = incoming[:, cols] + jnp.exp(rate_sum[:, cols]) * init[cols, :].T
            entering[:, cols] = value.astype(bf16)
            boundary_out[cols, :] = (own[:, cols] * value + local[:, cols]).T
        offset[...] = jnp.zeros_like(offset)

    step, step_col, cumul_row, cumul_col, causal = decay_terms(dt, rate)
    cumul_col = cumul_col + offset[:1]
    offset[...] = jnp.broadcast_to(cumul_col[SPAN - 1 :], offset.shape)
    growth = spread(jnp.exp(cumul_col), spread_matrix(heads))
    squares = jnp.zeros((SPAN, 1), f32)
    for k in range(0, width, 256):
        cols = slice(k, k + 256)
        carried = jnp.dot(c[...], entering[:, cols], preferred_element_type=f32)
        value = (y[:, cols] + growth[:, cols] * carried) * silu(gate[:, cols].astype(f32))
        mixed[:, cols] = value
        squares = squares + jnp.sum(value * value, axis=1, keepdims=True)
    if whole_group:
        inverse = lax.rsqrt(squares / width + norm_eps)
    piece = block // halves
    for q in range(SPAN // piece):
        rows = slice(q * piece, (q + 1) * piece)
        first = meta[1 + i * (SPAN // block) + q // halves]
        first = first + (q % halves) * (normed_out.shape[0] // halves)
        value = mixed[rows, :]
        if whole_group:
            value = value * inverse[rows] * gain[...]
        normed_out[pl.ds(pl.multiple_of(first, piece), piece), :] = value.astype(normed_out.dtype)


def partner_of(place, bit):
    size = 1 << bit
    return place + (1 - 2 * ((place // size) % 2)) * size


HALVES = 2
GROUP = 4
MULTIPLY, FIRST, SECOND, THIRD, ARRIVED, LOADED = range(6)
FIRST_Z = (0, 3, 8, 12)
ORDER = (
    82, 6, 83, 3, 81, 1, 22, 80, 0, 2, 17, 4, 18, 16, 33, 64, 38, 9, 20, 32,
    8, 7, 34, 54, 11, 36, 5, 23, 25, 27, 39, 65, 15, 12, 24, 43, 14, 41, 21, 10,
    40, 52, 28, 31, 37, 30, 57, 13, 47, 26, 44, 49, 59, 56, 55, 42, 29, 46, 50, 58,
    63, 60, 19, 45, 53, 48, 62, 35, 61, 51,
)


def project_kernel(
    act, w_own, w_other, out,
    w, acts, keep, y_send, y_recv, a_send, a_recv, b_send, b_recv, x_send, x_recv,
    w_sem, own_sem, act_send_sem, act_recv_sem, send_sem, recv_sem, x_send_sem, x_recv_sem,
):
    seq = lax.axis_index("seq")
    head = lax.axis_index("head")
    wide = w.shape[2]
    per = w_own.shape[1] // wide
    count = keep.shape[0]
    part = count // 2
    piece = out.shape[0] // HALVES
    rows = acts.shape[3]
    other_chip = (seq + 2) % 4
    near = [partner_of(head, bit) for bit in range(3)]
    across = [{"head": place} for place in near]
    over_x = {"seq": other_chip}

    def turned(t):
        value = 0
        for k in FIRST_Z:
            value = value + jnp.where(t == k, 1, 0)
        return value

    def target_of(stage, t):
        if stage == 2:
            return across[2]
        return {"head": near[stage] + turned(t) * (near[1 - stage] - near[stage])}

    def reorder(place, half):
        for slot, first in enumerate((0, 4, 2, 6)):
            acts[place, 1, half, slot * 2 * piece : (slot + 1) * 2 * piece] = acts[
                place, 0, half, first * piece : (first + 2) * piece
            ]

    def load(k):
        source = w_own if k < per else w_other
        first = (k % per) * wide
        return pltpu.make_async_copy(source.at[:, first : first + wide], w.at[k], w_sem.at[k])

    def own_copy(half):
        return pltpu.make_async_copy(
            act.at[half * rows : (half + 1) * rows], acts.at[0, 0, half], own_sem.at[half]
        )

    def act_copy(half):
        return pltpu.make_async_remote_copy(
            src_ref=acts.at[0, 0, half], dst_ref=acts.at[1, 0, half],
            send_sem=act_send_sem.at[half], recv_sem=act_recv_sem.at[half],
            device_id=over_x, device_id_type=MESH,
        )

    def head_copy(stage, t):
        source, target = ((y_send, y_recv), (a_send, a_recv), (b_send, b_recv))[stage]
        return pltpu.make_async_remote_copy(
            src_ref=source.at[t], dst_ref=target.at[t],
            send_sem=send_sem.at[stage, t], recv_sem=recv_sem.at[stage, t],
            device_id=target_of(stage, t), device_id_type=MESH,
        )

    def chip_copy(k):
        return pltpu.make_async_remote_copy(
            src_ref=x_send.at[k], dst_ref=x_recv.at[k],
            send_sem=x_send_sem.at[k], recv_sem=x_recv_sem.at[k],
            device_id=over_x, device_id_type=MESH,
        )

    for half in range(HALVES):
        own_copy(half).start()
    for k in range(GROUP):
        load(k).start()

    barrier = pltpu.get_barrier_semaphore()
    for target in across + [over_x]:
        pl.semaphore_signal(barrier, inc=1, device_id=target, device_id_type=MESH)
    pl.semaphore_wait(barrier, 4)

    for half in range(HALVES):
        own_copy(half).wait()
        act_copy(half).start()
        reorder(0, half)

    def multiply(t):
        place, half, group = t // part, (t % part) // GROUP, t % GROUP
        product = jnp.dot(
            acts[place, turned(t), half], w[group], preferred_element_type=f32
        )
        y_send[t] = product[rows // 2 :].astype(bf16)
        keep[t] = product[: rows // 2]
        head_copy(0, t).start()

    def first_stage(t):
        head_copy(0, t).wait_recv()
        a_send[t] = (keep[t, 2 * piece :] + y_recv[t, 2 * piece :].astype(f32)).astype(bf16)
        head_copy(1, t).start()
        keep[t, : 2 * piece] = keep[t, : 2 * piece] + y_recv[t, : 2 * piece].astype(f32)

    def second_stage(t):
        head_copy(1, t).wait_recv()
        b_send[t] = (keep[t, piece : 2 * piece] + a_recv[t, piece:].astype(f32)).astype(bf16)
        head_copy(2, t).start()
        keep[t, :piece] = keep[t, :piece] + a_recv[t, :piece].astype(f32)

    def place_out(t, home, value):
        group = t % GROUP
        core = (home % 2 + group // per) % 2
        column = ((home // 2) * 2 + core) * (per * wide) + (group % per) * wide
        first = ((t % part) // GROUP) * piece
        out[
            pl.ds(pl.multiple_of(first, piece), piece), pl.ds(pl.multiple_of(column, wide), wide)
        ] = value

    def third_stage(t):
        head_copy(2, t).wait_recv()
        value = (keep[t, :piece] + b_recv[t].astype(f32)).astype(bf16)

        @pl.when(t < part)
        def _():
            place_out(t, seq, value)

        @pl.when(t >= part)
        def _():
            x_send[t - part] = value
            chip_copy(t - part).start()

    def step(i, carry):
        code = 0
        for k, event in enumerate(ORDER):
            code = code + jnp.where(i == k, event, 0)
        kind, t = code // 16, code % 16

        @pl.when(kind == MULTIPLY)
        def _():
            multiply(t)

        @pl.when(kind == FIRST)
        def _():
            first_stage(t)

        @pl.when(kind == SECOND)
        def _():
            second_stage(t)

        @pl.when(kind == THIRD)
        def _():
            third_stage(t)

        for half in range(HALVES):
            @pl.when((kind == ARRIVED) & (t == half))
            def _():
                act_copy(half).wait_recv()
                reorder(1, half)

        for group in range(GROUP):
            @pl.when((kind == LOADED) & (t == group))
            def _():
                load(group).wait()

        return carry

    lax.fori_loop(0, len(ORDER), step, 0)

    def collect(k, carry):
        chip_copy(k).wait_recv()
        place_out(k, other_chip, x_recv[k])
        chip_copy(k).wait_send()
        return carry

    def drain(t, carry):
        for stage in range(3):
            head_copy(stage, t).wait_send()
        return carry

    lax.fori_loop(0, part, collect, 0)
    for half in range(HALVES):
        act_copy(half).wait_send()
    lax.fori_loop(0, count, drain, 0)


def project(normed, own, other):
    rows, width = normed.shape
    columns = own.shape[1]
    block = rows // 8
    piece = block // HALVES
    wide = 2 * columns // GROUP
    part = HALVES * GROUP
    count = 2 * part
    return pl.pallas_call(
        project_kernel,
        in_specs=[
            pl.BlockSpec(memory_space=pl.ANY),
            pl.BlockSpec(memory_space=pl.ANY),
            pl.BlockSpec(memory_space=pl.ANY),
        ],
        out_specs=pl.BlockSpec(memory_space=pltpu.VMEM),
        out_shape=jax.ShapeDtypeStruct((block, 4 * columns), bf16),
        scratch_shapes=[
            pltpu.VMEM((GROUP, width, wide), bf16),
            pltpu.VMEM((2, 2, HALVES, rows // HALVES, width), bf16),
            pltpu.VMEM((count, 4 * piece, wide), f32),
            pltpu.VMEM((count, 4 * piece, wide), bf16),
            pltpu.VMEM((count, 4 * piece, wide), bf16),
            pltpu.VMEM((count, 2 * piece, wide), bf16),
            pltpu.VMEM((count, 2 * piece, wide), bf16),
            pltpu.VMEM((count, piece, wide), bf16),
            pltpu.VMEM((count, piece, wide), bf16),
            pltpu.VMEM((part, piece, wide), bf16),
            pltpu.VMEM((part, piece, wide), bf16),
            pltpu.SemaphoreType.DMA((GROUP,)),
            pltpu.SemaphoreType.DMA((HALVES,)),
            pltpu.SemaphoreType.DMA((HALVES,)),
            pltpu.SemaphoreType.DMA((HALVES,)),
            pltpu.SemaphoreType.DMA((3, count)),
            pltpu.SemaphoreType.DMA((3, count)),
            pltpu.SemaphoreType.DMA((part,)),
            pltpu.SemaphoreType.DMA((part,)),
        ],
        compiler_params=pltpu.CompilerParams(
            vmem_limit_bytes=56 * 1024 * 1024, collective_id=0, has_side_effects=True
        ),
        name="project_and_sum",
    )(normed, own, other)


def tanh_silu(v):
    half = 0.5 * v
    return half + half * jnp.tanh(half)


def two_terms(values):
    high = values.astype(bf16)
    low = (values - high.astype(f32)).astype(bf16)
    return jnp.concatenate([high, low], axis=1)


def fill_matrix(matrix):
    heads = matrix.shape[0] // 2
    h = lax.broadcasted_iota(jnp.int32, matrix.shape, 0) % heads
    c = lax.broadcasted_iota(jnp.int32, matrix.shape, 1) // HEADDIM
    matrix[...] = jnp.where(c == h, 1.0, 0.0).astype(bf16)


def token_decays(dt, rate):
    step = softplus(dt).T
    log = -jnp.exp(rate) * step
    t = lax.broadcasted_iota(jnp.int32, (SPAN, SPAN), 0)
    s = lax.broadcasted_iota(jnp.int32, (SPAN, SPAN), 1)
    lower = jnp.where(t >= s, 1.0, 0.0).astype(f32)
    cumul = [
        jnp.dot(lower, log[k : k + SPAN], precision=highest, preferred_element_type=f32)
        for k in range(0, log.shape[0], SPAN)
    ]
    return step, cumul, t >= s


def conv_tile(cur, prev8, weight, bias):
    total = bias + weight[KERNEL - 1 : KERNEL] * cur
    for by in range(1, KERNEL):
        k = KERNEL - 1 - by
        total = total + weight[k : k + 1] * shifted(cur, prev8, by)
    return tanh_silu(total).astype(bf16)


def front_kernel(
    inner, inner_all, bc_all, dt, rate, wx, bx, wbc, bbc, tail_x, tail_bc,
    x_out, b_out, c_out, prior_out,
    bc_in, halo_x, halo_bc, prev, b_t, weight, matrix, scaled, total, local, land, hop,
    in_sem, halo_send, halo_recv, send_sem, recv_sem,
):
    q = pl.program_id(0)
    seq = lax.axis_index("seq")
    head = lax.axis_index("head")
    rows, wide = inner.shape
    heads = dt.shape[0]
    steps = land.shape[0]
    firsts = [pl.multiple_of((head + g) * STATE, STATE) for g in (0, GROUPS)]
    after = {"seq": (seq + 1) % 4}

    def bc_copy(k):
        return pltpu.make_async_copy(
            bc_all.at[:, pl.ds(firsts[k], STATE)], bc_in.at[k], in_sem.at[k]
        )

    def halo_copies():
        last = pl.ds(rows - 16, 16)
        pairs = [(inner_all.at[last], halo_x)] + [
            (bc_all.at[last, pl.ds(firsts[k], STATE)], halo_bc.at[k]) for k in range(2)
        ]
        return [
            pltpu.make_async_remote_copy(
                src_ref=source, dst_ref=dest, send_sem=halo_send.at[k], recv_sem=halo_recv.at[k],
                device_id=after, device_id_type=MESH,
            )
            for k, (source, dest) in enumerate(pairs)
        ]

    def copy(k):
        return pltpu.make_async_remote_copy(
            src_ref=hop.at[k], dst_ref=land.at[k],
            send_sem=send_sem.at[k], recv_sem=recv_sem.at[k],
            device_id=after, device_id_type=MESH,
        )

    def totals(k):
        cols = pl.ds(pl.multiple_of(k * wide, wide), wide)
        spread_log = jnp.dot(total[...], matrix[:, cols], preferred_element_type=f32)
        return spread_log[0:1] + spread_log[8:9]

    def fill_hop(k, state, log):
        hop[k, :STATE] = state.astype(bf16)
        high = log.astype(bf16).astype(f32)
        row = lax.broadcasted_iota(jnp.int32, (EXTRA, wide), 0)
        hop[k, STATE:] = jnp.where(row == 0, high, jnp.where(row == 1, log - high, 0.0)).astype(bf16)
        copy(k).start()

    def pass_on(k):
        copy(k).wait_recv()
        own = totals(k)
        tail = land[k, STATE:].astype(f32)
        fill_hop(
            k, jnp.exp(own) * land[k, :STATE].astype(f32) + local[k], tail[0:1] + tail[1:2] + own
        )

    @pl.when(q == 0)
    def _():
        for k in range(2):
            bc_copy(k).start()
        barrier = pltpu.get_barrier_semaphore()
        for by in (1, 3):
            pl.semaphore_signal(
                barrier, inc=1, device_id={"seq": (seq + by) % 4}, device_id_type=MESH
            )
        fill_matrix(matrix)
        step, cumul, _ = token_decays(dt[...], rate[...])
        ends = [part[SPAN - 1 :] for part in cumul]
        later = jnp.zeros_like(ends[0])
        for k in range(len(cumul) - 1, -1, -1):
            span = slice(k * SPAN, (k + 1) * SPAN)
            later = later + ends[k]
            weight[span] = two_terms(jnp.exp(later - cumul[k]) * step[span])
        high = later.astype(bf16).astype(f32)
        row = lax.broadcasted_iota(jnp.int32, (16, heads), 0)
        total[...] = two_terms(
            jnp.where(row < 8, jnp.broadcast_to(high, row.shape), jnp.broadcast_to(later - high, row.shape))
        )
        pl.semaphore_wait(barrier, 2)

        @pl.when(seq < 3)
        def _():
            for piece in halo_copies():
                piece.start()

        for k in range(2):
            bc_copy(k).wait()

    def conv_rows(source, k, cols, w, b):
        first = k * SPAN
        cur = source[first : first + SPAN, cols].astype(f32)
        before = source[first - 16 : first, cols].astype(f32)[8:]
        return conv_tile(cur, before, w, b)

    chunk = 256
    spans = rows // SPAN
    order = list(range(1, spans)) + [0]

    def conv_x(k):
        span = slice(k * SPAN, (k + 1) * SPAN)
        for c in range(0, wide, chunk):
            cols = slice(c, c + chunk)
            if k:
                value = conv_rows(inner, k, cols, wx[:, cols], bx[:, cols])
            else:
                value = conv_tile(
                    inner[span, cols].astype(f32), prev[:, cols], wx[:, cols], bx[:, cols]
                )
            x_out[span, cols] = value
            at = pl.ds(pl.multiple_of(q * wide + c, chunk), chunk)
            factor = jnp.dot(weight[span], matrix[:, at], preferred_element_type=f32)
            scaled[span, cols] = (value.astype(f32) * factor).astype(bf16)

    def conv_bc(k):
        span = slice(k * SPAN, (k + 1) * SPAN)
        for g, out in enumerate((b_out, c_out)):
            at = pl.ds(firsts[g], STATE)
            source = bc_in.at[g]
            if k:
                value = conv_rows(source, k, slice(0, STATE), wbc[:, at], bbc[:, at])
            else:
                before = prev[:, wide + g * STATE : wide + (g + 1) * STATE]
                value = conv_tile(source[span].astype(f32), before, wbc[:, at], bbc[:, at])
            out[span] = value
            if g == 0:
                b_t[:, span] = value.astype(f32).T.astype(bf16)

    for k in order[:-1]:
        conv_x(k)

    @pl.when(q == 0)
    def _():
        for k in order[:-1]:
            conv_bc(k)

        @pl.when(seq > 0)
        def _():
            for piece in halo_copies():
                piece.wait_recv()
            for g in range(2):
                prev[:, wide + g * STATE : wide + (g + 1) * STATE] = halo_bc[g].astype(f32)[8:]

        @pl.when(seq == 0)
        def _():
            for g in range(2):
                prev[8 - KERNEL + 1 :, wide + g * STATE : wide + (g + 1) * STATE] = tail_bc[
                    :, pl.ds(firsts[g], STATE)
                ].astype(f32)

        conv_bc(0)

    @pl.when(seq > 0)
    def _():
        at = pl.ds(pl.multiple_of(q * wide, wide), wide)
        prev[:, :wide] = halo_x[:, at].astype(f32)[8:]

    @pl.when(seq == 0)
    def _():
        prev[8 - KERNEL + 1 :, :wide] = tail_x[...].astype(f32)

    conv_x(0)
    state = jnp.dot(b_t[...], scaled[...], preferred_element_type=f32)
    local[q] = state

    @pl.when(seq == 0)
    def _():
        fill_hop(q, local[q], totals(q))

    @pl.when((seq == 1) & (q > 0))
    def _():
        pass_on(q - 1)

    @pl.when(q == steps - 1)
    def _():
        @pl.when(seq == 1)
        def _():
            pass_on(steps - 1)

        @pl.when(seq == 2)
        def _():
            def relay(k, carry):
                pass_on(k)
                return carry

            lax.fori_loop(0, steps, relay, 0)

        @pl.when(seq == 3)
        def _():
            for k in range(steps):
                copy(k).wait_recv()

        @pl.when(seq > 0)
        def _():
            for k in range(steps):
                prior_out[:, k * wide : (k + 1) * wide] = land[k]

        @pl.when(seq == 0)
        def _():
            prior_out[...] = jnp.zeros_like(prior_out)

        @pl.when(seq < 3)
        def _():
            for k in range(steps):
                copy(k).wait_send()
            for piece in halo_copies():
                piece.wait_send()


def gated_kernel(
    x, b, c, gate, dt, rate, skip, gain, prior, init, normed_out, boundary_out,
    state, mixed, matrix,
):
    i = pl.program_id(0)
    head = lax.axis_index("head")
    width = x.shape[1]
    total_rows = normed_out.shape[0]
    chunk = 256

    @pl.when(i == 0)
    def _():
        fill_matrix(matrix)
        tail = prior[STATE:].astype(f32)
        factor = jnp.exp(tail[0:1] + tail[1:2])
        for k in range(0, width, chunk):
            cols = slice(k, k + chunk)
            state[:, cols] = prior[:STATE, cols].astype(f32) + factor[:, cols] * init[cols, :].T

    step, cumul, causal = token_decays(dt[...], rate[...])
    cumul = cumul[0]
    middle = 0.5 * cumul[SPAN - 1 :]
    heads = middle.shape[1]
    factors = two_terms(
        jnp.concatenate(
            [
                jnp.exp(cumul - middle),
                jnp.exp(middle - cumul) * step,
                jnp.broadcast_to(jnp.exp(middle), (8, heads)),
                jnp.broadcast_to(skip[...], (8, heads)),
            ],
            axis=0,
        )
    )
    scores = lax.dot_general(
        c[...], b[...], (((1,), (1,)), ((), ())), preferred_element_type=f32
    )
    left = jnp.concatenate([jnp.where(causal, scores, 0.0).astype(bf16), c[...]], axis=1)
    b_t = b[...].astype(f32).T.astype(bf16)
    squares = jnp.zeros((SPAN, 1), f32)
    for k in range(0, width, chunk):
        cols = slice(k, k + chunk)
        spread_all = jnp.dot(factors, matrix[:, cols], preferred_element_type=f32)
        half_decay = spread_all[2 * SPAN : 2 * SPAN + 1]
        value = x[:, cols].astype(f32)
        weighted = (value * spread_all[SPAN : 2 * SPAN]).astype(bf16)
        before = half_decay * state[:, cols]
        inside = jnp.dot(
            left, jnp.concatenate([weighted, before.astype(bf16)], axis=0),
            preferred_element_type=f32,
        )
        written = jnp.dot(b_t, weighted, preferred_element_type=f32)
        state[:, cols] = half_decay * (before + written)
        value = spread_all[:SPAN] * inside + spread_all[2 * SPAN + 8 : 2 * SPAN + 9] * value
        value = value * tanh_silu(gate[:, cols].astype(f32))
        mixed[:, cols] = value
        squares = squares + jnp.sum(value * value, axis=1, keepdims=True)
    inverse = lax.rsqrt(squares / width + norm_eps)
    block = total_rows // 8
    piece = block // HALVES
    for p in range(SPAN // piece):
        rows = slice(p * piece, (p + 1) * piece)
        owner = i * (SPAN // block) + p // HALVES
        slot = 0
        for bit in range(3):
            differs = (owner // (1 << bit) + head // (1 << bit)) % 2
            slot = slot + differs * (4 >> bit)
        first = (p % HALVES) * (total_rows // HALVES) + slot * piece
        normed_out[pl.ds(pl.multiple_of(first, piece), piece), :] = (
            mixed[rows, :] * inverse[rows] * gain[...]
        ).astype(bf16)

    @pl.when(i == pl.num_programs(0) - 1)
    def _():
        for k in range(0, width, chunk):
            cols = slice(k, k + chunk)
            boundary_out[cols, :] = state[:, cols].T


QUARTERS = 4


def front(inner, gate, bc, dt, rate, skip, wx, bx, wbc, bbc, tail_x, tail_bc, init, gain):
    rows, width = inner.shape
    heads = dt.shape[0]
    wide = width // QUARTERS
    any_space = pl.BlockSpec(memory_space=pl.ANY)
    slots = (QUARTERS, STATE + EXTRA, wide)

    def const(shape, *index):
        return pl.BlockSpec(shape, lambda i: index)

    def across(height):
        return pl.BlockSpec((height, wide), lambda i: (0, i))

    conv_x, conv_b, conv_c, prior = pl.pallas_call(
        front_kernel,
        grid=(QUARTERS,),
        in_specs=[
            across(rows),
            any_space,
            any_space,
            const(dt.shape, 0, 0),
            const((1, heads), 0, 0),
            across(KERNEL),
            across(1),
            const(wbc.shape, 0, 0),
            const((1, wbc.shape[1]), 0, 0),
            across(KERNEL - 1),
            const(tail_bc.shape, 0, 0),
        ],
        out_specs=[
            across(rows),
            const((rows, STATE), 0, 0),
            const((rows, STATE), 0, 0),
            const((STATE + EXTRA, width), 0, 0),
        ],
        out_shape=[
            jax.ShapeDtypeStruct((rows, width), bf16),
            jax.ShapeDtypeStruct((rows, STATE), bf16),
            jax.ShapeDtypeStruct((rows, STATE), bf16),
            jax.ShapeDtypeStruct((STATE + EXTRA, width), bf16),
        ],
        scratch_shapes=[
            pltpu.VMEM((2, rows, STATE), bf16),
            pltpu.VMEM((16, width), bf16),
            pltpu.VMEM((2, 16, STATE), bf16),
            pltpu.VMEM((8, wide + 2 * STATE), f32),
            pltpu.VMEM((STATE, rows), bf16),
            pltpu.VMEM((rows, 2 * heads), bf16),
            pltpu.VMEM((2 * heads, width), bf16),
            pltpu.VMEM((rows, wide), bf16),
            pltpu.VMEM((16, 2 * heads), bf16),
            pltpu.VMEM((QUARTERS, STATE, wide), f32),
            pltpu.VMEM(slots, bf16),
            pltpu.VMEM(slots, bf16),
            pltpu.SemaphoreType.DMA((2,)),
            pltpu.SemaphoreType.DMA((3,)),
            pltpu.SemaphoreType.DMA((3,)),
            pltpu.SemaphoreType.DMA((QUARTERS,)),
            pltpu.SemaphoreType.DMA((QUARTERS,)),
        ],
        compiler_params=pltpu.CompilerParams(
            vmem_limit_bytes=FRONT_LIMIT, collective_id=1, has_side_effects=True
        ),
        name="conv_states_and_chain",
    )(inner, inner, bc, dt, rate[None], wx, bx[None], wbc, bbc[None], tail_x, tail_bc)

    def span(columns):
        return pl.BlockSpec((SPAN, columns), lambda i: (i, 0))

    normed, boundary = pl.pallas_call(
        gated_kernel,
        grid=(rows // SPAN,),
        in_specs=[
            span(width),
            span(STATE),
            span(STATE),
            span(width),
            pl.BlockSpec((heads, SPAN), lambda i: (0, i)),
            const((1, heads), 0, 0),
            const((1, heads), 0, 0),
            const((1, width), 0, 0),
            const((STATE + EXTRA, width), 0, 0),
            const((width, STATE), 0, 0),
        ],
        out_specs=[const((rows, width), 0, 0), const((width, STATE), 0, 0)],
        out_shape=[
            jax.ShapeDtypeStruct((rows, width), bf16),
            jax.ShapeDtypeStruct((width, STATE), f32),
        ],
        scratch_shapes=[
            pltpu.VMEM((STATE, width), f32),
            pltpu.VMEM((SPAN, width), f32),
            pltpu.VMEM((2 * heads, width), bf16),
        ],
        compiler_params=pltpu.CompilerParams(vmem_limit_bytes=FRONT_LIMIT),
        name="outputs_and_gate",
    )(
        conv_x, conv_b, conv_c, gate, dt, rate[None], skip[None], gain[None], prior,
        init.reshape(width, STATE),
    )
    return normed, boundary


def params():
    return pltpu.CompilerParams(vmem_limit_bytes=VMEM_LIMIT)


def body(
    inner_input,
    gate_input,
    bc_input,
    dt_input,
    log_rate,
    skip_weight,
    conv_weight_x,
    conv_bias_x,
    conv_weight_bc,
    conv_bias_bc,
    conv_tail_x,
    conv_tail_bc,
    init_state,
    norm_gain,
    out_weight,
):
    seq_count = lax.axis_size("seq")
    head_count = lax.axis_size("head")
    seq_index = lax.axis_index("seq")
    head_index = lax.axis_index("head")
    rows, width = inner_input.shape
    heads = dt_input.shape[0]
    per_group = MIXER_HEADS // GROUPS
    group = (head_index * heads // per_group).astype(jnp.int32)
    spans = rows // SPAN
    block = rows // head_count
    group_width = DINNER // GROUPS
    whole_group = width == group_width

    other_core = lax.ppermute(out_weight, "seq", [(i, i ^ 1) for i in range(seq_count)])

    projected = (
        seq_count == 4 and head_count == 8 and whole_group and rows == 512 and width == 2048
        and out_weight.shape[1] % 512 == 0
    )
    if projected:
        normed, boundary = front(
            inner_input, gate_input, bc_input, dt_input, log_rate, skip_weight, conv_weight_x,
            conv_bias_x, conv_weight_bc, conv_bias_bc, conv_tail_x, conv_tail_bc, init_state,
            norm_gain,
        )
        boundary = boundary.reshape(1, heads, HEADDIM, STATE)
        return (project(normed, out_weight, other_core), boundary)

    def pair_columns(table, axis):
        return [
            lax.dynamic_slice_in_dim(table, (g + group) * STATE, STATE, axis) for g in (0, GROUPS)
        ]

    tail_rows = rows - KERNEL + 1
    last_rows = jnp.concatenate(
        [inner_input[tail_rows:]] + pair_columns(bc_input[tail_rows:], 1), axis=1
    )
    arrived = lax.ppermute(last_rows, "seq", [(i, i + 1) for i in range(seq_count - 1)])
    first_rows = jnp.concatenate([conv_tail_x] + pair_columns(conv_tail_bc, 1), axis=1)
    halo = jnp.where(seq_index == 0, first_rows, arrived)
    halo = jnp.pad(halo, ((8 - KERNEL + 1, 0), (0, 0)))
    rate = log_rate[:, None]

    def const(shape, *index):
        return pl.BlockSpec(shape, lambda i, *_: index)

    span_x = pl.BlockSpec((SPAN, width), lambda i, *_: (i, 0))
    span_bc = pl.BlockSpec((SPAN, STATE), lambda i, *_: (i, 0))
    span_dt = pl.BlockSpec((heads, SPAN), lambda i, *_: (0, i))

    conv_x, conv_b, conv_c, enter, sent, local = pl.pallas_call(
        state_kernel,
        grid_spec=pltpu.PrefetchScalarGridSpec(
            num_scalar_prefetch=1,
            grid=(spans,),
            in_specs=[
                span_x,
                pl.BlockSpec((SPAN, STATE), lambda i, g: (i, g[0])),
                pl.BlockSpec((SPAN, STATE), lambda i, g: (i, g[0] + GROUPS)),
                span_dt,
                const((heads, 1), 0, 0),
                const((KERNEL, width), 0, 0),
                const((1, width), 0, 0),
                pl.BlockSpec((KERNEL, STATE), lambda i, g: (0, g[0])),
                pl.BlockSpec((KERNEL, STATE), lambda i, g: (0, g[0] + GROUPS)),
                pl.BlockSpec((1, STATE), lambda i, g: (0, g[0])),
                pl.BlockSpec((1, STATE), lambda i, g: (0, g[0] + GROUPS)),
                const((8, width), 0, 0),
                const((8, STATE), 0, width // STATE),
                const((8, STATE), 0, width // STATE + 1),
            ],
            out_specs=[
                span_x,
                span_bc,
                span_bc,
                pl.BlockSpec((1, STATE, width), lambda i, *_: (i, 0, 0)),
                const((STATE + EXTRA, width), 0, 0),
                const((STATE, width), 0, 0),
            ],
            scratch_shapes=[
                pltpu.VMEM((8, width), f32),
                pltpu.VMEM((8, STATE), f32),
                pltpu.VMEM((8, STATE), f32),
                pltpu.VMEM((STATE, width), f32),
                pltpu.VMEM((8, width), f32),
            ],
        ),
        out_shape=[
            jax.ShapeDtypeStruct((rows, width), bf16),
            jax.ShapeDtypeStruct((rows, STATE), bf16),
            jax.ShapeDtypeStruct((rows, STATE), bf16),
            jax.ShapeDtypeStruct((spans, STATE, width), bf16),
            jax.ShapeDtypeStruct((STATE + EXTRA, width), bf16),
            jax.ShapeDtypeStruct((STATE, width), f32),
        ],
        compiler_params=params(),
        name="conv_and_states",
    )(
        group[None],
        inner_input, bc_input, bc_input, dt_input, rate,
        conv_weight_x, conv_bias_x[None], conv_weight_bc, conv_weight_bc,
        conv_bias_bc[None], conv_bias_bc[None], halo, halo, halo,
    )

    chained = seq_count == 4 and width % (PARTS * 128) == 0
    local_specs = [
        span_x,
        span_bc,
        span_bc,
        span_dt,
        const((heads, 1), 0, 0),
        const((1, heads), 0, 0),
        pl.BlockSpec((1, STATE, width), lambda i: (i, 0, 0)),
    ]
    local_args = (conv_x, conv_b, conv_c, dt_input, rate, skip_weight[None], enter)
    y_shape = jax.ShapeDtypeStruct((rows, width), f32)
    if chained:
        slots = (PARTS, STATE + EXTRA, width // PARTS)
        y_local, prior = pl.pallas_call(
            chain_kernel,
            grid=(spans,),
            in_specs=local_specs
            + [const((STATE, width), 0, 0), const((STATE + EXTRA, width), 0, 0)],
            out_specs=[span_x, const((STATE + EXTRA, width), 0, 0)],
            out_shape=[y_shape, jax.ShapeDtypeStruct((STATE + EXTRA, width), bf16)],
            scratch_shapes=[
                pltpu.VMEM(slots, bf16),
                pltpu.VMEM(slots, bf16),
                pltpu.SemaphoreType.DMA((PARTS,)),
                pltpu.SemaphoreType.DMA((PARTS,)),
            ],
            compiler_params=pltpu.CompilerParams(
                vmem_limit_bytes=VMEM_LIMIT, collective_id=1, has_side_effects=True
            ),
            name="local_outputs_and_chain",
        )(*local_args, local, sent)
        gathered = prior[None]
    else:
        gathered = lax.all_gather(sent, "seq")
        y_local = pl.pallas_call(
            local_kernel,
            grid=(spans,),
            in_specs=local_specs,
            out_specs=span_x,
            out_shape=y_shape,
            compiler_params=params(),
            name="local_outputs",
        )(*local_args)

    bits = head_count.bit_length() - 1
    distance = jnp.arange(head_count, dtype=jnp.int32) ^ head_index
    slot = jnp.zeros_like(distance)
    for bit in range(bits):
        slot = slot + ((distance >> bit) & 1) * (head_count >> (bit + 1))
    meta = jnp.concatenate([seq_index[None].astype(jnp.int32), slot.astype(jnp.int32) * block])

    normed, boundary = pl.pallas_call(
        functools.partial(
            output_kernel, block=block, halves=1, whole_group=whole_group, chained=chained
        ),
        grid_spec=pltpu.PrefetchScalarGridSpec(
            num_scalar_prefetch=1,
            grid=(spans,),
            in_specs=[
                span_x,
                span_bc,
                span_x,
                span_dt,
                const((heads, 1), 0, 0),
                const((1, width), 0, 0),
                const((gathered.shape[0], STATE + EXTRA, width), 0, 0, 0),
                const((EXTRA, width), STATE // EXTRA, 0),
                const((width, STATE), 0, 0),
                const((STATE, width), 0, 0),
            ],
            out_specs=[const((rows, width), 0, 0), const((width, STATE), 0, 0)],
            scratch_shapes=[
                pltpu.VMEM((STATE, width), f32),
                pltpu.VMEM((STATE, width), bf16),
                pltpu.VMEM((SPAN, width), f32),
                pltpu.VMEM((8, heads), f32),
            ],
        ),
        out_shape=[
            jax.ShapeDtypeStruct((rows, width), bf16 if whole_group else f32),
            jax.ShapeDtypeStruct((width, STATE), f32),
        ],
        compiler_params=params(),
        name="gated_outputs",
    )(
        meta,
        y_local, conv_c, gate_input, dt_input, rate, norm_gain[None], gathered, sent,
        init_state.reshape(width, STATE), local,
    )
    boundary = boundary.reshape(1, heads, HEADDIM, STATE)

    if not whole_group:
        piece = min(width, group_width)
        pieces = normed.reshape(rows, width // piece, piece)
        squares = jnp.sum(pieces * pieces, axis=2).T
        blocks = squares.reshape(squares.shape[0], head_count, block)
        ordered = jnp.take(blocks, slot, axis=1).reshape(squares.shape)
        own = (head_index * (width // piece) + jnp.arange(width // piece)) * piece // group_width
        member = (own[:, None] == jnp.arange(GROUPS)[None, :]).astype(f32)
        totals = lax.psum(jnp.dot(member.T, ordered, precision=highest), "head")
        sums = jnp.dot(member, totals, precision=highest)
        inverse = lax.rsqrt(sums / group_width + norm_eps)
        back = jnp.zeros_like(slot).at[slot].set(jnp.arange(head_count, dtype=slot.dtype))
        inverse = jnp.take(inverse.reshape(blocks.shape), back, axis=1).reshape(squares.shape).T
        normed = (
            (pieces * inverse[:, :, None]).reshape(rows, width) * norm_gain[None, :]
        ).astype(bf16)

    chips = seq_count // 2

    def around(value, by):
        if by % chips == 0:
            return value
        return lax.ppermute(
            value, "seq", [(i, (i + 2 * by) % seq_count) for i in range(seq_count)]
        )

    def across(value, bit):
        return lax.ppermute(
            value, "head", [(i, i ^ (1 << bit)) for i in range(head_count)]
        )

    def reduced(act, weight):
        half = rows // 2
        give = jnp.dot(act[half:], weight, preferred_element_type=f32).astype(bf16)
        keep = jnp.dot(act[:half], weight, preferred_element_type=f32)
        keep = keep + across(give, 0).astype(f32)
        for bit in range(1, bits):
            half = half // 2
            got = across(keep[half:].astype(bf16), bit)
            keep = keep[:half] + got.astype(f32)
        return keep.astype(bf16)

    core = seq_index % 2
    columns = out_weight.shape[1]
    layer_out = jnp.zeros((block, seq_count, columns), bf16)
    acts = [around(normed, by) for by in range(chips)]
    done = [[reduced(act, w) for w in (out_weight, other_core)] for act in acts]
    for by in range(chips):
        mine, other = [around(d, -by) for d in done[by]]
        chip = (seq_index // 2 + by) % chips
        layer_out = lax.dynamic_update_slice(
            layer_out, mine[:, None], (0, chip * 2 + core, 0)
        )
        layer_out = lax.dynamic_update_slice(
            layer_out, other[:, None], (0, chip * 2 + 1 - core, 0)
        )
    return (layer_out.reshape(block, seq_count * columns), boundary)


def solution(mesh):
    in_specs = (
        P("seq", "head"),
        P("seq", "head"),
        P("seq", None),
        P("head", "seq"),
        P("head"),
        P("head"),
        P(None, "head"),
        P("head"),
        P(),
        P(),
        P(None, "head"),
        P(),
        P("head", None, None),
        P("head"),
        P("head", "seq"),
    )
    out_specs = (P(("seq", "head"), None), P("seq", "head", None, None))
    return jax.shard_map(body, mesh=mesh, in_specs=in_specs, out_specs=out_specs, check_vma=False)
```

```python
import functools

import jax
import jax.numpy as jnp
from jax import lax
from jax.experimental import pallas as pl
from jax.experimental.pallas import tpu as pltpu
from jax.sharding import PartitionSpec as P

MIXER_HEADS = 256
HEADDIM = 64
STATE = 256
GROUPS = 8
KERNEL = 4
SPAN = 128
DINNER = 16384
EXTRA = 16
VMEM_LIMIT = 48 * 1024 * 1024
LAYER_LIMIT = 62 * 1024 * 1024

highest = lax.Precision.HIGHEST
norm_eps = 1e-05
f32 = jnp.float32
bf16 = jnp.bfloat16
MESH = pl.DeviceIdType.MESH


def silu(v):
    return v * (1.0 / (1.0 + jnp.exp(-v)))


def shifted(cur, prev8, by):
    moved = pltpu.roll(cur, by, 0)
    before = pltpu.roll(prev8, by, 0)
    row = lax.broadcasted_iota(jnp.int32, before.shape, 0)
    first = jnp.where(row < by, before, moved[:8])
    return jnp.concatenate([first, moved[8:]], axis=0)


def conv_block(in_ref, prev_ref, w_ref, b_ref, out_ref, chunk):
    width = in_ref.shape[1]
    rows = in_ref.shape[0]
    for c in range(0, width, chunk):
        cols = slice(c, c + chunk)
        cur = in_ref[:, cols].astype(f32)
        prev8 = prev_ref[:, cols]
        total = b_ref[:, cols] + w_ref[KERNEL - 1 : KERNEL, cols] * cur
        for by in range(1, KERNEL):
            k = KERNEL - 1 - by
            total = total + w_ref[k : k + 1, cols] * shifted(cur, prev8, by)
        prev_ref[:, cols] = cur[rows - 8 :]
        out_ref[:, cols] = silu(total).astype(bf16)


def spread_matrix(heads):
    h = lax.broadcasted_iota(jnp.int32, (heads, heads * HEADDIM), 0)
    c = lax.broadcasted_iota(jnp.int32, (heads, heads * HEADDIM), 1)
    return jnp.where(c // HEADDIM == h, 1.0, 0.0).astype(f32)


def spread(values, matrix):
    return jnp.dot(values, matrix, precision=highest, preferred_element_type=f32)


def softplus(v):
    e = jnp.exp(-jnp.abs(v))
    u = 1.0 + e
    series = e * (1.0 - e * (0.5 - e * (1.0 / 3.0 - 0.25 * e)))
    return jnp.maximum(v, 0.0) + jnp.where(e < 0.015625, series, jnp.log(u))


def transposed_dot(lhs, rhs):
    return lax.dot_general(
        lhs, rhs, (((1,), (1,)), ((), ())), precision=highest, preferred_element_type=f32
    )


def decay_terms(dt_ref, rate_ref):
    step = softplus(dt_ref[...])
    log = -jnp.exp(rate_ref[...]) * step
    t = lax.broadcasted_iota(jnp.int32, (SPAN, SPAN), 0)
    s = lax.broadcasted_iota(jnp.int32, (SPAN, SPAN), 1)
    lower = jnp.where(t >= s, 1.0, 0.0).astype(f32)
    eye = jnp.where(t == s, 1.0, 0.0).astype(f32)
    cumul_row = transposed_dot(log, lower)
    cumul_col = transposed_dot(lower, log)
    step_col = transposed_dot(eye, step)
    return step, step_col, cumul_row, cumul_col, t >= s


def state_kernel(
    g_ref, inner, bin_, cin, dt, rate, wx, bx, wb, wc, bb, bc, halo_x, halo_b, halo_c,
    x_out, b_out, c_out, enter_out, send_out, local_out,
    prev_x, prev_b, prev_c, state, total,
):
    i = pl.program_id(0)
    heads = dt.shape[0]

    @pl.when(i == 0)
    def _():
        prev_x[...] = halo_x[...].astype(f32)
        prev_b[...] = halo_b[...].astype(f32)
        prev_c[...] = halo_c[...].astype(f32)
        state[...] = jnp.zeros_like(state)
        total[...] = jnp.zeros_like(total)

    conv_block(inner, prev_x, wx, bx, x_out, 256)
    conv_block(bin_, prev_b, wb, bb, b_out, 256)
    conv_block(cin, prev_c, wc, bc, c_out, 256)
    step, step_col, cumul_row, cumul_col, causal = decay_terms(dt, rate)
    last = cumul_col[SPAN - 1 :]
    matrix = spread_matrix(heads)
    weights = spread(jnp.exp(last - cumul_col) * step_col, matrix)
    last8 = spread(jnp.broadcast_to(last, (8, heads)), matrix)
    enter_out[0] = state[...].astype(bf16)
    weighted = (x_out[...].astype(f32) * weights).astype(bf16)
    b_t = b_out[...].astype(f32).T.astype(bf16)
    written = jnp.dot(b_t, weighted, preferred_element_type=f32)
    state[...] = jnp.exp(last8[:1]) * state[...] + written
    total[...] += last8

    @pl.when(i == pl.num_programs(0) - 1)
    def _():
        local_out[...] = state[...]
        send_out[:STATE] = state[...].astype(bf16)
        tl = total[:1]
        high = tl.astype(bf16).astype(f32)
        row = lax.broadcasted_iota(jnp.int32, (EXTRA, tl.shape[1]), 0)
        send_out[STATE:] = jnp.where(row == 0, high, jnp.where(row == 1, tl - high, 0.0)).astype(bf16)


PARTS = 4


def chain_kernel(
    x, b, c, dt, rate, skip, enter, local, sent, y_out, prior_out,
    land, hop, send_sem, recv_sem,
):
    i = pl.program_id(0)
    seq = lax.axis_index("seq")
    last = 3
    wide = land.shape[2]

    def copy(k):
        return pltpu.make_async_remote_copy(
            src_ref=hop.at[k], dst_ref=land.at[k],
            send_sem=send_sem.at[k], recv_sem=recv_sem.at[k],
            device_id={"seq": (seq + 1) % 4}, device_id_type=MESH,
        )

    def joined(k):
        cols = slice(k * wide, (k + 1) * wide)
        own = sent[STATE : STATE + 1, cols].astype(f32) + sent[STATE + 1 : STATE + 2, cols].astype(f32)
        tail = land[k, STATE:].astype(f32)
        hop[k, :STATE] = (
            jnp.exp(own) * land[k, :STATE].astype(f32) + local[:, cols]
        ).astype(bf16)
        log = tail[0:1] + tail[1:2] + own
        high = log.astype(bf16).astype(f32)
        row = lax.broadcasted_iota(jnp.int32, (EXTRA, wide), 0)
        hop[k, STATE:] = jnp.where(row == 0, high, jnp.where(row == 1, log - high, 0.0)).astype(bf16)

    @pl.when(i == 0)
    def _():
        barrier = pltpu.get_barrier_semaphore()

        for by in (1, 3):
            pl.semaphore_signal(
                barrier, inc=1, device_id={"seq": (seq + by) % 4}, device_id_type=MESH
            )
        pl.semaphore_wait(barrier, 2)

        @pl.when(seq == 0)
        def _():
            for k in range(PARTS):
                hop[k] = sent[:, k * wide : (k + 1) * wide]
                copy(k).start()

        @pl.when(seq == 1)
        def _():
            for k in range(PARTS):
                copy(k).wait_recv()
                joined(k)
                copy(k).start()

    local_kernel(x, b, c, dt, rate, skip, enter, y_out)

    @pl.when(i == pl.num_programs(0) - 1)
    def _():
        @pl.when(seq == 2)
        def _():
            for k in range(PARTS):
                copy(k).wait_recv()
                joined(k)
                copy(k).start()

        @pl.when(seq == 3)
        def _():
            for k in range(PARTS):
                copy(k).wait_recv()

        @pl.when(seq > 0)
        def _():
            for k in range(PARTS):
                prior_out[:, k * wide : (k + 1) * wide] = land[k]

        @pl.when(seq == 0)
        def _():
            prior_out[...] = jnp.zeros_like(prior_out)

        @pl.when(seq < last)
        def _():
            for k in range(PARTS):
                copy(k).wait_send()


def local_kernel(x, b, c, dt, rate, skip, enter, y_out):
    heads = dt.shape[0]
    step, step_col, cumul_row, cumul_col, causal = decay_terms(dt, rate)
    matrix = spread_matrix(heads)
    scores = lax.dot_general(
        c[...], b[...], (((1,), (1,)), ((), ())), preferred_element_type=f32
    )
    row_term = jnp.log(step) - cumul_row
    growth = spread(jnp.exp(cumul_col), matrix)
    skip_row = spread(jnp.broadcast_to(skip[...], (8, heads)), matrix)[:1]
    lane = lax.broadcasted_iota(jnp.int32, (SPAN, 2 * HEADDIM), 1)
    zero = jnp.zeros((SPAN, 2 * HEADDIM), bf16)
    for pair in range(heads // 2):
        cols = slice(pair * 2 * HEADDIM, (pair + 1) * 2 * HEADDIM)
        mixers = []
        for h in (2 * pair, 2 * pair + 1):
            power = jnp.where(causal, cumul_col[:, h : h + 1] + row_term[h : h + 1], -1e30)
            mixers.append((scores * jnp.exp(power)).astype(bf16))
        xp = x[:, cols]
        both = jnp.concatenate(
            [jnp.where(lane < HEADDIM, xp, zero), jnp.where(lane >= HEADDIM, xp, zero)], axis=0
        )
        inside = jnp.dot(
            jnp.concatenate(mixers, axis=1), both, preferred_element_type=f32
        )
        carried = jnp.dot(c[...], enter[0, :, cols], preferred_element_type=f32)
        y_out[:, cols] = (
            inside + growth[:, cols] * carried + skip_row[:, cols] * xp.astype(f32)
        )


def output_kernel(
    meta, y, c, gate, dt, rate, gain, gathered, own_tail, init, local, normed_out, boundary_out,
    incoming, entering, mixed, offset, *, block, halves, whole_group, chained,
):
    i = pl.program_id(0)
    heads = dt.shape[0]
    width = y.shape[1]
    count = gathered.shape[0]

    @pl.when(i == 0)
    def _():
        place = meta[0]
        rate_sum = jnp.zeros((1, width), f32)
        incoming[...] = jnp.zeros_like(incoming)
        if chained:
            tail = gathered[0, STATE:].astype(f32)
            incoming[...] = gathered[0, :STATE].astype(f32)
            rate_sum = tail[0:1] + tail[1:2]
        for k in range(-1 if chained else count - 2, -1, -1):
            live = k < place
            tail = gathered[k, STATE:].astype(f32)
            factor = jnp.where(live, jnp.exp(rate_sum), 0.0)
            incoming[...] += factor * gathered[k, :STATE].astype(f32)
            rate_sum = rate_sum + jnp.where(live, tail[0:1] + tail[1:2], 0.0)
        tail = (own_tail[...] if chained else gathered[place, STATE:]).astype(f32)
        own = jnp.exp(tail[0:1] + tail[1:2])
        for k in range(0, width, 256):
            cols = slice(k, k + 256)
            value = incoming[:, cols] + jnp.exp(rate_sum[:, cols]) * init[cols, :].T
            entering[:, cols] = value.astype(bf16)
            boundary_out[cols, :] = (own[:, cols] * value + local[:, cols]).T
        offset[...] = jnp.zeros_like(offset)

    step, step_col, cumul_row, cumul_col, causal = decay_terms(dt, rate)
    cumul_col = cumul_col + offset[:1]
    offset[...] = jnp.broadcast_to(cumul_col[SPAN - 1 :], offset.shape)
    growth = spread(jnp.exp(cumul_col), spread_matrix(heads))
    squares = jnp.zeros((SPAN, 1), f32)
    for k in range(0, width, 256):
        cols = slice(k, k + 256)
        carried = jnp.dot(c[...], entering[:, cols], preferred_element_type=f32)
        value = (y[:, cols] + growth[:, cols] * carried) * silu(gate[:, cols].astype(f32))
        mixed[:, cols] = value
        squares = squares + jnp.sum(value * value, axis=1, keepdims=True)
    if whole_group:
        inverse = lax.rsqrt(squares / width + norm_eps)
    piece = block // halves
    for q in range(SPAN // piece):
        rows = slice(q * piece, (q + 1) * piece)
        first = meta[1 + i * (SPAN // block) + q // halves]
        first = first + (q % halves) * (normed_out.shape[0] // halves)
        value = mixed[rows, :]
        if whole_group:
            value = value * inverse[rows] * gain[...]
        normed_out[pl.ds(pl.multiple_of(first, piece), piece), :] = value.astype(normed_out.dtype)


def partner_of(place, bit):
    size = 1 << bit
    return place + (1 - 2 * ((place // size) % 2)) * size


HALVES = 2
GROUP = 4
QUARTERS = 4
MULTIPLY, FIRST, SECOND, THIRD, ARRIVED, LOADED = range(6)
FIRST_Z = (0, 3, 8, 12)
ORDER = (
    82, 6, 83, 3, 81, 1, 22, 80, 0, 2, 17, 4, 18, 16, 33, 64, 38, 9, 20, 32,
    8, 7, 34, 54, 11, 36, 5, 23, 25, 27, 39, 65, 15, 12, 24, 43, 14, 41, 21, 10,
    40, 52, 28, 31, 37, 30, 57, 13, 47, 26, 44, 49, 59, 56, 55, 42, 29, 46, 50, 58,
    63, 60, 19, 45, 53, 48, 62, 35, 61, 51,
)


def tanh_silu(v):
    half = 0.5 * v
    return half + half * jnp.tanh(half)


def two_terms(values):
    high = values.astype(bf16)
    low = (values - high.astype(f32)).astype(bf16)
    return jnp.concatenate([high, low], axis=1)


def fill_matrix(matrix):
    heads = matrix.shape[0] // 2
    h = lax.broadcasted_iota(jnp.int32, matrix.shape, 0) % heads
    c = lax.broadcasted_iota(jnp.int32, matrix.shape, 1) // HEADDIM
    matrix[...] = jnp.where(c == h, 1.0, 0.0).astype(bf16)


def token_decays(dt, rate):
    step = softplus(dt).T
    log = -jnp.exp(rate) * step
    t = lax.broadcasted_iota(jnp.int32, (SPAN, SPAN), 0)
    s = lax.broadcasted_iota(jnp.int32, (SPAN, SPAN), 1)
    lower = jnp.where(t >= s, 1.0, 0.0).astype(f32)
    cumul = [
        jnp.dot(lower, log[k : k + SPAN], precision=highest, preferred_element_type=f32)
        for k in range(0, log.shape[0], SPAN)
    ]
    return step, cumul, t >= s


def conv_tile(cur, prev8, weight, bias):
    total = bias + weight[KERNEL - 1 : KERNEL] * cur
    for by in range(1, KERNEL):
        k = KERNEL - 1 - by
        total = total + weight[k : k + 1] * shifted(cur, prev8, by)
    return tanh_silu(total).astype(bf16)


def layer_kernel(
    inner, gate_all, bc_all, dt, rate, skip, wx, bx, wbc, bbc, tail_x, tail_bc, init_all, gain, w_own,
    out, state_out,
    x, gate, bc, init, halo_x, halo_bc, prev, b_t, weight, factors, matrix, scaled, total, state,
    land, hop, mixed,
    w, acts, keep, y_send, y_recv, a_send, a_recv, b_send, b_recv, x_send, x_recv,
    in_sem, load_sem, halo_send, halo_recv, hop_send, hop_recv, w_sem, w_send, w_recv,
    act_send_sem, act_recv_sem, send_sem, recv_sem, x_send_sem, x_recv_sem,
):
    seq = lax.axis_index("seq")
    head = lax.axis_index("head")
    rows, width = x.shape
    heads = dt.shape[0]
    spans = rows // SPAN
    strip = width // QUARTERS
    wide = w.shape[2]
    per = w_own.shape[1] // wide
    count = keep.shape[0]
    part = count // 2
    piece = out.shape[0] // HALVES
    half_rows = acts.shape[2]
    other_chip = (seq + 2) % 4
    near = [partner_of(head, bit) for bit in range(3)]
    across = [{"head": place} for place in near]
    over_x = {"seq": other_chip}
    after = {"seq": (seq + 1) % 4}
    other_core = {"seq": partner_of(seq, 0)}
    firsts = [pl.multiple_of((head + g) * STATE, STATE) for g in (0, GROUPS)]
    chunk = 256

    def remote(source, dest, send, recv, target):
        return pltpu.make_async_remote_copy(
            src_ref=source, dst_ref=dest, send_sem=send, recv_sem=recv,
            device_id=target, device_id_type=MESH,
        )

    def strip_of(k):
        return pl.ds(pl.multiple_of(k * strip, strip), strip)

    def inner_copy(k):
        cols = slice(k * strip, (k + 1) * strip)
        return pltpu.make_async_copy(inner.at[:, cols], x.at[:, cols], in_sem.at[k])

    def bc_copy(k):
        return pltpu.make_async_copy(
            bc_all.at[:, pl.ds(firsts[k], STATE)], bc.at[k], load_sem.at[k]
        )

    def gate_copy():
        return pltpu.make_async_copy(gate_all, gate, load_sem.at[2])

    def init_copy():
        return pltpu.make_async_copy(init_all, init, load_sem.at[3])

    def state_copy():
        return pltpu.make_async_copy(state, state_out, load_sem.at[4])

    def own_weights(k):
        return pltpu.make_async_copy(
            w_own.at[:, k * wide : (k + 1) * wide], w.at[k], w_sem.at[k]
        )

    def other_weights(k):
        narrow = wide // 2
        cols = pl.ds(pl.multiple_of(k * narrow, narrow), narrow)
        place = pl.ds(pl.multiple_of(k % 2 * narrow, narrow), narrow)
        return remote(
            w_own.at[:, cols], w.at[per + k // 2, :, place], w_send.at[k], w_recv.at[k], other_core
        )

    def halo_copies():
        last = pl.ds(rows - 16, 16)
        pairs = [(inner.at[last], halo_x)] + [
            (bc_all.at[last, pl.ds(firsts[k], STATE)], halo_bc.at[k]) for k in range(2)
        ]
        return [
            remote(source, dest, halo_send.at[k], halo_recv.at[k], after)
            for k, (source, dest) in enumerate(pairs)
        ]

    def hop_copy(k):
        return remote(hop.at[k], land.at[k], hop_send.at[k], hop_recv.at[k], after)

    def act_copy(half):
        return remote(
            acts.at[0, half], acts.at[1, half], act_send_sem.at[half], act_recv_sem.at[half], over_x
        )

    def chip_copy(k):
        return remote(x_send.at[k], x_recv.at[k], x_send_sem.at[k], x_recv_sem.at[k], over_x)

    def turned(t):
        value = 0
        for k in FIRST_Z:
            value = value + jnp.where(t == k, 1, 0)
        return value

    def head_copy(stage, t):
        source, dest = ((y_send, y_recv), (a_send, a_recv), (b_send, b_recv))[stage]
        target = across[2]
        if stage < 2:
            target = {"head": near[stage] + turned(t) * (near[1 - stage] - near[stage])}
        return remote(
            source.at[t], dest.at[t], send_sem.at[stage, t], recv_sem.at[stage, t], target
        )

    for k in range(2):
        bc_copy(k).start()
    for k in range(QUARTERS):
        inner_copy(k).start()

    barrier = pltpu.get_barrier_semaphore()
    greeted = across + [over_x, after, {"seq": (seq + 3) % 4}]
    for target in greeted:
        pl.semaphore_signal(barrier, inc=1, device_id=target, device_id_type=MESH)

    init_copy().start()
    gate_copy().start()

    fill_matrix(matrix)
    step, cumul, causal = token_decays(dt[...], rate[...])
    ends = [value[SPAN - 1 :] for value in cumul]
    later = jnp.zeros_like(ends[0])
    for k in range(spans - 1, -1, -1):
        span = slice(k * SPAN, (k + 1) * SPAN)
        later = later + ends[k]
        weight[span] = two_terms(jnp.exp(later - cumul[k]) * step[span])
    row = lax.broadcasted_iota(jnp.int32, (16, heads), 0)
    high = later.astype(bf16).astype(f32)
    total[...] = two_terms(jnp.where(row < 8, high, later - high))

    pl.semaphore_wait(barrier, len(greeted))

    @pl.when(seq < 3)
    def _():
        for copy in halo_copies():
            copy.start()

    for k in range(per):
        own_weights(k).start()

    for k in range(spans):
        middle = 0.5 * ends[k]
        factors[k] = two_terms(
            jnp.concatenate(
                [
                    jnp.exp(cumul[k] - middle),
                    jnp.exp(middle - cumul[k]) * step[k * SPAN : (k + 1) * SPAN],
                    jnp.broadcast_to(jnp.exp(middle), (8, heads)),
                    jnp.broadcast_to(skip[...], (8, heads)),
                ],
                axis=0,
            )
        )

    def conv_rows(source, k, cols, before, kernel, bias):
        span = slice(k * SPAN, (k + 1) * SPAN)
        if k:
            before = source[k * SPAN - 16 : k * SPAN, cols].astype(f32)[8:]
        value = conv_tile(source[span, cols].astype(f32), before, kernel, bias)
        source[span, cols] = value
        return value

    def conv_bc(k):
        for g in range(2):
            at = pl.ds(firsts[g], STATE)
            before = None if k else prev[:, strip + g * STATE : strip + (g + 1) * STATE]
            value = conv_rows(bc.at[g], k, slice(0, STATE), before, wbc[:, at], bbc[:, at])
            if g == 0:
                b_t[:, k * SPAN : (k + 1) * SPAN] = value.astype(f32).T.astype(bf16)

    for k in range(2):
        bc_copy(k).wait()
    for k in range(spans - 1, 0, -1):
        conv_bc(k)

    @pl.when(seq > 0)
    def _():
        for copy in halo_copies():
            copy.wait_recv()
        for g in range(2):
            prev[:, strip + g * STATE : strip + (g + 1) * STATE] = halo_bc[g].astype(f32)[8:]

    @pl.when(seq == 0)
    def _():
        for g in range(2):
            prev[8 - KERNEL + 1 :, strip + g * STATE : strip + (g + 1) * STATE] = tail_bc[
                :, pl.ds(firsts[g], STATE)
            ].astype(f32)
        land[...] = jnp.zeros_like(land)

    conv_bc(0)

    def totals(k):
        spread_log = jnp.dot(total[...], matrix[:, strip_of(k)], preferred_element_type=f32)
        return spread_log[0:1] + spread_log[8:9]

    def fill_hop(k, value, log):
        hop[k, :STATE] = value.astype(bf16)
        top = log.astype(bf16).astype(f32)
        line = lax.broadcasted_iota(jnp.int32, (EXTRA, strip), 0)
        hop[k, STATE:] = jnp.where(line == 0, top, jnp.where(line == 1, log - top, 0.0)).astype(bf16)
        hop_copy(k).start()

    def pass_on(k):
        hop_copy(k).wait_recv()
        own = totals(k)
        tail = land[k, STATE:].astype(f32)
        fill_hop(
            k,
            jnp.exp(own) * land[k, :STATE].astype(f32) + state[:, strip_of(k)],
            tail[0:1] + tail[1:2] + own,
        )

    for k in range(QUARTERS):
        inner_copy(k).wait()

    def quarter(q, carry):
        @pl.when(seq > 0)
        def _():
            prev[:, :strip] = halo_x[:, strip_of(q)].astype(f32)[8:]

        @pl.when(seq == 0)
        def _():
            prev[8 - KERNEL + 1 :, :strip] = tail_x[:, strip_of(q)].astype(f32)

        for k in range(spans - 1, -1, -1):
            span = slice(k * SPAN, (k + 1) * SPAN)
            for c in range(0, strip, chunk):
                at = pl.ds(pl.multiple_of(q * strip + c, chunk), chunk)
                value = conv_rows(x, k, at, prev[:, c : c + chunk], wx[:, at], bx[:, at])
                factor = jnp.dot(weight[span], matrix[:, at], preferred_element_type=f32)
                scaled[span, c : c + chunk] = (value.astype(f32) * factor).astype(bf16)
        state[:, strip_of(q)] = jnp.dot(b_t[...], scaled[...], preferred_element_type=f32)

        @pl.when(seq == 0)
        def _():
            fill_hop(q, state[:, strip_of(q)], totals(q))

        @pl.when((seq == 1) & (q > 0))
        def _():
            pass_on(q - 1)

        other_weights(q).start()
        return carry

    lax.fori_loop(0, QUARTERS, quarter, 0)

    @pl.when(seq == 1)
    def _():
        pass_on(QUARTERS - 1)

    @pl.when(seq == 2)
    def _():
        def relay(k, carry):
            pass_on(k)
            return carry

        lax.fori_loop(0, QUARTERS, relay, 0)

    @pl.when(seq == 3)
    def _():
        for k in range(QUARTERS):
            hop_copy(k).wait_recv()

    init_copy().wait()
    gate_copy().wait()

    def enter(k, carry):
        tail = land[k, STATE:].astype(f32)
        factor = jnp.exp(tail[0:1] + tail[1:2])
        for c in range(0, strip, chunk):
            at = pl.ds(pl.multiple_of(k * strip + c, chunk), chunk)
            state[:, at] = (
                land[k, :STATE, c : c + chunk].astype(f32) + factor[:, c : c + chunk] * init[at, :].T
            )
        return carry

    lax.fori_loop(0, QUARTERS, enter, 0)

    def gated(i, carry):
        first_row = pl.multiple_of(i * SPAN, SPAN)
        span = pl.ds(first_row, SPAN)
        c_rows = bc[1, span]
        scores = lax.dot_general(
            c_rows, bc[0, span], (((1,), (1,)), ((), ())), preferred_element_type=f32
        )
        left = jnp.concatenate([jnp.where(causal, scores, 0.0).astype(bf16), c_rows], axis=1)
        turned_b = b_t[:, span]
        squares = jnp.zeros((SPAN, 1), f32)
        broad = 1024
        for k in range(0, width, broad):
            cols = slice(k, k + broad)
            spread_all = jnp.dot(factors[i], matrix[:, cols], preferred_element_type=f32)
            half_decay = spread_all[2 * SPAN : 2 * SPAN + 1]
            value = x[span, cols].astype(f32)
            weighted = (value * spread_all[SPAN : 2 * SPAN]).astype(bf16)
            before = half_decay * state[:, cols]
            inside = jnp.dot(
                left, jnp.concatenate([weighted, before.astype(bf16)], axis=0),
                preferred_element_type=f32,
            )
            written = jnp.dot(turned_b, weighted, preferred_element_type=f32)
            state[:, cols] = half_decay * (before + written)
            value = spread_all[:SPAN] * inside + spread_all[2 * SPAN + 8 : 2 * SPAN + 9] * value
            value = value * tanh_silu(gate[span, cols].astype(f32))
            mixed[:, cols] = value
            squares = squares + jnp.sum(value * value, axis=1, keepdims=True)
        inverse = lax.rsqrt(squares / width + norm_eps)
        block = HALVES * piece
        for p in range(SPAN // piece):
            lines = slice(p * piece, (p + 1) * piece)
            owner = i * (SPAN // block) + p // HALVES
            slot = 0
            for bit in range(3):
                differs = (owner // (1 << bit) + head // (1 << bit)) % 2
                slot = slot + differs * (4 >> bit)
            acts[0, p % HALVES, pl.ds(pl.multiple_of(slot * piece, piece), piece)] = (
                mixed[lines, :] * inverse[lines] * gain[...]
            ).astype(bf16)
        return carry

    lax.fori_loop(0, spans, gated, 0)
    for half in range(HALVES):
        act_copy(half).start()
    state_copy().start()

    def multiply(t):
        place, half, group = t // part, (t % part) // GROUP, t % GROUP
        product = jnp.dot(acts[place, half], w[group], preferred_element_type=f32)
        near_z = turned(t) == 1
        two = 2 * piece
        middle = [product[two : 2 * two], product[2 * two : 3 * two]]
        y_send[t, :two] = jnp.where(near_z, middle[0], middle[1]).astype(bf16)
        y_send[t, two:] = product[3 * two :].astype(bf16)
        head_copy(0, t).start()
        keep[t, :two] = product[:two]
        keep[t, two:] = jnp.where(near_z, middle[1], middle[0])

    def first_stage(t):
        head_copy(0, t).wait_recv()
        a_send[t] = (keep[t, 2 * piece :] + y_recv[t, 2 * piece :].astype(f32)).astype(bf16)
        head_copy(1, t).start()
        keep[t, : 2 * piece] = keep[t, : 2 * piece] + y_recv[t, : 2 * piece].astype(f32)

    def second_stage(t):
        head_copy(1, t).wait_recv()
        b_send[t] = (keep[t, piece : 2 * piece] + a_recv[t, piece:].astype(f32)).astype(bf16)
        head_copy(2, t).start()
        keep[t, :piece] = keep[t, :piece] + a_recv[t, :piece].astype(f32)

    def place_out(t, home, value):
        group = t % GROUP
        core = (home % 2 + group // per) % 2
        column = ((home // 2) * 2 + core) * (per * wide) + (group % per) * wide
        first = ((t % part) // GROUP) * piece
        out[
            pl.ds(pl.multiple_of(first, piece), piece), pl.ds(pl.multiple_of(column, wide), wide)
        ] = value

    def third_stage(t):
        head_copy(2, t).wait_recv()
        value = (keep[t, :piece] + b_recv[t].astype(f32)).astype(bf16)

        @pl.when(t < part)
        def _():
            place_out(t, seq, value)

        @pl.when(t >= part)
        def _():
            x_send[t - part] = value
            chip_copy(t - part).start()

    def event(i, carry):
        code = 0
        for k, value in enumerate(ORDER):
            code = code + jnp.where(i == k, value, 0)
        kind, t = code // 16, code % 16

        @pl.when(kind == MULTIPLY)
        def _():
            multiply(t)

        @pl.when(kind == FIRST)
        def _():
            first_stage(t)

        @pl.when(kind == SECOND)
        def _():
            second_stage(t)

        @pl.when(kind == THIRD)
        def _():
            third_stage(t)

        @pl.when(kind == ARRIVED)
        def _():
            act_copy(t).wait_recv()

        @pl.when((kind == LOADED) & (t < per))
        def _():
            own_weights_at(t)

        @pl.when((kind == LOADED) & (t >= per))
        def _():
            for k in range(2):
                other_weights(2 * (t - per) + k).wait_recv()

        return carry

    def own_weights_at(t):
        for k in range(per):
            @pl.when(t == k)
            def _():
                own_weights(k).wait()

    lax.fori_loop(0, len(ORDER), event, 0)

    def collect(k, carry):
        chip_copy(k).wait_recv()
        place_out(k, other_chip, x_recv[k])
        chip_copy(k).wait_send()
        return carry

    def drain(t, carry):
        for stage in range(3):
            head_copy(stage, t).wait_send()
        return carry

    lax.fori_loop(0, part, collect, 0)
    for half in range(HALVES):
        act_copy(half).wait_send()
    for k in range(QUARTERS):
        other_weights(k).wait_send()
    state_copy().wait()

    @pl.when(seq < 3)
    def _():
        for k in range(QUARTERS):
            hop_copy(k).wait_send()
        for copy in halo_copies():
            copy.wait_send()

    lax.fori_loop(0, count, drain, 0)


def finish_kernel(summed, state, out, boundary_out):
    out[...] = summed[...]
    boundary_out[...] = state[...].T


def layer(inner, gate, bc, dt, rate, skip, wx, bx, wbc, bbc, tail_x, tail_bc, init, gain, own):
    rows, width = inner.shape
    heads = dt.shape[0]
    columns = own.shape[1]
    strip = width // QUARTERS
    block = rows // 8
    piece = block // HALVES
    wide = 2 * columns // GROUP
    part = HALVES * GROUP
    count = 2 * part
    spans = rows // SPAN
    anywhere = pl.BlockSpec(memory_space=pl.ANY)
    vmem = pl.BlockSpec(memory_space=pltpu.VMEM)
    slots = (QUARTERS, STATE + EXTRA, strip)
    dma = pltpu.SemaphoreType.DMA
    summed, state = pl.pallas_call(
        layer_kernel,
        in_specs=[anywhere] * 3 + [vmem] * 9 + [anywhere, vmem, anywhere],
        out_specs=[vmem, anywhere],
        out_shape=[
            jax.ShapeDtypeStruct((block, 4 * columns), bf16),
            jax.ShapeDtypeStruct((STATE, width), f32),
        ],
        scratch_shapes=[
            pltpu.VMEM((rows, width), bf16),
            pltpu.VMEM((rows, width), bf16),
            pltpu.VMEM((2, rows, STATE), bf16),
            pltpu.VMEM((width, STATE), f32),
            pltpu.VMEM((16, width), bf16),
            pltpu.VMEM((2, 16, STATE), bf16),
            pltpu.VMEM((8, strip + 2 * STATE), f32),
            pltpu.VMEM((STATE, rows), bf16),
            pltpu.VMEM((rows, 2 * heads), bf16),
            pltpu.VMEM((spans, 2 * SPAN + 16, 2 * heads), bf16),
            pltpu.VMEM((2 * heads, width), bf16),
            pltpu.VMEM((rows, strip), bf16),
            pltpu.VMEM((16, 2 * heads), bf16),
            pltpu.VMEM((STATE, width), f32),
            pltpu.VMEM(slots, bf16),
            pltpu.VMEM(slots, bf16),
            pltpu.VMEM((SPAN, width), f32),
            pltpu.VMEM((GROUP, width, wide), bf16),
            pltpu.VMEM((2, HALVES, rows // HALVES, width), bf16),
            pltpu.VMEM((count, 4 * piece, wide), f32),
            pltpu.VMEM((count, 4 * piece, wide), bf16),
            pltpu.VMEM((count, 4 * piece, wide), bf16),
            pltpu.VMEM((count, 2 * piece, wide), bf16),
            pltpu.VMEM((count, 2 * piece, wide), bf16),
            pltpu.VMEM((count, piece, wide), bf16),
            pltpu.VMEM((count, piece, wide), bf16),
            pltpu.VMEM((part, piece, wide), bf16),
            pltpu.VMEM((part, piece, wide), bf16),
            dma((QUARTERS,)),
            dma((5,)),
            dma((3,)),
            dma((3,)),
            dma((QUARTERS,)),
            dma((QUARTERS,)),
            dma((GROUP // 2,)),
            dma((QUARTERS,)),
            dma((QUARTERS,)),
            dma((HALVES,)),
            dma((HALVES,)),
            dma((3, count)),
            dma((3, count)),
            dma((part,)),
            dma((part,)),
        ],
        compiler_params=pltpu.CompilerParams(
            vmem_limit_bytes=LAYER_LIMIT, collective_id=0, has_side_effects=True
        ),
        name="layer",
    )(
        inner, gate, bc, dt, rate[None], skip[None], wx, bx[None], wbc, bbc[None], tail_x, tail_bc,
        init.reshape(width, STATE), gain[None], own,
    )
    steps = 4
    return pl.pallas_call(
        finish_kernel,
        grid=(steps,),
        in_specs=[
            pl.BlockSpec((block, columns), lambda i: (0, i)),
            pl.BlockSpec((STATE, width // steps), lambda i: (0, i)),
        ],
        out_specs=[
            pl.BlockSpec((block, columns), lambda i: (0, i)),
            pl.BlockSpec((width // steps, STATE), lambda i: (i, 0)),
        ],
        out_shape=[
            jax.ShapeDtypeStruct((block, 4 * columns), bf16),
            jax.ShapeDtypeStruct((width, STATE), f32),
        ],
        compiler_params=params(),
        name="finish",
    )(summed, state)


def params():
    return pltpu.CompilerParams(vmem_limit_bytes=VMEM_LIMIT)


def body(
    inner_input,
    gate_input,
    bc_input,
    dt_input,
    log_rate,
    skip_weight,
    conv_weight_x,
    conv_bias_x,
    conv_weight_bc,
    conv_bias_bc,
    conv_tail_x,
    conv_tail_bc,
    init_state,
    norm_gain,
    out_weight,
):
    seq_count = lax.axis_size("seq")
    head_count = lax.axis_size("head")
    seq_index = lax.axis_index("seq")
    head_index = lax.axis_index("head")
    rows, width = inner_input.shape
    heads = dt_input.shape[0]
    per_group = MIXER_HEADS // GROUPS
    group = (head_index * heads // per_group).astype(jnp.int32)
    spans = rows // SPAN
    block = rows // head_count
    group_width = DINNER // GROUPS
    whole_group = width == group_width

    projected = (
        seq_count == 4 and head_count == 8 and whole_group and rows == 512 and width == 2048
        and out_weight.shape[1] % 512 == 0
    )
    if projected:
        out, boundary = layer(
            inner_input, gate_input, bc_input, dt_input, log_rate, skip_weight, conv_weight_x,
            conv_bias_x, conv_weight_bc, conv_bias_bc, conv_tail_x, conv_tail_bc, init_state,
            norm_gain, out_weight,
        )
        return (out, boundary.reshape(1, heads, HEADDIM, STATE))

    other_core = lax.ppermute(out_weight, "seq", [(i, i ^ 1) for i in range(seq_count)])

    def pair_columns(table, axis):
        return [
            lax.dynamic_slice_in_dim(table, (g + group) * STATE, STATE, axis) for g in (0, GROUPS)
        ]

    tail_rows = rows - KERNEL + 1
    last_rows = jnp.concatenate(
        [inner_input[tail_rows:]] + pair_columns(bc_input[tail_rows:], 1), axis=1
    )
    arrived = lax.ppermute(last_rows, "seq", [(i, i + 1) for i in range(seq_count - 1)])
    first_rows = jnp.concatenate([conv_tail_x] + pair_columns(conv_tail_bc, 1), axis=1)
    halo = jnp.where(seq_index == 0, first_rows, arrived)
    halo = jnp.pad(halo, ((8 - KERNEL + 1, 0), (0, 0)))
    rate = log_rate[:, None]

    def const(shape, *index):
        return pl.BlockSpec(shape, lambda i, *_: index)

    span_x = pl.BlockSpec((SPAN, width), lambda i, *_: (i, 0))
    span_bc = pl.BlockSpec((SPAN, STATE), lambda i, *_: (i, 0))
    span_dt = pl.BlockSpec((heads, SPAN), lambda i, *_: (0, i))

    conv_x, conv_b, conv_c, enter, sent, local = pl.pallas_call(
        state_kernel,
        grid_spec=pltpu.PrefetchScalarGridSpec(
            num_scalar_prefetch=1,
            grid=(spans,),
            in_specs=[
                span_x,
                pl.BlockSpec((SPAN, STATE), lambda i, g: (i, g[0])),
                pl.BlockSpec((SPAN, STATE), lambda i, g: (i, g[0] + GROUPS)),
                span_dt,
                const((heads, 1), 0, 0),
                const((KERNEL, width), 0, 0),
                const((1, width), 0, 0),
                pl.BlockSpec((KERNEL, STATE), lambda i, g: (0, g[0])),
                pl.BlockSpec((KERNEL, STATE), lambda i, g: (0, g[0] + GROUPS)),
                pl.BlockSpec((1, STATE), lambda i, g: (0, g[0])),
                pl.BlockSpec((1, STATE), lambda i, g: (0, g[0] + GROUPS)),
                const((8, width), 0, 0),
                const((8, STATE), 0, width // STATE),
                const((8, STATE), 0, width // STATE + 1),
            ],
            out_specs=[
                span_x,
                span_bc,
                span_bc,
                pl.BlockSpec((1, STATE, width), lambda i, *_: (i, 0, 0)),
                const((STATE + EXTRA, width), 0, 0),
                const((STATE, width), 0, 0),
            ],
            scratch_shapes=[
                pltpu.VMEM((8, width), f32),
                pltpu.VMEM((8, STATE), f32),
                pltpu.VMEM((8, STATE), f32),
                pltpu.VMEM((STATE, width), f32),
                pltpu.VMEM((8, width), f32),
            ],
        ),
        out_shape=[
            jax.ShapeDtypeStruct((rows, width), bf16),
            jax.ShapeDtypeStruct((rows, STATE), bf16),
            jax.ShapeDtypeStruct((rows, STATE), bf16),
            jax.ShapeDtypeStruct((spans, STATE, width), bf16),
            jax.ShapeDtypeStruct((STATE + EXTRA, width), bf16),
            jax.ShapeDtypeStruct((STATE, width), f32),
        ],
        compiler_params=params(),
        name="conv_and_states",
    )(
        group[None],
        inner_input, bc_input, bc_input, dt_input, rate,
        conv_weight_x, conv_bias_x[None], conv_weight_bc, conv_weight_bc,
        conv_bias_bc[None], conv_bias_bc[None], halo, halo, halo,
    )

    chained = seq_count == 4 and width % (PARTS * 128) == 0
    local_specs = [
        span_x,
        span_bc,
        span_bc,
        span_dt,
        const((heads, 1), 0, 0),
        const((1, heads), 0, 0),
        pl.BlockSpec((1, STATE, width), lambda i: (i, 0, 0)),
    ]
    local_args = (conv_x, conv_b, conv_c, dt_input, rate, skip_weight[None], enter)
    y_shape = jax.ShapeDtypeStruct((rows, width), f32)
    if chained:
        slots = (PARTS, STATE + EXTRA, width // PARTS)
        y_local, prior = pl.pallas_call(
            chain_kernel,
            grid=(spans,),
            in_specs=local_specs
            + [const((STATE, width), 0, 0), const((STATE + EXTRA, width), 0, 0)],
            out_specs=[span_x, const((STATE + EXTRA, width), 0, 0)],
            out_shape=[y_shape, jax.ShapeDtypeStruct((STATE + EXTRA, width), bf16)],
            scratch_shapes=[
                pltpu.VMEM(slots, bf16),
                pltpu.VMEM(slots, bf16),
                pltpu.SemaphoreType.DMA((PARTS,)),
                pltpu.SemaphoreType.DMA((PARTS,)),
            ],
            compiler_params=pltpu.CompilerParams(
                vmem_limit_bytes=VMEM_LIMIT, collective_id=1, has_side_effects=True
            ),
            name="local_outputs_and_chain",
        )(*local_args, local, sent)
        gathered = prior[None]
    else:
        gathered = lax.all_gather(sent, "seq")
        y_local = pl.pallas_call(
            local_kernel,
            grid=(spans,),
            in_specs=local_specs,
            out_specs=span_x,
            out_shape=y_shape,
            compiler_params=params(),
            name="local_outputs",
        )(*local_args)

    bits = head_count.bit_length() - 1
    distance = jnp.arange(head_count, dtype=jnp.int32) ^ head_index
    slot = jnp.zeros_like(distance)
    for bit in range(bits):
        slot = slot + ((distance >> bit) & 1) * (head_count >> (bit + 1))
    meta = jnp.concatenate([seq_index[None].astype(jnp.int32), slot.astype(jnp.int32) * block])

    normed, boundary = pl.pallas_call(
        functools.partial(
            output_kernel, block=block, halves=1, whole_group=whole_group, chained=chained
        ),
        grid_spec=pltpu.PrefetchScalarGridSpec(
            num_scalar_prefetch=1,
            grid=(spans,),
            in_specs=[
                span_x,
                span_bc,
                span_x,
                span_dt,
                const((heads, 1), 0, 0),
                const((1, width), 0, 0),
                const((gathered.shape[0], STATE + EXTRA, width), 0, 0, 0),
                const((EXTRA, width), STATE // EXTRA, 0),
                const((width, STATE), 0, 0),
                const((STATE, width), 0, 0),
            ],
            out_specs=[const((rows, width), 0, 0), const((width, STATE), 0, 0)],
            scratch_shapes=[
                pltpu.VMEM((STATE, width), f32),
                pltpu.VMEM((STATE, width), bf16),
                pltpu.VMEM((SPAN, width), f32),
                pltpu.VMEM((8, heads), f32),
            ],
        ),
        out_shape=[
            jax.ShapeDtypeStruct((rows, width), bf16 if whole_group else f32),
            jax.ShapeDtypeStruct((width, STATE), f32),
        ],
        compiler_params=params(),
        name="gated_outputs",
    )(
        meta,
        y_local, conv_c, gate_input, dt_input, rate, norm_gain[None], gathered, sent,
        init_state.reshape(width, STATE), local,
    )
    boundary = boundary.reshape(1, heads, HEADDIM, STATE)

    if not whole_group:
        piece = min(width, group_width)
        pieces = normed.reshape(rows, width // piece, piece)
        squares = jnp.sum(pieces * pieces, axis=2).T
        blocks = squares.reshape(squares.shape[0], head_count, block)
        ordered = jnp.take(blocks, slot, axis=1).reshape(squares.shape)
        own = (head_index * (width // piece) + jnp.arange(width // piece)) * piece // group_width
        member = (own[:, None] == jnp.arange(GROUPS)[None, :]).astype(f32)
        totals = lax.psum(jnp.dot(member.T, ordered, precision=highest), "head")
        sums = jnp.dot(member, totals, precision=highest)
        inverse = lax.rsqrt(sums / group_width + norm_eps)
        back = jnp.zeros_like(slot).at[slot].set(jnp.arange(head_count, dtype=slot.dtype))
        inverse = jnp.take(inverse.reshape(blocks.shape), back, axis=1).reshape(squares.shape).T
        normed = (
            (pieces * inverse[:, :, None]).reshape(rows, width) * norm_gain[None, :]
        ).astype(bf16)

    chips = seq_count // 2

    def around(value, by):
        if by % chips == 0:
            return value
        return lax.ppermute(
            value, "seq", [(i, (i + 2 * by) % seq_count) for i in range(seq_count)]
        )

    def across(value, bit):
        return lax.ppermute(
            value, "head", [(i, i ^ (1 << bit)) for i in range(head_count)]
        )

    def reduced(act, weight):
        half = rows // 2
        give = jnp.dot(act[half:], weight, preferred_element_type=f32).astype(bf16)
        keep = jnp.dot(act[:half], weight, preferred_element_type=f32)
        keep = keep + across(give, 0).astype(f32)
        for bit in range(1, bits):
            half = half // 2
            got = across(keep[half:].astype(bf16), bit)
            keep = keep[:half] + got.astype(f32)
        return keep.astype(bf16)

    core = seq_index % 2
    columns = out_weight.shape[1]
    layer_out = jnp.zeros((block, seq_count, columns), bf16)
    acts = [around(normed, by) for by in range(chips)]
    done = [[reduced(act, w) for w in (out_weight, other_core)] for act in acts]
    for by in range(chips):
        mine, other = [around(d, -by) for d in done[by]]
        chip = (seq_index // 2 + by) % chips
        layer_out = lax.dynamic_update_slice(
            layer_out, mine[:, None], (0, chip * 2 + core, 0)
        )
        layer_out = lax.dynamic_update_slice(
            layer_out, other[:, None], (0, chip * 2 + 1 - core, 0)
        )
    return (layer_out.reshape(block, seq_count * columns), boundary)


def solution(mesh):
    in_specs = (
        P("seq", "head"),
        P("seq", "head"),
        P("seq", None),
        P("head", "seq"),
        P("head"),
        P("head"),
        P(None, "head"),
        P("head"),
        P(),
        P(),
        P(None, "head"),
        P(),
        P("head", None, None),
        P("head"),
        P("head", "seq"),
    )
    out_specs = (P(("seq", "head"), None), P("seq", "head", None, None))
    return jax.shard_map(body, mesh=mesh, in_specs=in_specs, out_specs=out_specs, check_vma=False)
```

```python
import functools

import jax
import jax.numpy as jnp
from jax import lax
from jax.experimental import pallas as pl
from jax.experimental.pallas import tpu as pltpu
from jax.sharding import PartitionSpec as P

MIXER_HEADS = 256
HEADDIM = 64
STATE = 256
GROUPS = 8
KERNEL = 4
SPAN = 128
DINNER = 16384
EXTRA = 16
VMEM_LIMIT = 48 * 1024 * 1024
LAYER_LIMIT = 62 * 1024 * 1024

highest = lax.Precision.HIGHEST
norm_eps = 1e-05
f32 = jnp.float32
bf16 = jnp.bfloat16
MESH = pl.DeviceIdType.MESH


def silu(v):
    return v * (1.0 / (1.0 + jnp.exp(-v)))


def shifted(cur, prev8, by):
    moved = pltpu.roll(cur, by, 0)
    before = pltpu.roll(prev8, by, 0)
    row = lax.broadcasted_iota(jnp.int32, before.shape, 0)
    first = jnp.where(row < by, before, moved[:8])
    return jnp.concatenate([first, moved[8:]], axis=0)


def conv_block(in_ref, prev_ref, w_ref, b_ref, out_ref, chunk):
    width = in_ref.shape[1]
    rows = in_ref.shape[0]
    for c in range(0, width, chunk):
        cols = slice(c, c + chunk)
        cur = in_ref[:, cols].astype(f32)
        prev8 = prev_ref[:, cols]
        total = b_ref[:, cols] + w_ref[KERNEL - 1 : KERNEL, cols] * cur
        for by in range(1, KERNEL):
            k = KERNEL - 1 - by
            total = total + w_ref[k : k + 1, cols] * shifted(cur, prev8, by)
        prev_ref[:, cols] = cur[rows - 8 :]
        out_ref[:, cols] = silu(total).astype(bf16)


def spread_matrix(heads):
    h = lax.broadcasted_iota(jnp.int32, (heads, heads * HEADDIM), 0)
    c = lax.broadcasted_iota(jnp.int32, (heads, heads * HEADDIM), 1)
    return jnp.where(c // HEADDIM == h, 1.0, 0.0).astype(f32)


def spread(values, matrix):
    return jnp.dot(values, matrix, precision=highest, preferred_element_type=f32)


def softplus(v):
    e = jnp.exp(-jnp.abs(v))
    u = 1.0 + e
    series = e * (1.0 - e * (0.5 - e * (1.0 / 3.0 - 0.25 * e)))
    return jnp.maximum(v, 0.0) + jnp.where(e < 0.015625, series, jnp.log(u))


def transposed_dot(lhs, rhs):
    return lax.dot_general(
        lhs, rhs, (((1,), (1,)), ((), ())), precision=highest, preferred_element_type=f32
    )


def decay_terms(dt_ref, rate_ref):
    step = softplus(dt_ref[...])
    log = -jnp.exp(rate_ref[...]) * step
    t = lax.broadcasted_iota(jnp.int32, (SPAN, SPAN), 0)
    s = lax.broadcasted_iota(jnp.int32, (SPAN, SPAN), 1)
    lower = jnp.where(t >= s, 1.0, 0.0).astype(f32)
    eye = jnp.where(t == s, 1.0, 0.0).astype(f32)
    cumul_row = transposed_dot(log, lower)
    cumul_col = transposed_dot(lower, log)
    step_col = transposed_dot(eye, step)
    return step, step_col, cumul_row, cumul_col, t >= s


def state_kernel(
    g_ref, inner, bin_, cin, dt, rate, wx, bx, wb, wc, bb, bc, halo_x, halo_b, halo_c,
    x_out, b_out, c_out, enter_out, send_out, local_out,
    prev_x, prev_b, prev_c, state, total,
):
    i = pl.program_id(0)
    heads = dt.shape[0]

    @pl.when(i == 0)
    def _():
        prev_x[...] = halo_x[...].astype(f32)
        prev_b[...] = halo_b[...].astype(f32)
        prev_c[...] = halo_c[...].astype(f32)
        state[...] = jnp.zeros_like(state)
        total[...] = jnp.zeros_like(total)

    conv_block(inner, prev_x, wx, bx, x_out, 256)
    conv_block(bin_, prev_b, wb, bb, b_out, 256)
    conv_block(cin, prev_c, wc, bc, c_out, 256)
    step, step_col, cumul_row, cumul_col, causal = decay_terms(dt, rate)
    last = cumul_col[SPAN - 1 :]
    matrix = spread_matrix(heads)
    weights = spread(jnp.exp(last - cumul_col) * step_col, matrix)
    last8 = spread(jnp.broadcast_to(last, (8, heads)), matrix)
    enter_out[0] = state[...].astype(bf16)
    weighted = (x_out[...].astype(f32) * weights).astype(bf16)
    b_t = b_out[...].astype(f32).T.astype(bf16)
    written = jnp.dot(b_t, weighted, preferred_element_type=f32)
    state[...] = jnp.exp(last8[:1]) * state[...] + written
    total[...] += last8

    @pl.when(i == pl.num_programs(0) - 1)
    def _():
        local_out[...] = state[...]
        send_out[:STATE] = state[...].astype(bf16)
        tl = total[:1]
        high = tl.astype(bf16).astype(f32)
        row = lax.broadcasted_iota(jnp.int32, (EXTRA, tl.shape[1]), 0)
        send_out[STATE:] = jnp.where(row == 0, high, jnp.where(row == 1, tl - high, 0.0)).astype(bf16)


PARTS = 4


def chain_kernel(
    x, b, c, dt, rate, skip, enter, local, sent, y_out, prior_out,
    land, hop, send_sem, recv_sem,
):
    i = pl.program_id(0)
    seq = lax.axis_index("seq")
    last = 3
    wide = land.shape[2]

    def copy(k):
        return pltpu.make_async_remote_copy(
            src_ref=hop.at[k], dst_ref=land.at[k],
            send_sem=send_sem.at[k], recv_sem=recv_sem.at[k],
            device_id={"seq": (seq + 1) % 4}, device_id_type=MESH,
        )

    def joined(k):
        cols = slice(k * wide, (k + 1) * wide)
        own = sent[STATE : STATE + 1, cols].astype(f32) + sent[STATE + 1 : STATE + 2, cols].astype(f32)
        tail = land[k, STATE:].astype(f32)
        hop[k, :STATE] = (
            jnp.exp(own) * land[k, :STATE].astype(f32) + local[:, cols]
        ).astype(bf16)
        log = tail[0:1] + tail[1:2] + own
        high = log.astype(bf16).astype(f32)
        row = lax.broadcasted_iota(jnp.int32, (EXTRA, wide), 0)
        hop[k, STATE:] = jnp.where(row == 0, high, jnp.where(row == 1, log - high, 0.0)).astype(bf16)

    @pl.when(i == 0)
    def _():
        barrier = pltpu.get_barrier_semaphore()

        for by in (1, 3):
            pl.semaphore_signal(
                barrier, inc=1, device_id={"seq": (seq + by) % 4}, device_id_type=MESH
            )
        pl.semaphore_wait(barrier, 2)

        @pl.when(seq == 0)
        def _():
            for k in range(PARTS):
                hop[k] = sent[:, k * wide : (k + 1) * wide]
                copy(k).start()

        @pl.when(seq == 1)
        def _():
            for k in range(PARTS):
                copy(k).wait_recv()
                joined(k)
                copy(k).start()

    local_kernel(x, b, c, dt, rate, skip, enter, y_out)

    @pl.when(i == pl.num_programs(0) - 1)
    def _():
        @pl.when(seq == 2)
        def _():
            for k in range(PARTS):
                copy(k).wait_recv()
                joined(k)
                copy(k).start()

        @pl.when(seq == 3)
        def _():
            for k in range(PARTS):
                copy(k).wait_recv()

        @pl.when(seq > 0)
        def _():
            for k in range(PARTS):
                prior_out[:, k * wide : (k + 1) * wide] = land[k]

        @pl.when(seq == 0)
        def _():
            prior_out[...] = jnp.zeros_like(prior_out)

        @pl.when(seq < last)
        def _():
            for k in range(PARTS):
                copy(k).wait_send()


def local_kernel(x, b, c, dt, rate, skip, enter, y_out):
    heads = dt.shape[0]
    step, step_col, cumul_row, cumul_col, causal = decay_terms(dt, rate)
    matrix = spread_matrix(heads)
    scores = lax.dot_general(
        c[...], b[...], (((1,), (1,)), ((), ())), preferred_element_type=f32
    )
    row_term = jnp.log(step) - cumul_row
    growth = spread(jnp.exp(cumul_col), matrix)
    skip_row = spread(jnp.broadcast_to(skip[...], (8, heads)), matrix)[:1]
    lane = lax.broadcasted_iota(jnp.int32, (SPAN, 2 * HEADDIM), 1)
    zero = jnp.zeros((SPAN, 2 * HEADDIM), bf16)
    for pair in range(heads // 2):
        cols = slice(pair * 2 * HEADDIM, (pair + 1) * 2 * HEADDIM)
        mixers = []
        for h in (2 * pair, 2 * pair + 1):
            power = jnp.where(causal, cumul_col[:, h : h + 1] + row_term[h : h + 1], -1e30)
            mixers.append((scores * jnp.exp(power)).astype(bf16))
        xp = x[:, cols]
        both = jnp.concatenate(
            [jnp.where(lane < HEADDIM, xp, zero), jnp.where(lane >= HEADDIM, xp, zero)], axis=0
        )
        inside = jnp.dot(
            jnp.concatenate(mixers, axis=1), both, preferred_element_type=f32
        )
        carried = jnp.dot(c[...], enter[0, :, cols], preferred_element_type=f32)
        y_out[:, cols] = (
            inside + growth[:, cols] * carried + skip_row[:, cols] * xp.astype(f32)
        )


def output_kernel(
    meta, y, c, gate, dt, rate, gain, gathered, own_tail, init, local, normed_out, boundary_out,
    incoming, entering, mixed, offset, *, block, halves, whole_group, chained,
):
    i = pl.program_id(0)
    heads = dt.shape[0]
    width = y.shape[1]
    count = gathered.shape[0]

    @pl.when(i == 0)
    def _():
        place = meta[0]
        rate_sum = jnp.zeros((1, width), f32)
        incoming[...] = jnp.zeros_like(incoming)
        if chained:
            tail = gathered[0, STATE:].astype(f32)
            incoming[...] = gathered[0, :STATE].astype(f32)
            rate_sum = tail[0:1] + tail[1:2]
        for k in range(-1 if chained else count - 2, -1, -1):
            live = k < place
            tail = gathered[k, STATE:].astype(f32)
            factor = jnp.where(live, jnp.exp(rate_sum), 0.0)
            incoming[...] += factor * gathered[k, :STATE].astype(f32)
            rate_sum = rate_sum + jnp.where(live, tail[0:1] + tail[1:2], 0.0)
        tail = (own_tail[...] if chained else gathered[place, STATE:]).astype(f32)
        own = jnp.exp(tail[0:1] + tail[1:2])
        for k in range(0, width, 256):
            cols = slice(k, k + 256)
            value = incoming[:, cols] + jnp.exp(rate_sum[:, cols]) * init[cols, :].T
            entering[:, cols] = value.astype(bf16)
            boundary_out[cols, :] = (own[:, cols] * value + local[:, cols]).T
        offset[...] = jnp.zeros_like(offset)

    step, step_col, cumul_row, cumul_col, causal = decay_terms(dt, rate)
    cumul_col = cumul_col + offset[:1]
    offset[...] = jnp.broadcast_to(cumul_col[SPAN - 1 :], offset.shape)
    growth = spread(jnp.exp(cumul_col), spread_matrix(heads))
    squares = jnp.zeros((SPAN, 1), f32)
    for k in range(0, width, 256):
        cols = slice(k, k + 256)
        carried = jnp.dot(c[...], entering[:, cols], preferred_element_type=f32)
        value = (y[:, cols] + growth[:, cols] * carried) * silu(gate[:, cols].astype(f32))
        mixed[:, cols] = value
        squares = squares + jnp.sum(value * value, axis=1, keepdims=True)
    if whole_group:
        inverse = lax.rsqrt(squares / width + norm_eps)
    piece = block // halves
    for q in range(SPAN // piece):
        rows = slice(q * piece, (q + 1) * piece)
        first = meta[1 + i * (SPAN // block) + q // halves]
        first = first + (q % halves) * (normed_out.shape[0] // halves)
        value = mixed[rows, :]
        if whole_group:
            value = value * inverse[rows] * gain[...]
        normed_out[pl.ds(pl.multiple_of(first, piece), piece), :] = value.astype(normed_out.dtype)


def partner_of(place, bit):
    size = 1 << bit
    return place + (1 - 2 * ((place // size) % 2)) * size


HALVES = 2
GROUP = 4
QUARTERS = 4
MULTIPLY, FIRST, SECOND, THIRD, ARRIVED, LOADED = range(6)
FIRST_Z = (0, 3, 8, 12)
ORDER = (
    82, 6, 83, 3, 81, 1, 22, 80, 0, 2, 17, 4, 18, 16, 33, 64, 38, 9, 20, 32,
    8, 7, 34, 54, 11, 36, 5, 23, 25, 27, 39, 65, 15, 12, 24, 43, 14, 41, 21, 10,
    40, 52, 28, 31, 37, 30, 57, 13, 47, 26, 44, 49, 59, 56, 55, 42, 29, 46, 50, 58,
    63, 60, 19, 45, 53, 48, 62, 35, 61, 51,
)


def tanh_silu(v):
    half = 0.5 * v
    return half + half * jnp.tanh(half)


def two_terms(values):
    high = values.astype(bf16)
    low = (values - high.astype(f32)).astype(bf16)
    return jnp.concatenate([high, low], axis=1)


def fill_matrix(matrix):
    heads = matrix.shape[0] // 2
    h = lax.broadcasted_iota(jnp.int32, matrix.shape, 0) % heads
    c = lax.broadcasted_iota(jnp.int32, matrix.shape, 1) // HEADDIM
    matrix[...] = jnp.where(c == h, 1.0, 0.0).astype(bf16)


def token_decays(dt, rate):
    step = softplus(dt).T
    log = -jnp.exp(rate) * step
    t = lax.broadcasted_iota(jnp.int32, (SPAN, SPAN), 0)
    s = lax.broadcasted_iota(jnp.int32, (SPAN, SPAN), 1)
    lower = jnp.where(t >= s, 1.0, 0.0).astype(f32)
    cumul = [
        jnp.dot(lower, log[k : k + SPAN], precision=highest, preferred_element_type=f32)
        for k in range(0, log.shape[0], SPAN)
    ]
    return step, cumul, t >= s


def conv_tile(cur, prev8, weight, bias):
    total = bias + weight[KERNEL - 1 : KERNEL] * cur
    for by in range(1, KERNEL):
        k = KERNEL - 1 - by
        total = total + weight[k : k + 1] * shifted(cur, prev8, by)
    return tanh_silu(total).astype(bf16)


def layer_kernel(
    inner, gate_all, bc_all, dt, rate, skip, wx, bx, wbc, bbc, tail_x, tail_bc, init_all, gain, w_own,
    out, state_out,
    x, gate, bc, init, halo_x, halo_bc, prev, b_t, weight, factors, matrix, scaled, total, state,
    land, hop, left, squares,
    w, acts, keep, y_send, y_recv, a_send, a_recv, b_send, b_recv, x_send, x_recv,
    in_sem, load_sem, halo_send, halo_recv, hop_send, hop_recv, w_sem, w_send, w_recv,
    act_send_sem, act_recv_sem, send_sem, recv_sem, x_send_sem, x_recv_sem,
):
    seq = lax.axis_index("seq")
    head = lax.axis_index("head")
    rows, width = x.shape
    heads = dt.shape[0]
    spans = rows // SPAN
    strip = width // QUARTERS
    wide = w.shape[2]
    per = w_own.shape[1] // wide
    count = keep.shape[0]
    part = count // 2
    piece = out.shape[0] // HALVES
    half_rows = acts.shape[2]
    other_chip = (seq + 2) % 4
    near = [partner_of(head, bit) for bit in range(3)]
    across = [{"head": place} for place in near]
    over_x = {"seq": other_chip}
    after = {"seq": (seq + 1) % 4}
    other_core = {"seq": partner_of(seq, 0)}
    firsts = [pl.multiple_of((head + g) * STATE, STATE) for g in (0, GROUPS)]
    chunk = 256

    def remote(source, dest, send, recv, target):
        return pltpu.make_async_remote_copy(
            src_ref=source, dst_ref=dest, send_sem=send, recv_sem=recv,
            device_id=target, device_id_type=MESH,
        )

    def strip_of(k):
        return pl.ds(pl.multiple_of(k * strip, strip), strip)

    def inner_copy(k):
        cols = slice(k * strip, (k + 1) * strip)
        return pltpu.make_async_copy(inner.at[:, cols], x.at[:, cols], in_sem.at[k])

    def bc_copy(k):
        return pltpu.make_async_copy(
            bc_all.at[:, pl.ds(firsts[k], STATE)], bc.at[k], load_sem.at[k]
        )

    def gate_copy():
        return pltpu.make_async_copy(gate_all, gate, load_sem.at[2])

    def init_copy():
        return pltpu.make_async_copy(init_all, init, load_sem.at[3])

    def state_copy():
        return pltpu.make_async_copy(state, state_out, load_sem.at[4])

    def own_weights(k):
        cols = pl.ds(pl.multiple_of(k * wide, wide), wide)
        return pltpu.make_async_copy(w_own.at[:, cols], w.at[k], w_sem.at[k])

    def other_weights(k):
        narrow = wide // 2
        place = pl.ds(pl.multiple_of(k % 2 * narrow, narrow), narrow)
        return remote(
            w.at[k // 2, :, place], w.at[per + k // 2, :, place], w_send.at[k], w_recv.at[k],
            other_core,
        )

    def halo_copies():
        last = pl.ds(rows - 16, 16)
        pairs = [(inner.at[last], halo_x)] + [
            (bc_all.at[last, pl.ds(firsts[k], STATE)], halo_bc.at[k]) for k in range(2)
        ]
        return [
            remote(source, dest, halo_send.at[k], halo_recv.at[k], after)
            for k, (source, dest) in enumerate(pairs)
        ]

    def hop_copy(k):
        return remote(hop.at[k], land.at[k], hop_send.at[k], hop_recv.at[k], after)

    def act_copy(half):
        return remote(
            acts.at[0, half], acts.at[1, half], act_send_sem.at[half], act_recv_sem.at[half], over_x
        )

    def chip_copy(k):
        return remote(x_send.at[k], x_recv.at[k], x_send_sem.at[k], x_recv_sem.at[k], over_x)

    def turned(t):
        value = 0
        for k in FIRST_Z:
            value = value + jnp.where(t == k, 1, 0)
        return value

    def head_copy(stage, t):
        source, dest = ((y_send, y_recv), (a_send, a_recv), (b_send, b_recv))[stage]
        target = across[2]
        if stage < 2:
            target = {"head": near[stage] + turned(t) * (near[1 - stage] - near[stage])}
        return remote(
            source.at[t], dest.at[t], send_sem.at[stage, t], recv_sem.at[stage, t], target
        )

    for k in range(2):
        bc_copy(k).start()
    for k in range(QUARTERS):
        inner_copy(k).start()

    barrier = pltpu.get_barrier_semaphore()
    greeted = across + [over_x, after, {"seq": (seq + 3) % 4}]
    for target in greeted:
        pl.semaphore_signal(barrier, inc=1, device_id=target, device_id_type=MESH)

    for k in range(per):
        own_weights(k).start()
    init_copy().start()
    gate_copy().start()

    fill_matrix(matrix)
    step, cumul, causal = token_decays(dt[...], rate[...])
    ends = [value[SPAN - 1 :] for value in cumul]
    later = jnp.zeros_like(ends[0])
    for k in range(spans - 1, -1, -1):
        span = slice(k * SPAN, (k + 1) * SPAN)
        later = later + ends[k]
        weight[span] = two_terms(jnp.exp(later - cumul[k]) * step[span])
    row = lax.broadcasted_iota(jnp.int32, (16, heads), 0)
    high = later.astype(bf16).astype(f32)
    total[...] = two_terms(jnp.where(row < 8, high, later - high))

    pl.semaphore_wait(barrier, len(greeted))

    @pl.when(seq < 3)
    def _():
        for copy in halo_copies():
            copy.start()

    def conv_rows(source, k, cols, before, kernel, bias):
        span = slice(k * SPAN, (k + 1) * SPAN)
        if k:
            before = source[k * SPAN - 16 : k * SPAN, cols].astype(f32)[8:]
        value = conv_tile(source[span, cols].astype(f32), before, kernel, bias)
        source[span, cols] = value
        return value

    def conv_bc(g, k):
        at = pl.ds(firsts[g], STATE)
        before = None if k else prev[:, strip + g * STATE : strip + (g + 1) * STATE]
        return conv_rows(bc.at[g], k, slice(0, STATE), before, wbc[:, at], bbc[:, at])

    def conv_b(k):
        value = conv_bc(0, k)
        b_t[:, k * SPAN : (k + 1) * SPAN] = value.astype(f32).T.astype(bf16)

    for k in range(2):
        bc_copy(k).wait()
    for k in range(spans - 1, 0, -1):
        conv_b(k)

    @pl.when(seq > 0)
    def _():
        for copy in halo_copies():
            copy.wait_recv()
        for g in range(2):
            prev[:, strip + g * STATE : strip + (g + 1) * STATE] = halo_bc[g].astype(f32)[8:]

    @pl.when(seq == 0)
    def _():
        for g in range(2):
            prev[8 - KERNEL + 1 :, strip + g * STATE : strip + (g + 1) * STATE] = tail_bc[
                :, pl.ds(firsts[g], STATE)
            ].astype(f32)
        land[...] = jnp.zeros_like(land)

    conv_b(0)

    def totals(k):
        spread_log = jnp.dot(total[...], matrix[:, strip_of(k)], preferred_element_type=f32)
        return spread_log[0:1] + spread_log[8:9]

    def fill_hop(k, value, log):
        hop[k, :STATE] = value.astype(bf16)
        top = log.astype(bf16).astype(f32)
        line = lax.broadcasted_iota(jnp.int32, (EXTRA, strip), 0)
        hop[k, STATE:] = jnp.where(line == 0, top, jnp.where(line == 1, log - top, 0.0)).astype(bf16)
        hop_copy(k).start()

    def pass_on(k):
        hop_copy(k).wait_recv()
        own = totals(k)
        tail = land[k, STATE:].astype(f32)
        fill_hop(
            k,
            jnp.exp(own) * land[k, :STATE].astype(f32) + state[:, strip_of(k)],
            tail[0:1] + tail[1:2] + own,
        )

    for k in range(QUARTERS):
        inner_copy(k).wait()

    def quarter(q, carry):
        @pl.when(seq > 0)
        def _():
            prev[:, :strip] = halo_x[:, strip_of(q)].astype(f32)[8:]

        @pl.when(seq == 0)
        def _():
            prev[8 - KERNEL + 1 :, :strip] = tail_x[:, strip_of(q)].astype(f32)

        for k in range(spans - 1, -1, -1):
            span = slice(k * SPAN, (k + 1) * SPAN)
            for c in range(0, strip, chunk):
                at = pl.ds(pl.multiple_of(q * strip + c, chunk), chunk)
                value = conv_rows(x, k, at, prev[:, c : c + chunk], wx[:, at], bx[:, at])
                factor = jnp.dot(weight[span], matrix[:, at], preferred_element_type=f32)
                scaled[span, c : c + chunk] = (value.astype(f32) * factor).astype(bf16)
        state[:, strip_of(q)] = jnp.dot(b_t[...], scaled[...], preferred_element_type=f32)

        @pl.when(seq == 0)
        def _():
            fill_hop(q, state[:, strip_of(q)], totals(q))

        @pl.when((seq == 1) & (q > 0))
        def _():
            pass_on(q - 1)

        @pl.when(q % 2 == 0)
        def _():
            own_weights(q // 2).wait()

        other_weights(q).start()
        return carry

    lax.fori_loop(0, QUARTERS, quarter, 0)

    @pl.when(seq == 1)
    def _():
        pass_on(QUARTERS - 1)

    for k in range(spans - 1, -1, -1):
        conv_bc(1, k)

    for k in range(spans):
        middle = 0.5 * ends[k]
        factors[k] = two_terms(
            jnp.concatenate(
                [
                    jnp.exp(cumul[k] - middle),
                    jnp.exp(middle - cumul[k]) * step[k * SPAN : (k + 1) * SPAN],
                    jnp.broadcast_to(jnp.exp(middle), (8, heads)),
                    jnp.broadcast_to(skip[...], (8, heads)),
                ],
                axis=0,
            )
        )

    for i in range(spans):
        span = slice(i * SPAN, (i + 1) * SPAN)
        scores = lax.dot_general(
            bc[1, span], bc[0, span], (((1,), (1,)), ((), ())), preferred_element_type=f32
        )
        left[i, :, :SPAN] = jnp.where(causal, scores, 0.0).astype(bf16)
        left[i, :, SPAN:] = bc[1, span]
    squares[...] = jnp.zeros_like(squares)
    init_copy().wait()
    gate_copy().wait()

    def gated(q, carry):
        @pl.when(seq == 2)
        def _():
            pass_on(q)

        @pl.when(seq == 3)
        def _():
            hop_copy(q).wait_recv()

        tail = land[q, STATE:].astype(f32)
        factor = jnp.exp(tail[0:1] + tail[1:2])
        for c in range(0, strip, chunk):
            at = pl.ds(pl.multiple_of(q * strip + c, chunk), chunk)
            state[:, at] = (
                land[q, :STATE, c : c + chunk].astype(f32) + factor[:, c : c + chunk] * init[at, :].T
            )
        cols = strip_of(q)
        spot = pl.ds(pl.multiple_of(q % 2 * strip, strip), strip)
        for i in range(spans):
            span = slice(i * SPAN, (i + 1) * SPAN)
            spread_all = jnp.dot(factors[i], matrix[:, cols], preferred_element_type=f32)
            half_decay = spread_all[2 * SPAN : 2 * SPAN + 1]
            value = x[span, cols].astype(f32)
            weighted = (value * spread_all[SPAN : 2 * SPAN]).astype(bf16)
            before = half_decay * state[:, cols]
            inside = jnp.dot(
                left[i], jnp.concatenate([weighted, before.astype(bf16)], axis=0),
                preferred_element_type=f32,
            )
            written = jnp.dot(b_t[:, span], weighted, preferred_element_type=f32)
            state[:, cols] = half_decay * (before + written)
            value = spread_all[:SPAN] * inside + spread_all[2 * SPAN + 8 : 2 * SPAN + 9] * value
            value = value * tanh_silu(gate[span, cols].astype(f32))
            keep[part + 2 * i + q // 2, :, spot] = value
            square = value * value
            for c in range(0, strip, 128):
                squares[i] = squares[i] + square[:, c : c + 128]
        return carry

    lax.fori_loop(0, QUARTERS, gated, 0)

    def normalized(half):
        block = HALVES * piece
        for i in range(spans):
            for p in range(SPAN // block):
                first = p * block + half * piece
                lines = slice(first, first + piece)
                inverse = lax.rsqrt(
                    jnp.sum(squares[i, lines], axis=1, keepdims=True) / width + norm_eps
                )
                owner = i * (SPAN // block) + p
                slot = 0
                for bit in range(3):
                    differs = (owner // (1 << bit) + head // (1 << bit)) % 2
                    slot = slot + differs * (4 >> bit)
                place = pl.ds(pl.multiple_of(slot * piece, piece), piece)
                for c in range(width // wide):
                    cols = slice(c * wide, (c + 1) * wide)
                    acts[0, half, place, cols] = (
                        keep[part + 2 * i + c, lines, :] * inverse * gain[:, cols]
                    ).astype(bf16)

    for half in range(HALVES):
        normalized(half)
        act_copy(half).start()
    state_copy().start()

    def multiply(t):
        place, half, group = t // part, (t % part) // GROUP, t % GROUP
        product = jnp.dot(acts[place, half], w[group], preferred_element_type=f32)
        near_z = turned(t) == 1
        two = 2 * piece
        middle = [product[two : 2 * two], product[2 * two : 3 * two]]
        y_send[t, :two] = jnp.where(near_z, middle[0], middle[1]).astype(bf16)
        y_send[t, two:] = product[3 * two :].astype(bf16)
        head_copy(0, t).start()
        keep[t, :two] = product[:two]
        keep[t, two:] = jnp.where(near_z, middle[1], middle[0])

    def first_stage(t):
        head_copy(0, t).wait_recv()
        a_send[t] = (keep[t, 2 * piece :] + y_recv[t, 2 * piece :].astype(f32)).astype(bf16)
        head_copy(1, t).start()
        keep[t, : 2 * piece] = keep[t, : 2 * piece] + y_recv[t, : 2 * piece].astype(f32)

    def second_stage(t):
        head_copy(1, t).wait_recv()
        b_send[t] = (keep[t, piece : 2 * piece] + a_recv[t, piece:].astype(f32)).astype(bf16)
        head_copy(2, t).start()
        keep[t, :piece] = keep[t, :piece] + a_recv[t, :piece].astype(f32)

    def place_out(t, home, value):
        group = t % GROUP
        core = (home % 2 + group // per) % 2
        column = ((home // 2) * 2 + core) * (per * wide) + (group % per) * wide
        first = ((t % part) // GROUP) * piece
        out[
            pl.ds(pl.multiple_of(first, piece), piece), pl.ds(pl.multiple_of(column, wide), wide)
        ] = value

    def third_stage(t):
        head_copy(2, t).wait_recv()
        value = (keep[t, :piece] + b_recv[t].astype(f32)).astype(bf16)

        @pl.when(t < part)
        def _():
            place_out(t, seq, value)

        @pl.when(t >= part)
        def _():
            x_send[t - part] = value
            chip_copy(t - part).start()

    def event(i, carry):
        code = 0
        for k, value in enumerate(ORDER):
            code = code + jnp.where(i == k, value, 0)
        kind, t = code // 16, code % 16

        @pl.when(kind == MULTIPLY)
        def _():
            multiply(t)

        @pl.when(kind == FIRST)
        def _():
            first_stage(t)

        @pl.when(kind == SECOND)
        def _():
            second_stage(t)

        @pl.when(kind == THIRD)
        def _():
            third_stage(t)

        @pl.when(kind == ARRIVED)
        def _():
            act_copy(t).wait_recv()

        @pl.when((kind == LOADED) & (t >= per))
        def _():
            for k in range(2):
                other_weights(2 * (t - per) + k).wait_recv()

        return carry

    lax.fori_loop(0, len(ORDER), event, 0)

    def collect(k, carry):
        chip_copy(k).wait_recv()
        place_out(k, other_chip, x_recv[k])
        chip_copy(k).wait_send()
        return carry

    def drain(t, carry):
        for stage in range(3):
            head_copy(stage, t).wait_send()
        return carry

    lax.fori_loop(0, part, collect, 0)
    for half in range(HALVES):
        act_copy(half).wait_send()
    for k in range(QUARTERS):
        other_weights(k).wait_send()
    state_copy().wait()

    @pl.when(seq < 3)
    def _():
        for k in range(QUARTERS):
            hop_copy(k).wait_send()
        for copy in halo_copies():
            copy.wait_send()

    lax.fori_loop(0, count, drain, 0)


def finish_kernel(summed, state, out, boundary_out):
    out[...] = summed[...]
    boundary_out[...] = state[...].T


def layer(inner, gate, bc, dt, rate, skip, wx, bx, wbc, bbc, tail_x, tail_bc, init, gain, own):
    rows, width = inner.shape
    heads = dt.shape[0]
    columns = own.shape[1]
    strip = width // QUARTERS
    block = rows // 8
    piece = block // HALVES
    wide = 2 * columns // GROUP
    part = HALVES * GROUP
    count = 2 * part
    spans = rows // SPAN
    anywhere = pl.BlockSpec(memory_space=pl.ANY)
    vmem = pl.BlockSpec(memory_space=pltpu.VMEM)
    slots = (QUARTERS, STATE + EXTRA, strip)
    dma = pltpu.SemaphoreType.DMA
    summed, state = pl.pallas_call(
        layer_kernel,
        in_specs=[anywhere] * 3 + [vmem] * 9 + [anywhere, vmem, anywhere],
        out_specs=[vmem, anywhere],
        out_shape=[
            jax.ShapeDtypeStruct((block, 4 * columns), bf16),
            jax.ShapeDtypeStruct((STATE, width), f32),
        ],
        scratch_shapes=[
            pltpu.VMEM((rows, width), bf16),
            pltpu.VMEM((rows, width), bf16),
            pltpu.VMEM((2, rows, STATE), bf16),
            pltpu.VMEM((width, STATE), f32),
            pltpu.VMEM((16, width), bf16),
            pltpu.VMEM((2, 16, STATE), bf16),
            pltpu.VMEM((8, strip + 2 * STATE), f32),
            pltpu.VMEM((STATE, rows), bf16),
            pltpu.VMEM((rows, 2 * heads), bf16),
            pltpu.VMEM((spans, 2 * SPAN + 16, 2 * heads), bf16),
            pltpu.VMEM((2 * heads, width), bf16),
            pltpu.VMEM((rows, strip), bf16),
            pltpu.VMEM((16, 2 * heads), bf16),
            pltpu.VMEM((STATE, width), f32),
            pltpu.VMEM(slots, bf16),
            pltpu.VMEM(slots, bf16),
            pltpu.VMEM((spans, SPAN, SPAN + STATE), bf16),
            pltpu.VMEM((spans, SPAN, 128), f32),
            pltpu.VMEM((GROUP, width, wide), bf16),
            pltpu.VMEM((2, HALVES, rows // HALVES, width), bf16),
            pltpu.VMEM((count, 4 * piece, wide), f32),
            pltpu.VMEM((count, 4 * piece, wide), bf16),
            pltpu.VMEM((count, 4 * piece, wide), bf16),
            pltpu.VMEM((count, 2 * piece, wide), bf16),
            pltpu.VMEM((count, 2 * piece, wide), bf16),
            pltpu.VMEM((count, piece, wide), bf16),
            pltpu.VMEM((count, piece, wide), bf16),
            pltpu.VMEM((part, piece, wide), bf16),
            pltpu.VMEM((part, piece, wide), bf16),
            dma((QUARTERS,)),
            dma((5,)),
            dma((3,)),
            dma((3,)),
            dma((QUARTERS,)),
            dma((QUARTERS,)),
            dma((GROUP // 2,)),
            dma((QUARTERS,)),
            dma((QUARTERS,)),
            dma((HALVES,)),
            dma((HALVES,)),
            dma((3, count)),
            dma((3, count)),
            dma((part,)),
            dma((part,)),
        ],
        compiler_params=pltpu.CompilerParams(
            vmem_limit_bytes=LAYER_LIMIT, collective_id=0, has_side_effects=True
        ),
        name="layer",
    )(
        inner, gate, bc, dt, rate[None], skip[None], wx, bx[None], wbc, bbc[None], tail_x, tail_bc,
        init.reshape(width, STATE), gain[None], own,
    )
    steps = 4
    return pl.pallas_call(
        finish_kernel,
        grid=(steps,),
        in_specs=[
            pl.BlockSpec((block, columns), lambda i: (0, i)),
            pl.BlockSpec((STATE, width // steps), lambda i: (0, i)),
        ],
        out_specs=[
            pl.BlockSpec((block, columns), lambda i: (0, i)),
            pl.BlockSpec((width // steps, STATE), lambda i: (i, 0)),
        ],
        out_shape=[
            jax.ShapeDtypeStruct((block, 4 * columns), bf16),
            jax.ShapeDtypeStruct((width, STATE), f32),
        ],
        compiler_params=pltpu.CompilerParams(vmem_limit_bytes=LAYER_LIMIT),
        name="finish",
    )(summed, state)


def params():
    return pltpu.CompilerParams(vmem_limit_bytes=VMEM_LIMIT)


def body(
    inner_input,
    gate_input,
    bc_input,
    dt_input,
    log_rate,
    skip_weight,
    conv_weight_x,
    conv_bias_x,
    conv_weight_bc,
    conv_bias_bc,
    conv_tail_x,
    conv_tail_bc,
    init_state,
    norm_gain,
    out_weight,
):
    seq_count = lax.axis_size("seq")
    head_count = lax.axis_size("head")
    seq_index = lax.axis_index("seq")
    head_index = lax.axis_index("head")
    rows, width = inner_input.shape
    heads = dt_input.shape[0]
    per_group = MIXER_HEADS // GROUPS
    group = (head_index * heads // per_group).astype(jnp.int32)
    spans = rows // SPAN
    block = rows // head_count
    group_width = DINNER // GROUPS
    whole_group = width == group_width

    projected = (
        seq_count == 4 and head_count == 8 and whole_group and rows == 512 and width == 2048
        and out_weight.shape[1] % 512 == 0
    )
    if projected:
        out, boundary = layer(
            inner_input, gate_input, bc_input, dt_input, log_rate, skip_weight, conv_weight_x,
            conv_bias_x, conv_weight_bc, conv_bias_bc, conv_tail_x, conv_tail_bc, init_state,
            norm_gain, out_weight,
        )
        return (out, boundary.reshape(1, heads, HEADDIM, STATE))

    other_core = lax.ppermute(out_weight, "seq", [(i, i ^ 1) for i in range(seq_count)])

    def pair_columns(table, axis):
        return [
            lax.dynamic_slice_in_dim(table, (g + group) * STATE, STATE, axis) for g in (0, GROUPS)
        ]

    tail_rows = rows - KERNEL + 1
    last_rows = jnp.concatenate(
        [inner_input[tail_rows:]] + pair_columns(bc_input[tail_rows:], 1), axis=1
    )
    arrived = lax.ppermute(last_rows, "seq", [(i, i + 1) for i in range(seq_count - 1)])
    first_rows = jnp.concatenate([conv_tail_x] + pair_columns(conv_tail_bc, 1), axis=1)
    halo = jnp.where(seq_index == 0, first_rows, arrived)
    halo = jnp.pad(halo, ((8 - KERNEL + 1, 0), (0, 0)))
    rate = log_rate[:, None]

    def const(shape, *index):
        return pl.BlockSpec(shape, lambda i, *_: index)

    span_x = pl.BlockSpec((SPAN, width), lambda i, *_: (i, 0))
    span_bc = pl.BlockSpec((SPAN, STATE), lambda i, *_: (i, 0))
    span_dt = pl.BlockSpec((heads, SPAN), lambda i, *_: (0, i))

    conv_x, conv_b, conv_c, enter, sent, local = pl.pallas_call(
        state_kernel,
        grid_spec=pltpu.PrefetchScalarGridSpec(
            num_scalar_prefetch=1,
            grid=(spans,),
            in_specs=[
                span_x,
                pl.BlockSpec((SPAN, STATE), lambda i, g: (i, g[0])),
                pl.BlockSpec((SPAN, STATE), lambda i, g: (i, g[0] + GROUPS)),
                span_dt,
                const((heads, 1), 0, 0),
                const((KERNEL, width), 0, 0),
                const((1, width), 0, 0),
                pl.BlockSpec((KERNEL, STATE), lambda i, g: (0, g[0])),
                pl.BlockSpec((KERNEL, STATE), lambda i, g: (0, g[0] + GROUPS)),
                pl.BlockSpec((1, STATE), lambda i, g: (0, g[0])),
                pl.BlockSpec((1, STATE), lambda i, g: (0, g[0] + GROUPS)),
                const((8, width), 0, 0),
                const((8, STATE), 0, width // STATE),
                const((8, STATE), 0, width // STATE + 1),
            ],
            out_specs=[
                span_x,
                span_bc,
                span_bc,
                pl.BlockSpec((1, STATE, width), lambda i, *_: (i, 0, 0)),
                const((STATE + EXTRA, width), 0, 0),
                const((STATE, width), 0, 0),
            ],
            scratch_shapes=[
                pltpu.VMEM((8, width), f32),
                pltpu.VMEM((8, STATE), f32),
                pltpu.VMEM((8, STATE), f32),
                pltpu.VMEM((STATE, width), f32),
                pltpu.VMEM((8, width), f32),
            ],
        ),
        out_shape=[
            jax.ShapeDtypeStruct((rows, width), bf16),
            jax.ShapeDtypeStruct((rows, STATE), bf16),
            jax.ShapeDtypeStruct((rows, STATE), bf16),
            jax.ShapeDtypeStruct((spans, STATE, width), bf16),
            jax.ShapeDtypeStruct((STATE + EXTRA, width), bf16),
            jax.ShapeDtypeStruct((STATE, width), f32),
        ],
        compiler_params=params(),
        name="conv_and_states",
    )(
        group[None],
        inner_input, bc_input, bc_input, dt_input, rate,
        conv_weight_x, conv_bias_x[None], conv_weight_bc, conv_weight_bc,
        conv_bias_bc[None], conv_bias_bc[None], halo, halo, halo,
    )

    chained = seq_count == 4 and width % (PARTS * 128) == 0
    local_specs = [
        span_x,
        span_bc,
        span_bc,
        span_dt,
        const((heads, 1), 0, 0),
        const((1, heads), 0, 0),
        pl.BlockSpec((1, STATE, width), lambda i: (i, 0, 0)),
    ]
    local_args = (conv_x, conv_b, conv_c, dt_input, rate, skip_weight[None], enter)
    y_shape = jax.ShapeDtypeStruct((rows, width), f32)
    if chained:
        slots = (PARTS, STATE + EXTRA, width // PARTS)
        y_local, prior = pl.pallas_call(
            chain_kernel,
            grid=(spans,),
            in_specs=local_specs
            + [const((STATE, width), 0, 0), const((STATE + EXTRA, width), 0, 0)],
            out_specs=[span_x, const((STATE + EXTRA, width), 0, 0)],
            out_shape=[y_shape, jax.ShapeDtypeStruct((STATE + EXTRA, width), bf16)],
            scratch_shapes=[
                pltpu.VMEM(slots, bf16),
                pltpu.VMEM(slots, bf16),
                pltpu.SemaphoreType.DMA((PARTS,)),
                pltpu.SemaphoreType.DMA((PARTS,)),
            ],
            compiler_params=pltpu.CompilerParams(
                vmem_limit_bytes=VMEM_LIMIT, collective_id=1, has_side_effects=True
            ),
            name="local_outputs_and_chain",
        )(*local_args, local, sent)
        gathered = prior[None]
    else:
        gathered = lax.all_gather(sent, "seq")
        y_local = pl.pallas_call(
            local_kernel,
            grid=(spans,),
            in_specs=local_specs,
            out_specs=span_x,
            out_shape=y_shape,
            compiler_params=params(),
            name="local_outputs",
        )(*local_args)

    bits = head_count.bit_length() - 1
    distance = jnp.arange(head_count, dtype=jnp.int32) ^ head_index
    slot = jnp.zeros_like(distance)
    for bit in range(bits):
        slot = slot + ((distance >> bit) & 1) * (head_count >> (bit + 1))
    meta = jnp.concatenate([seq_index[None].astype(jnp.int32), slot.astype(jnp.int32) * block])

    normed, boundary = pl.pallas_call(
        functools.partial(
            output_kernel, block=block, halves=1, whole_group=whole_group, chained=chained
        ),
        grid_spec=pltpu.PrefetchScalarGridSpec(
            num_scalar_prefetch=1,
            grid=(spans,),
            in_specs=[
                span_x,
                span_bc,
                span_x,
                span_dt,
                const((heads, 1), 0, 0),
                const((1, width), 0, 0),
                const((gathered.shape[0], STATE + EXTRA, width), 0, 0, 0),
                const((EXTRA, width), STATE // EXTRA, 0),
                const((width, STATE), 0, 0),
                const((STATE, width), 0, 0),
            ],
            out_specs=[const((rows, width), 0, 0), const((width, STATE), 0, 0)],
            scratch_shapes=[
                pltpu.VMEM((STATE, width), f32),
                pltpu.VMEM((STATE, width), bf16),
                pltpu.VMEM((SPAN, width), f32),
                pltpu.VMEM((8, heads), f32),
            ],
        ),
        out_shape=[
            jax.ShapeDtypeStruct((rows, width), bf16 if whole_group else f32),
            jax.ShapeDtypeStruct((width, STATE), f32),
        ],
        compiler_params=params(),
        name="gated_outputs",
    )(
        meta,
        y_local, conv_c, gate_input, dt_input, rate, norm_gain[None], gathered, sent,
        init_state.reshape(width, STATE), local,
    )
    boundary = boundary.reshape(1, heads, HEADDIM, STATE)

    if not whole_group:
        piece = min(width, group_width)
        pieces = normed.reshape(rows, width // piece, piece)
        squares = jnp.sum(pieces * pieces, axis=2).T
        blocks = squares.reshape(squares.shape[0], head_count, block)
        ordered = jnp.take(blocks, slot, axis=1).reshape(squares.shape)
        own = (head_index * (width // piece) + jnp.arange(width // piece)) * piece // group_width
        member = (own[:, None] == jnp.arange(GROUPS)[None, :]).astype(f32)
        totals = lax.psum(jnp.dot(member.T, ordered, precision=highest), "head")
        sums = jnp.dot(member, totals, precision=highest)
        inverse = lax.rsqrt(sums / group_width + norm_eps)
        back = jnp.zeros_like(slot).at[slot].set(jnp.arange(head_count, dtype=slot.dtype))
        inverse = jnp.take(inverse.reshape(blocks.shape), back, axis=1).reshape(squares.shape).T
        normed = (
            (pieces * inverse[:, :, None]).reshape(rows, width) * norm_gain[None, :]
        ).astype(bf16)

    chips = seq_count // 2

    def around(value, by):
        if by % chips == 0:
            return value
        return lax.ppermute(
            value, "seq", [(i, (i + 2 * by) % seq_count) for i in range(seq_count)]
        )

    def across(value, bit):
        return lax.ppermute(
            value, "head", [(i, i ^ (1 << bit)) for i in range(head_count)]
        )

    def reduced(act, weight):
        half = rows // 2
        give = jnp.dot(act[half:], weight, preferred_element_type=f32).astype(bf16)
        keep = jnp.dot(act[:half], weight, preferred_element_type=f32)
        keep = keep + across(give, 0).astype(f32)
        for bit in range(1, bits):
            half = half // 2
            got = across(keep[half:].astype(bf16), bit)
            keep = keep[:half] + got.astype(f32)
        return keep.astype(bf16)

    core = seq_index % 2
    columns = out_weight.shape[1]
    layer_out = jnp.zeros((block, seq_count, columns), bf16)
    acts = [around(normed, by) for by in range(chips)]
    done = [[reduced(act, w) for w in (out_weight, other_core)] for act in acts]
    for by in range(chips):
        mine, other = [around(d, -by) for d in done[by]]
        chip = (seq_index // 2 + by) % chips
        layer_out = lax.dynamic_update_slice(
            layer_out, mine[:, None], (0, chip * 2 + core, 0)
        )
        layer_out = lax.dynamic_update_slice(
            layer_out, other[:, None], (0, chip * 2 + 1 - core, 0)
        )
    return (layer_out.reshape(block, seq_count * columns), boundary)


def solution(mesh):
    in_specs = (
        P("seq", "head"),
        P("seq", "head"),
        P("seq", None),
        P("head", "seq"),
        P("head"),
        P("head"),
        P(None, "head"),
        P("head"),
        P(),
        P(),
        P(None, "head"),
        P(),
        P("head", None, None),
        P("head"),
        P("head", "seq"),
    )
    out_specs = (P(("seq", "head"), None), P("seq", "head", None, None))
    return jax.shard_map(body, mesh=mesh, in_specs=in_specs, out_specs=out_specs, check_vma=False)
```

```python
import functools

import jax
import jax.numpy as jnp
from jax import lax
from jax.experimental import pallas as pl
from jax.experimental.pallas import tpu as pltpu
from jax.sharding import PartitionSpec as P

MIXER_HEADS = 256
HEADDIM = 64
STATE = 256
GROUPS = 8
KERNEL = 4
SPAN = 128
DINNER = 16384
EXTRA = 16
VMEM_LIMIT = 48 * 1024 * 1024
LAYER_LIMIT = 62 * 1024 * 1024

highest = lax.Precision.HIGHEST
norm_eps = 1e-05
f32 = jnp.float32
bf16 = jnp.bfloat16
MESH = pl.DeviceIdType.MESH


def silu(v):
    return v * (1.0 / (1.0 + jnp.exp(-v)))


def shifted(cur, prev8, by):
    moved = pltpu.roll(cur, by, 0)
    before = pltpu.roll(prev8, by, 0)
    row = lax.broadcasted_iota(jnp.int32, before.shape, 0)
    first = jnp.where(row < by, before, moved[:8])
    return jnp.concatenate([first, moved[8:]], axis=0)


def conv_block(in_ref, prev_ref, w_ref, b_ref, out_ref, chunk):
    width = in_ref.shape[1]
    rows = in_ref.shape[0]
    for c in range(0, width, chunk):
        cols = slice(c, c + chunk)
        cur = in_ref[:, cols].astype(f32)
        prev8 = prev_ref[:, cols]
        total = b_ref[:, cols] + w_ref[KERNEL - 1 : KERNEL, cols] * cur
        for by in range(1, KERNEL):
            k = KERNEL - 1 - by
            total = total + w_ref[k : k + 1, cols] * shifted(cur, prev8, by)
        prev_ref[:, cols] = cur[rows - 8 :]
        out_ref[:, cols] = silu(total).astype(bf16)


def spread_matrix(heads):
    h = lax.broadcasted_iota(jnp.int32, (heads, heads * HEADDIM), 0)
    c = lax.broadcasted_iota(jnp.int32, (heads, heads * HEADDIM), 1)
    return jnp.where(c // HEADDIM == h, 1.0, 0.0).astype(f32)


def spread(values, matrix):
    return jnp.dot(values, matrix, precision=highest, preferred_element_type=f32)


def softplus(v):
    e = jnp.exp(-jnp.abs(v))
    u = 1.0 + e
    series = e * (1.0 - e * (0.5 - e * (1.0 / 3.0 - 0.25 * e)))
    return jnp.maximum(v, 0.0) + jnp.where(e < 0.015625, series, jnp.log(u))


def transposed_dot(lhs, rhs):
    return lax.dot_general(
        lhs, rhs, (((1,), (1,)), ((), ())), precision=highest, preferred_element_type=f32
    )


def decay_terms(dt_ref, rate_ref):
    step = softplus(dt_ref[...])
    log = -jnp.exp(rate_ref[...]) * step
    t = lax.broadcasted_iota(jnp.int32, (SPAN, SPAN), 0)
    s = lax.broadcasted_iota(jnp.int32, (SPAN, SPAN), 1)
    lower = jnp.where(t >= s, 1.0, 0.0).astype(f32)
    eye = jnp.where(t == s, 1.0, 0.0).astype(f32)
    cumul_row = transposed_dot(log, lower)
    cumul_col = transposed_dot(lower, log)
    step_col = transposed_dot(eye, step)
    return step, step_col, cumul_row, cumul_col, t >= s


def state_kernel(
    g_ref, inner, bin_, cin, dt, rate, wx, bx, wb, wc, bb, bc, halo_x, halo_b, halo_c,
    x_out, b_out, c_out, enter_out, send_out, local_out,
    prev_x, prev_b, prev_c, state, total,
):
    i = pl.program_id(0)
    heads = dt.shape[0]

    @pl.when(i == 0)
    def _():
        prev_x[...] = halo_x[...].astype(f32)
        prev_b[...] = halo_b[...].astype(f32)
        prev_c[...] = halo_c[...].astype(f32)
        state[...] = jnp.zeros_like(state)
        total[...] = jnp.zeros_like(total)

    conv_block(inner, prev_x, wx, bx, x_out, 256)
    conv_block(bin_, prev_b, wb, bb, b_out, 256)
    conv_block(cin, prev_c, wc, bc, c_out, 256)
    step, step_col, cumul_row, cumul_col, causal = decay_terms(dt, rate)
    last = cumul_col[SPAN - 1 :]
    matrix = spread_matrix(heads)
    weights = spread(jnp.exp(last - cumul_col) * step_col, matrix)
    last8 = spread(jnp.broadcast_to(last, (8, heads)), matrix)
    enter_out[0] = state[...].astype(bf16)
    weighted = (x_out[...].astype(f32) * weights).astype(bf16)
    b_t = b_out[...].astype(f32).T.astype(bf16)
    written = jnp.dot(b_t, weighted, preferred_element_type=f32)
    state[...] = jnp.exp(last8[:1]) * state[...] + written
    total[...] += last8

    @pl.when(i == pl.num_programs(0) - 1)
    def _():
        local_out[...] = state[...]
        send_out[:STATE] = state[...].astype(bf16)
        tl = total[:1]
        high = tl.astype(bf16).astype(f32)
        row = lax.broadcasted_iota(jnp.int32, (EXTRA, tl.shape[1]), 0)
        send_out[STATE:] = jnp.where(row == 0, high, jnp.where(row == 1, tl - high, 0.0)).astype(bf16)


PARTS = 4


def chain_kernel(
    x, b, c, dt, rate, skip, enter, local, sent, y_out, prior_out,
    land, hop, send_sem, recv_sem,
):
    i = pl.program_id(0)
    seq = lax.axis_index("seq")
    last = 3
    wide = land.shape[2]

    def copy(k):
        return pltpu.make_async_remote_copy(
            src_ref=hop.at[k], dst_ref=land.at[k],
            send_sem=send_sem.at[k], recv_sem=recv_sem.at[k],
            device_id={"seq": (seq + 1) % 4}, device_id_type=MESH,
        )

    def joined(k):
        cols = slice(k * wide, (k + 1) * wide)
        own = sent[STATE : STATE + 1, cols].astype(f32) + sent[STATE + 1 : STATE + 2, cols].astype(f32)
        tail = land[k, STATE:].astype(f32)
        hop[k, :STATE] = (
            jnp.exp(own) * land[k, :STATE].astype(f32) + local[:, cols]
        ).astype(bf16)
        log = tail[0:1] + tail[1:2] + own
        high = log.astype(bf16).astype(f32)
        row = lax.broadcasted_iota(jnp.int32, (EXTRA, wide), 0)
        hop[k, STATE:] = jnp.where(row == 0, high, jnp.where(row == 1, log - high, 0.0)).astype(bf16)

    @pl.when(i == 0)
    def _():
        barrier = pltpu.get_barrier_semaphore()

        for by in (1, 3):
            pl.semaphore_signal(
                barrier, inc=1, device_id={"seq": (seq + by) % 4}, device_id_type=MESH
            )
        pl.semaphore_wait(barrier, 2)

        @pl.when(seq == 0)
        def _():
            for k in range(PARTS):
                hop[k] = sent[:, k * wide : (k + 1) * wide]
                copy(k).start()

        @pl.when(seq == 1)
        def _():
            for k in range(PARTS):
                copy(k).wait_recv()
                joined(k)
                copy(k).start()

    local_kernel(x, b, c, dt, rate, skip, enter, y_out)

    @pl.when(i == pl.num_programs(0) - 1)
    def _():
        @pl.when(seq == 2)
        def _():
            for k in range(PARTS):
                copy(k).wait_recv()
                joined(k)
                copy(k).start()

        @pl.when(seq == 3)
        def _():
            for k in range(PARTS):
                copy(k).wait_recv()

        @pl.when(seq > 0)
        def _():
            for k in range(PARTS):
                prior_out[:, k * wide : (k + 1) * wide] = land[k]

        @pl.when(seq == 0)
        def _():
            prior_out[...] = jnp.zeros_like(prior_out)

        @pl.when(seq < last)
        def _():
            for k in range(PARTS):
                copy(k).wait_send()


def local_kernel(x, b, c, dt, rate, skip, enter, y_out):
    heads = dt.shape[0]
    step, step_col, cumul_row, cumul_col, causal = decay_terms(dt, rate)
    matrix = spread_matrix(heads)
    scores = lax.dot_general(
        c[...], b[...], (((1,), (1,)), ((), ())), preferred_element_type=f32
    )
    row_term = jnp.log(step) - cumul_row
    growth = spread(jnp.exp(cumul_col), matrix)
    skip_row = spread(jnp.broadcast_to(skip[...], (8, heads)), matrix)[:1]
    lane = lax.broadcasted_iota(jnp.int32, (SPAN, 2 * HEADDIM), 1)
    zero = jnp.zeros((SPAN, 2 * HEADDIM), bf16)
    for pair in range(heads // 2):
        cols = slice(pair * 2 * HEADDIM, (pair + 1) * 2 * HEADDIM)
        mixers = []
        for h in (2 * pair, 2 * pair + 1):
            power = jnp.where(causal, cumul_col[:, h : h + 1] + row_term[h : h + 1], -1e30)
            mixers.append((scores * jnp.exp(power)).astype(bf16))
        xp = x[:, cols]
        both = jnp.concatenate(
            [jnp.where(lane < HEADDIM, xp, zero), jnp.where(lane >= HEADDIM, xp, zero)], axis=0
        )
        inside = jnp.dot(
            jnp.concatenate(mixers, axis=1), both, preferred_element_type=f32
        )
        carried = jnp.dot(c[...], enter[0, :, cols], preferred_element_type=f32)
        y_out[:, cols] = (
            inside + growth[:, cols] * carried + skip_row[:, cols] * xp.astype(f32)
        )


def output_kernel(
    meta, y, c, gate, dt, rate, gain, gathered, own_tail, init, local, normed_out, boundary_out,
    incoming, entering, mixed, offset, *, block, halves, whole_group, chained,
):
    i = pl.program_id(0)
    heads = dt.shape[0]
    width = y.shape[1]
    count = gathered.shape[0]

    @pl.when(i == 0)
    def _():
        place = meta[0]
        rate_sum = jnp.zeros((1, width), f32)
        incoming[...] = jnp.zeros_like(incoming)
        if chained:
            tail = gathered[0, STATE:].astype(f32)
            incoming[...] = gathered[0, :STATE].astype(f32)
            rate_sum = tail[0:1] + tail[1:2]
        for k in range(-1 if chained else count - 2, -1, -1):
            live = k < place
            tail = gathered[k, STATE:].astype(f32)
            factor = jnp.where(live, jnp.exp(rate_sum), 0.0)
            incoming[...] += factor * gathered[k, :STATE].astype(f32)
            rate_sum = rate_sum + jnp.where(live, tail[0:1] + tail[1:2], 0.0)
        tail = (own_tail[...] if chained else gathered[place, STATE:]).astype(f32)
        own = jnp.exp(tail[0:1] + tail[1:2])
        for k in range(0, width, 256):
            cols = slice(k, k + 256)
            value = incoming[:, cols] + jnp.exp(rate_sum[:, cols]) * init[cols, :].T
            entering[:, cols] = value.astype(bf16)
            boundary_out[cols, :] = (own[:, cols] * value + local[:, cols]).T
        offset[...] = jnp.zeros_like(offset)

    step, step_col, cumul_row, cumul_col, causal = decay_terms(dt, rate)
    cumul_col = cumul_col + offset[:1]
    offset[...] = jnp.broadcast_to(cumul_col[SPAN - 1 :], offset.shape)
    growth = spread(jnp.exp(cumul_col), spread_matrix(heads))
    squares = jnp.zeros((SPAN, 1), f32)
    for k in range(0, width, 256):
        cols = slice(k, k + 256)
        carried = jnp.dot(c[...], entering[:, cols], preferred_element_type=f32)
        value = (y[:, cols] + growth[:, cols] * carried) * silu(gate[:, cols].astype(f32))
        mixed[:, cols] = value
        squares = squares + jnp.sum(value * value, axis=1, keepdims=True)
    if whole_group:
        inverse = lax.rsqrt(squares / width + norm_eps)
    piece = block // halves
    for q in range(SPAN // piece):
        rows = slice(q * piece, (q + 1) * piece)
        first = meta[1 + i * (SPAN // block) + q // halves]
        first = first + (q % halves) * (normed_out.shape[0] // halves)
        value = mixed[rows, :]
        if whole_group:
            value = value * inverse[rows] * gain[...]
        normed_out[pl.ds(pl.multiple_of(first, piece), piece), :] = value.astype(normed_out.dtype)


def partner_of(place, bit):
    size = 1 << bit
    return place + (1 - 2 * ((place // size) % 2)) * size


HALVES = 2
QUARTERS = 4
WIDES = 3
NARROWS = 4
NARROW = 256
ARRIVED = 8
WIDE_Z = (1, 2, 3)
NARROW_Z = (0, 1, 7)
ORDER = (
    131, 129, 130, 2, 4, 162, 0, 1, 163, 5, 36, 194, 32, 195, 34, 68, 3, 33,
    256, 7, 128, 64, 66, 6, 37, 65, 39, 8, 69, 35, 98, 38, 71, 257, 133, 10,
    40, 70, 9, 134, 165, 135, 72, 101, 197, 42, 11, 167, 67, 132, 103, 41, 74, 96,
    166, 161, 229, 73, 43, 198, 97, 199, 100, 160, 105, 102, 104, 227, 164, 106, 75, 196,
    226, 192, 231, 193, 230, 99, 107, 228, 224, 225,
)


def tanh_silu(v):
    half = 0.5 * v
    return half + half * jnp.tanh(half)


def two_terms(values):
    high = values.astype(bf16)
    low = (values - high.astype(f32)).astype(bf16)
    return jnp.concatenate([high, low], axis=1)


def fill_matrix(matrix):
    heads = matrix.shape[0] // 2
    h = lax.broadcasted_iota(jnp.int32, matrix.shape, 0) % heads
    c = lax.broadcasted_iota(jnp.int32, matrix.shape, 1) // HEADDIM
    matrix[...] = jnp.where(c == h, 1.0, 0.0).astype(bf16)


def token_decays(dt, rate):
    step = softplus(dt).T
    log = -jnp.exp(rate) * step
    t = lax.broadcasted_iota(jnp.int32, (SPAN, SPAN), 0)
    s = lax.broadcasted_iota(jnp.int32, (SPAN, SPAN), 1)
    lower = jnp.where(t >= s, 1.0, 0.0).astype(f32)
    cumul = [
        jnp.dot(lower, log[k : k + SPAN], precision=highest, preferred_element_type=f32)
        for k in range(0, log.shape[0], SPAN)
    ]
    return step, cumul, t >= s


def conv_tile(cur, prev8, weight, bias):
    total = bias + weight[KERNEL - 1 : KERNEL] * cur
    for by in range(1, KERNEL):
        k = KERNEL - 1 - by
        total = total + weight[k : k + 1] * shifted(cur, prev8, by)
    return tanh_silu(total).astype(bf16)


def layer_kernel(
    inner, gate_all, bc_all, dt, rate, skip, wx, bx, wbc, bbc, tail_x, tail_bc, init_all, gain, w_own,
    out, state_out,
    x, gate, bc, halo_x, halo_bc, prev, b_t, weight, factors, matrix, scaled, total, state,
    land, hop, left, squares, w, w_last, acts,
    keep, y_send, y_recv, a_send, a_recv, b_send, b_recv, out_held, x_send, x_recv,
    n_keep, ny_send, ny_recv, na_send, na_recv, nb_send, nb_recv, n_held, nx_send, nx_recv,
    in_sem, load_sem, init_sem, halo_send, halo_recv, hop_send, hop_recv, w_sem, w_send, w_recv,
    act_send_sem, act_recv_sem,
    send_sem, recv_sem, out_sem, x_send_sem, x_recv_sem,
    n_send_sem, n_recv_sem, n_out_sem, nx_send_sem, nx_recv_sem,
):
    seq = lax.axis_index("seq")
    head = lax.axis_index("head")
    rows, width = x.shape
    heads = dt.shape[0]
    spans = rows // SPAN
    strip = width // QUARTERS
    wide = w.shape[2]
    columns = w_own.shape[1]
    piece = out.shape[0] // HALVES
    wides = keep.shape[0] // 2
    narrows = n_keep.shape[0] // 2
    other_chip = (seq + 2) % 4
    near = [partner_of(head, bit) for bit in range(3)]
    across = [{"head": place} for place in near]
    over_x = {"seq": other_chip}
    after = {"seq": (seq + 1) % 4}
    other_core = {"seq": partner_of(seq, 0)}
    firsts = [pl.multiple_of((head + g) * STATE, STATE) for g in (0, GROUPS)]
    chunk = 256

    def remote(source, dest, send, recv, target):
        return pltpu.make_async_remote_copy(
            src_ref=source, dst_ref=dest, send_sem=send, recv_sem=recv,
            device_id=target, device_id_type=MESH,
        )

    def strip_of(k):
        return pl.ds(pl.multiple_of(k * strip, strip), strip)

    def inner_copy(k):
        cols = slice(k * strip, (k + 1) * strip)
        return pltpu.make_async_copy(inner.at[:, cols], x.at[:, cols], in_sem.at[k])

    def bc_copy(k):
        return pltpu.make_async_copy(
            bc_all.at[:, pl.ds(firsts[k], STATE)], bc.at[k], load_sem.at[k]
        )

    def gate_copy():
        return pltpu.make_async_copy(gate_all, gate, load_sem.at[2])

    def init_copies():
        place = [(k, r) for k in range(QUARTERS) for r in range(strip // SPAN)]
        return [
            pltpu.make_async_copy(
                init_all.at[k * strip + r * SPAN : k * strip + (r + 1) * SPAN],
                keep.at[k, 0, :, r * STATE : (r + 1) * STATE],
                init_sem.at[k, r],
            )
            for k, r in place
        ]

    def state_copy():
        return pltpu.make_async_copy(state, state_out, load_sem.at[3])

    def own_first():
        return pltpu.make_async_copy(w_own.at[:, :wide], w.at[0], w_sem.at[0])

    def own_second():
        return pltpu.make_async_copy(w_own.at[:, wide:], w_last, w_sem.at[1])

    def other_weights(k):
        narrow = wide // 2
        place = slice(k % 2 * narrow, (k % 2 + 1) * narrow)
        source = w.at[0, :, place] if k < 2 else w_last.at[:, place]
        return remote(
            source, w.at[1 + k // 2, :, place], w_send.at[k], w_recv.at[k], other_core
        )

    def halo_copies():
        last = pl.ds(rows - 16, 16)
        pairs = [(inner.at[last], halo_x)] + [
            (bc_all.at[last, pl.ds(firsts[k], STATE)], halo_bc.at[k]) for k in range(2)
        ]
        return [
            remote(source, dest, halo_send.at[k], halo_recv.at[k], after)
            for k, (source, dest) in enumerate(pairs)
        ]

    def hop_copy(k):
        return remote(hop.at[k], land.at[k], hop_send.at[k], hop_recv.at[k], after)

    def act_copy(half):
        return remote(
            acts.at[0, half], acts.at[1, half], act_send_sem.at[half], act_recv_sem.at[half], over_x
        )

    def chip_copy(k):
        return remote(x_send.at[k], x_recv.at[k], x_send_sem.at[k], x_recv_sem.at[k], over_x)

    def chip_copy_narrow(k):
        return remote(nx_send.at[k], nx_recv.at[k], nx_send_sem.at[k], nx_recv_sem.at[k], over_x)

    def chosen(t, those):
        value = 0
        for k in those:
            value = value + jnp.where(t == k, 1, 0)
        return value

    broad = (
        keep, ((y_send, y_recv), (a_send, a_recv), (b_send, b_recv)), send_sem, recv_sem, WIDE_Z
    )
    slim = (
        n_keep, ((ny_send, ny_recv), (na_send, na_recv), (nb_send, nb_recv)),
        n_send_sem, n_recv_sem, NARROW_Z,
    )

    def head_copy(family, stage, t):
        _, buffers, sent, received, those = family
        source, dest = buffers[stage]
        target = across[2]
        if stage < 2:
            target = {"head": near[stage] + chosen(t, those) * (near[1 - stage] - near[stage])}
        return remote(source.at[t], dest.at[t], sent.at[stage, t], received.at[stage, t], target)

    for k in range(2):
        bc_copy(k).start()
    for k in range(QUARTERS):
        inner_copy(k).start()

    barrier = pltpu.get_barrier_semaphore()
    greeted = across + [over_x, after, {"seq": (seq + 3) % 4}]
    for target in greeted:
        pl.semaphore_signal(barrier, inc=1, device_id=target, device_id_type=MESH)

    own_first().start()
    own_second().start()
    for copy in init_copies():
        copy.start()
    gate_copy().start()

    fill_matrix(matrix)
    step, cumul, causal = token_decays(dt[...], rate[...])
    ends = [value[SPAN - 1 :] for value in cumul]
    later = jnp.zeros_like(ends[0])
    for k in range(spans - 1, -1, -1):
        span = slice(k * SPAN, (k + 1) * SPAN)
        later = later + ends[k]
        weight[span] = two_terms(jnp.exp(later - cumul[k]) * step[span])
    row = lax.broadcasted_iota(jnp.int32, (16, heads), 0)
    high = later.astype(bf16).astype(f32)
    total[...] = two_terms(jnp.where(row < 8, high, later - high))

    pl.semaphore_wait(barrier, len(greeted))

    @pl.when(seq < 3)
    def _():
        for copy in halo_copies():
            copy.start()

    def conv_rows(source, k, cols, before, kernel, bias):
        span = slice(k * SPAN, (k + 1) * SPAN)
        if k:
            before = source[k * SPAN - 16 : k * SPAN, cols].astype(f32)[8:]
        value = conv_tile(source[span, cols].astype(f32), before, kernel, bias)
        source[span, cols] = value
        return value

    def conv_bc(g, k):
        at = pl.ds(firsts[g], STATE)
        before = None if k else prev[:, strip + g * STATE : strip + (g + 1) * STATE]
        return conv_rows(bc.at[g], k, slice(0, STATE), before, wbc[:, at], bbc[:, at])

    def conv_b(k):
        value = conv_bc(0, k)
        b_t[:, k * SPAN : (k + 1) * SPAN] = value.astype(f32).T.astype(bf16)

    for k in range(2):
        bc_copy(k).wait()
    for k in range(spans - 1, 0, -1):
        conv_b(k)

    @pl.when(seq > 0)
    def _():
        for copy in halo_copies():
            copy.wait_recv()
        for g in range(2):
            prev[:, strip + g * STATE : strip + (g + 1) * STATE] = halo_bc[g].astype(f32)[8:]

    @pl.when(seq == 0)
    def _():
        for g in range(2):
            prev[8 - KERNEL + 1 :, strip + g * STATE : strip + (g + 1) * STATE] = tail_bc[
                :, pl.ds(firsts[g], STATE)
            ].astype(f32)
        land[...] = jnp.zeros_like(land)

    conv_b(0)

    def totals(k):
        spread_log = jnp.dot(total[...], matrix[:, strip_of(k)], preferred_element_type=f32)
        return spread_log[0:1] + spread_log[8:9]

    def fill_hop(k, value, log):
        hop[k, :STATE] = value.astype(bf16)
        top = log.astype(bf16).astype(f32)
        line = lax.broadcasted_iota(jnp.int32, (EXTRA, strip), 0)
        hop[k, STATE:] = jnp.where(line == 0, top, jnp.where(line == 1, log - top, 0.0)).astype(bf16)
        hop_copy(k).start()

    def pass_on(k):
        hop_copy(k).wait_recv()
        own = totals(k)
        tail = land[k, STATE:].astype(f32)
        fill_hop(
            k,
            jnp.exp(own) * land[k, :STATE].astype(f32) + state[:, strip_of(k)],
            tail[0:1] + tail[1:2] + own,
        )

    for k in range(QUARTERS):
        inner_copy(k).wait()

    def quarter(q, carry):
        @pl.when(seq > 0)
        def _():
            prev[:, :strip] = halo_x[:, strip_of(q)].astype(f32)[8:]

        @pl.when(seq == 0)
        def _():
            prev[8 - KERNEL + 1 :, :strip] = tail_x[:, strip_of(q)].astype(f32)

        for k in range(spans - 1, -1, -1):
            span = slice(k * SPAN, (k + 1) * SPAN)
            for c in range(0, strip, chunk):
                at = pl.ds(pl.multiple_of(q * strip + c, chunk), chunk)
                value = conv_rows(x, k, at, prev[:, c : c + chunk], wx[:, at], bx[:, at])
                factor = jnp.dot(weight[span], matrix[:, at], preferred_element_type=f32)
                scaled[span, c : c + chunk] = (value.astype(f32) * factor).astype(bf16)
        state[:, strip_of(q)] = jnp.dot(b_t[...], scaled[...], preferred_element_type=f32)

        @pl.when(seq == 0)
        def _():
            fill_hop(q, state[:, strip_of(q)], totals(q))

        @pl.when((seq == 1) & (q > 0))
        def _():
            pass_on(q - 1)

        @pl.when(q == 0)
        def _():
            own_first().wait()

        @pl.when(q == 2)
        def _():
            own_second().wait()

        for k in range(QUARTERS):
            @pl.when(q == k)
            def _():
                other_weights(k).start()

        return carry

    lax.fori_loop(0, QUARTERS, quarter, 0)

    @pl.when(seq == 1)
    def _():
        pass_on(QUARTERS - 1)

    for k in range(spans - 1, -1, -1):
        conv_bc(1, k)

    for k in range(spans):
        middle = 0.5 * ends[k]
        factors[k] = two_terms(
            jnp.concatenate(
                [
                    jnp.exp(cumul[k] - middle),
                    jnp.exp(middle - cumul[k]) * step[k * SPAN : (k + 1) * SPAN],
                    jnp.broadcast_to(jnp.exp(middle), (8, heads)),
                    jnp.broadcast_to(skip[...], (8, heads)),
                ],
                axis=0,
            )
        )

    for i in range(spans):
        span = slice(i * SPAN, (i + 1) * SPAN)
        scores = lax.dot_general(
            bc[1, span], bc[0, span], (((1,), (1,)), ((), ())), preferred_element_type=f32
        )
        left[i, :, :SPAN] = jnp.where(causal, scores, 0.0).astype(bf16)
        left[i, :, SPAN:] = bc[1, span]
    squares[...] = jnp.zeros_like(squares)
    for copy in init_copies():
        copy.wait()
    gate_copy().wait()

    def gated(q, carry):
        @pl.when(seq == 2)
        def _():
            pass_on(q)

        @pl.when(seq == 3)
        def _():
            hop_copy(q).wait_recv()

        tail = land[q, STATE:].astype(f32)
        factor = jnp.exp(tail[0:1] + tail[1:2])
        for r in range(strip // SPAN):
            lanes = slice(r * SPAN, (r + 1) * SPAN)
            at = pl.ds(pl.multiple_of(q * strip + r * SPAN, SPAN), SPAN)
            state[:, at] = (
                land[q, :STATE, lanes].astype(f32)
                + factor[:, lanes] * keep[q, 0, :, r * STATE : (r + 1) * STATE].T
            )
        cols = strip_of(q)
        spot = pl.ds(pl.multiple_of(q % 2 * strip, strip), strip)
        for i in range(spans):
            span = slice(i * SPAN, (i + 1) * SPAN)
            spread_all = jnp.dot(factors[i], matrix[:, cols], preferred_element_type=f32)
            half_decay = spread_all[2 * SPAN : 2 * SPAN + 1]
            value = x[span, cols].astype(f32)
            weighted = (value * spread_all[SPAN : 2 * SPAN]).astype(bf16)
            before = half_decay * state[:, cols]
            inside = jnp.dot(
                left[i], jnp.concatenate([weighted, before.astype(bf16)], axis=0),
                preferred_element_type=f32,
            )
            written = jnp.dot(b_t[:, span], weighted, preferred_element_type=f32)
            state[:, cols] = half_decay * (before + written)
            value = spread_all[:SPAN] * inside + spread_all[2 * SPAN + 8 : 2 * SPAN + 9] * value
            value = value * tanh_silu(gate[span, cols].astype(f32))
            keep[QUARTERS + 2 * i + q // 2, 0, :, spot] = value
            square = value * value
            for c in range(0, strip, 128):
                squares[i] = squares[i] + square[:, c : c + 128]
        return carry

    lax.fori_loop(0, QUARTERS, gated, 0)

    def normalized(half):
        block = HALVES * piece
        for i in range(spans):
            for p in range(SPAN // block):
                first = p * block + half * piece
                lines = slice(first, first + piece)
                inverse = lax.rsqrt(
                    jnp.sum(squares[i, lines], axis=1, keepdims=True) / width + norm_eps
                )
                owner = i * (SPAN // block) + p
                slot = 0
                for bit in range(3):
                    differs = (owner // (1 << bit) + head // (1 << bit)) % 2
                    slot = slot + differs * (4 >> bit)
                place = pl.ds(pl.multiple_of(slot * piece, piece), piece)
                for c in range(width // wide):
                    cols = slice(c * wide, (c + 1) * wide)
                    acts[0, half, place, cols] = (
                        keep[QUARTERS + 2 * i + c, 0, lines, :] * inverse * gain[:, cols]
                    ).astype(bf16)

    for half in range(HALVES):
        normalized(half)
        act_copy(half).start()
    state_copy().start()

    two = 2 * piece

    def send_product(family, t, product):
        held, buffers, _, _, those = family
        near_z = chosen(t, those) == 1
        sending = buffers[0][0]
        middle = [product[:, two : 2 * two], product[:, 2 * two : 3 * two]]
        sending[t, :, :two] = jnp.where(near_z, middle[0], middle[1]).astype(bf16)
        sending[t, :, two:] = product[:, 3 * two :].astype(bf16)
        head_copy(family, 0, t).start()
        held[t, :, :two] = product[:, :two]
        held[t, :, two:] = jnp.where(near_z, middle[1], middle[0])

    def first_stage(family, t):
        held, buffers = family[:2]
        arrived, sending = buffers[0][1], buffers[1][0]
        head_copy(family, 0, t).wait_recv()
        sending[t] = (held[t, :, two:] + arrived[t, :, two:].astype(f32)).astype(bf16)
        head_copy(family, 1, t).start()
        held[t, :, :two] = held[t, :, :two] + arrived[t, :, :two].astype(f32)

    def second_stage(family, t):
        held, buffers = family[:2]
        arrived, sending = buffers[1][1], buffers[2][0]
        head_copy(family, 1, t).wait_recv()
        sending[t] = (held[t, :, piece:two] + arrived[t, :, piece:].astype(f32)).astype(bf16)
        head_copy(family, 2, t).start()
        held[t, :, :piece] = held[t, :, :piece] + arrived[t, :, :piece].astype(f32)

    def third_stage(family, t):
        held, buffers = family[:2]
        head_copy(family, 2, t).wait_recv()
        return (held[t, :, :piece] + buffers[2][1][t].astype(f32)).astype(bf16)

    def wide_out(source, slot, home, t):
        group, half = t % WIDES, (t % wides) // WIDES
        partner = partner_of(home, 0)
        column = jnp.where(group == 0, home, partner) * columns + (group // 2) * wide
        place = pl.ds(pl.multiple_of(half * piece, piece), piece)
        return pltpu.make_async_copy(
            source.at[t], out.at[place, pl.ds(pl.multiple_of(column, wide), wide)], out_sem.at[slot]
        )

    def narrow_out(source, slot, home, t):
        column = home * columns + wide + t * NARROW
        return pltpu.make_async_copy(
            source.at[t], out.at[:, pl.ds(pl.multiple_of(column, NARROW), NARROW)],
            n_out_sem.at[slot],
        )

    def wide_multiply(t):
        place, half, group = t // wides, (t % wides) // WIDES, t % WIDES
        product = jnp.dot(acts[place, half], w[group], preferred_element_type=f32)
        send_product(broad, t, product[None])

    def narrow_multiply(t):
        lines = acts[t // NARROWS].reshape(rows, width)
        cols = pl.ds(pl.multiple_of(t % NARROWS * NARROW, NARROW), NARROW)
        product = jnp.dot(lines, w_last[:, cols], preferred_element_type=f32)
        send_product(slim, t, product.reshape(HALVES, rows // HALVES, NARROW))

    def wide_third(t):
        value = third_stage(broad, t)[0]

        @pl.when(t < wides)
        def _():
            out_held[t] = value
            wide_out(out_held, t, seq, t).start()

        @pl.when(t >= wides)
        def _():
            x_send[t - wides] = value
            chip_copy(t - wides).start()

    def narrow_third(t):
        value = third_stage(slim, t)

        @pl.when(t < NARROWS)
        def _():
            for half in range(HALVES):
                n_held[t, half * piece : (half + 1) * piece] = value[half]
            narrow_out(n_held, t, seq, t).start()

        @pl.when(t >= NARROWS)
        def _():
            for half in range(HALVES):
                nx_send[t - NARROWS, half * piece : (half + 1) * piece] = value[half]
            chip_copy_narrow(t - NARROWS).start()

    handlers = [
        wide_multiply,
        lambda t: first_stage(broad, t),
        lambda t: second_stage(broad, t),
        wide_third,
        narrow_multiply,
        lambda t: first_stage(slim, t),
        lambda t: second_stage(slim, t),
        narrow_third,
        lambda t: act_copy(t).wait_recv(),
    ]
    words = [
        sum(code << (9 * j) for j, code in enumerate(ORDER[k : k + 3]))
        for k in range(0, len(ORDER), 3)
    ]

    def event(i, carry):
        word = 0
        for k, value in enumerate(words):
            word = word + jnp.where(i // 3 == k, value, 0)
        low, mid, top = word % 512, word // 512 % 512, word // 262144
        code = jnp.where(i % 3 == 0, low, jnp.where(i % 3 == 1, mid, top))
        kind, t = code // 32, code % 32
        for k, handler in enumerate(handlers):
            @pl.when(kind == k)
            def _():
                handler(t)

        return carry

    for k in range(QUARTERS):
        other_weights(k).wait_recv()
    lax.fori_loop(0, len(ORDER), event, 0)

    def collect(k, carry):
        chip_copy(k).wait_recv()
        wide_out(x_recv, wides + k, other_chip, k).start()
        return carry

    def collect_narrow(k, carry):
        chip_copy_narrow(k).wait_recv()
        narrow_out(nx_recv, NARROWS + k, other_chip, k).start()
        return carry

    lax.fori_loop(0, wides, collect, 0)
    lax.fori_loop(0, NARROWS, collect_narrow, 0)

    for half in range(HALVES):
        act_copy(half).wait_send()
    for k in range(QUARTERS):
        other_weights(k).wait_send()
    state_copy().wait()

    @pl.when(seq < 3)
    def _():
        for k in range(QUARTERS):
            hop_copy(k).wait_send()
        for copy in halo_copies():
            copy.wait_send()

    def drain(t, carry):
        for stage in range(3):
            head_copy(broad, stage, t).wait_send()
        return carry

    def drain_narrow(t, carry):
        for stage in range(3):
            head_copy(slim, stage, t).wait_send()
        return carry

    def drain_out(k, carry):
        wide_out(out_held, k, seq, k).wait()
        wide_out(x_recv, wides + k, other_chip, k).wait()
        chip_copy(k).wait_send()
        return carry

    def drain_narrow_out(k, carry):
        narrow_out(n_held, k, seq, k).wait()
        narrow_out(nx_recv, NARROWS + k, other_chip, k).wait()
        chip_copy_narrow(k).wait_send()
        return carry

    lax.fori_loop(0, 2 * wides, drain, 0)
    lax.fori_loop(0, 2 * NARROWS, drain_narrow, 0)
    lax.fori_loop(0, wides, drain_out, 0)
    lax.fori_loop(0, NARROWS, drain_narrow_out, 0)


FINISH = 4


def finish_kernel(summed, state, out, boundary_out, sums, columns, rows, sem):
    wide, strip = sums.shape[1] // FINISH, columns.shape[1] // FINISH

    def part(k, step):
        return slice(k * step, (k + 1) * step)

    def copies(k):
        return [
            pltpu.make_async_copy(state.at[:, part(k, strip)], columns.at[:, part(k, strip)], sem.at[0, k]),
            pltpu.make_async_copy(summed.at[:, part(k, wide)], sums.at[:, part(k, wide)], sem.at[1, k]),
            pltpu.make_async_copy(rows.at[part(k, strip)], boundary_out.at[part(k, strip)], sem.at[2, k]),
            pltpu.make_async_copy(sums.at[:, part(k, wide)], out.at[:, part(k, wide)], sem.at[3, k]),
        ]

    for k in range(FINISH):
        for copy in copies(k)[:2]:
            copy.start()
    for k in range(FINISH):
        state_in, sum_in, state_back, sum_back = copies(k)
        state_in.wait()
        rows[part(k, strip)] = columns[:, part(k, strip)].T
        state_back.start()
        sum_in.wait()
        sum_back.start()
    for k in range(FINISH):
        for copy in copies(k)[2:]:
            copy.wait()


def layer(inner, gate, bc, dt, rate, skip, wx, bx, wbc, bbc, tail_x, tail_bc, init, gain, own):
    rows, width = inner.shape
    heads = dt.shape[0]
    columns = own.shape[1]
    strip = width // QUARTERS
    block = rows // 8
    piece = block // HALVES
    wide = columns // 2
    wides = HALVES * WIDES
    half_rows = rows // HALVES
    spans = rows // SPAN
    anywhere = pl.BlockSpec(memory_space=pl.ANY)
    vmem = pl.BlockSpec(memory_space=pltpu.VMEM)
    slots = (QUARTERS, STATE + EXTRA, strip)
    dma = pltpu.SemaphoreType.DMA
    summed, state = pl.pallas_call(
        layer_kernel,
        in_specs=[anywhere] * 3 + [vmem] * 9 + [anywhere, vmem, anywhere],
        out_specs=[anywhere, anywhere],
        out_shape=[
            jax.ShapeDtypeStruct((block, 4 * columns), bf16),
            jax.ShapeDtypeStruct((STATE, width), f32),
        ],
        scratch_shapes=[
            pltpu.VMEM((rows, width), bf16),
            pltpu.VMEM((rows, width), bf16),
            pltpu.VMEM((2, rows, STATE), bf16),
            pltpu.VMEM((16, width), bf16),
            pltpu.VMEM((2, 16, STATE), bf16),
            pltpu.VMEM((8, strip + 2 * STATE), f32),
            pltpu.VMEM((STATE, rows), bf16),
            pltpu.VMEM((rows, 2 * heads), bf16),
            pltpu.VMEM((spans, 2 * SPAN + 16, 2 * heads), bf16),
            pltpu.VMEM((2 * heads, width), bf16),
            pltpu.VMEM((rows, strip), bf16),
            pltpu.VMEM((16, 2 * heads), bf16),
            pltpu.VMEM((STATE, width), f32),
            pltpu.VMEM(slots, bf16),
            pltpu.VMEM(slots, bf16),
            pltpu.VMEM((spans, SPAN, SPAN + STATE), bf16),
            pltpu.VMEM((spans, SPAN, 128), f32),
            pltpu.VMEM((WIDES, width, wide), bf16),
            pltpu.VMEM((width, wide), bf16),
            pltpu.VMEM((2, HALVES, half_rows, width), bf16),
            pltpu.VMEM((2 * wides, 1, 4 * piece, wide), f32),
            pltpu.VMEM((2 * wides, 1, 4 * piece, wide), bf16),
            pltpu.VMEM((2 * wides, 1, 4 * piece, wide), bf16),
            pltpu.VMEM((2 * wides, 1, 2 * piece, wide), bf16),
            pltpu.VMEM((2 * wides, 1, 2 * piece, wide), bf16),
            pltpu.VMEM((2 * wides, 1, piece, wide), bf16),
            pltpu.VMEM((2 * wides, 1, piece, wide), bf16),
            pltpu.VMEM((wides, piece, wide), bf16),
            pltpu.VMEM((wides, piece, wide), bf16),
            pltpu.VMEM((wides, piece, wide), bf16),
            pltpu.VMEM((2 * NARROWS, HALVES, 4 * piece, NARROW), f32),
            pltpu.VMEM((2 * NARROWS, HALVES, 4 * piece, NARROW), bf16),
            pltpu.VMEM((2 * NARROWS, HALVES, 4 * piece, NARROW), bf16),
            pltpu.VMEM((2 * NARROWS, HALVES, 2 * piece, NARROW), bf16),
            pltpu.VMEM((2 * NARROWS, HALVES, 2 * piece, NARROW), bf16),
            pltpu.VMEM((2 * NARROWS, HALVES, piece, NARROW), bf16),
            pltpu.VMEM((2 * NARROWS, HALVES, piece, NARROW), bf16),
            pltpu.VMEM((NARROWS, block, NARROW), bf16),
            pltpu.VMEM((NARROWS, block, NARROW), bf16),
            pltpu.VMEM((NARROWS, block, NARROW), bf16),
            dma((QUARTERS,)),
            dma((4,)),
            dma((QUARTERS, strip // SPAN)),
            dma((3,)),
            dma((3,)),
            dma((QUARTERS,)),
            dma((QUARTERS,)),
            dma((2,)),
            dma((QUARTERS,)),
            dma((QUARTERS,)),
            dma((HALVES,)),
            dma((HALVES,)),
            dma((3, 2 * wides)),
            dma((3, 2 * wides)),
            dma((2 * wides,)),
            dma((wides,)),
            dma((wides,)),
            dma((3, 2 * NARROWS)),
            dma((3, 2 * NARROWS)),
            dma((2 * NARROWS,)),
            dma((NARROWS,)),
            dma((NARROWS,)),
        ],
        compiler_params=pltpu.CompilerParams(
            vmem_limit_bytes=LAYER_LIMIT, collective_id=0, has_side_effects=True
        ),
        name="layer",
    )(
        inner, gate, bc, dt, rate[None], skip[None], wx, bx[None], wbc, bbc[None], tail_x, tail_bc,
        init.reshape(width, STATE), gain[None], own,
    )
    return pl.pallas_call(
        finish_kernel,
        in_specs=[anywhere, anywhere],
        out_specs=[anywhere, anywhere],
        out_shape=[
            jax.ShapeDtypeStruct((block, 4 * columns), bf16),
            jax.ShapeDtypeStruct((width, STATE), f32),
        ],
        scratch_shapes=[
            pltpu.VMEM((block, 4 * columns), bf16),
            pltpu.VMEM((STATE, width), f32),
            pltpu.VMEM((width, STATE), f32),
            dma((4, FINISH)),
        ],
        compiler_params=pltpu.CompilerParams(vmem_limit_bytes=LAYER_LIMIT),
        name="finish",
    )(summed, state)


def params():
    return pltpu.CompilerParams(vmem_limit_bytes=VMEM_LIMIT)


def body(
    inner_input,
    gate_input,
    bc_input,
    dt_input,
    log_rate,
    skip_weight,
    conv_weight_x,
    conv_bias_x,
    conv_weight_bc,
    conv_bias_bc,
    conv_tail_x,
    conv_tail_bc,
    init_state,
    norm_gain,
    out_weight,
):
    seq_count = lax.axis_size("seq")
    head_count = lax.axis_size("head")
    seq_index = lax.axis_index("seq")
    head_index = lax.axis_index("head")
    rows, width = inner_input.shape
    heads = dt_input.shape[0]
    per_group = MIXER_HEADS // GROUPS
    group = (head_index * heads // per_group).astype(jnp.int32)
    spans = rows // SPAN
    block = rows // head_count
    group_width = DINNER // GROUPS
    whole_group = width == group_width

    projected = (
        seq_count == 4 and head_count == 8 and whole_group and rows == 512 and width == 2048
        and out_weight.shape[1] % 512 == 0
    )
    if projected:
        out, boundary = layer(
            inner_input, gate_input, bc_input, dt_input, log_rate, skip_weight, conv_weight_x,
            conv_bias_x, conv_weight_bc, conv_bias_bc, conv_tail_x, conv_tail_bc, init_state,
            norm_gain, out_weight,
        )
        return (out, boundary.reshape(1, heads, HEADDIM, STATE))

    other_core = lax.ppermute(out_weight, "seq", [(i, i ^ 1) for i in range(seq_count)])

    def pair_columns(table, axis):
        return [
            lax.dynamic_slice_in_dim(table, (g + group) * STATE, STATE, axis) for g in (0, GROUPS)
        ]

    tail_rows = rows - KERNEL + 1
    last_rows = jnp.concatenate(
        [inner_input[tail_rows:]] + pair_columns(bc_input[tail_rows:], 1), axis=1
    )
    arrived = lax.ppermute(last_rows, "seq", [(i, i + 1) for i in range(seq_count - 1)])
    first_rows = jnp.concatenate([conv_tail_x] + pair_columns(conv_tail_bc, 1), axis=1)
    halo = jnp.where(seq_index == 0, first_rows, arrived)
    halo = jnp.pad(halo, ((8 - KERNEL + 1, 0), (0, 0)))
    rate = log_rate[:, None]

    def const(shape, *index):
        return pl.BlockSpec(shape, lambda i, *_: index)

    span_x = pl.BlockSpec((SPAN, width), lambda i, *_: (i, 0))
    span_bc = pl.BlockSpec((SPAN, STATE), lambda i, *_: (i, 0))
    span_dt = pl.BlockSpec((heads, SPAN), lambda i, *_: (0, i))

    conv_x, conv_b, conv_c, enter, sent, local = pl.pallas_call(
        state_kernel,
        grid_spec=pltpu.PrefetchScalarGridSpec(
            num_scalar_prefetch=1,
            grid=(spans,),
            in_specs=[
                span_x,
                pl.BlockSpec((SPAN, STATE), lambda i, g: (i, g[0])),
                pl.BlockSpec((SPAN, STATE), lambda i, g: (i, g[0] + GROUPS)),
                span_dt,
                const((heads, 1), 0, 0),
                const((KERNEL, width), 0, 0),
                const((1, width), 0, 0),
                pl.BlockSpec((KERNEL, STATE), lambda i, g: (0, g[0])),
                pl.BlockSpec((KERNEL, STATE), lambda i, g: (0, g[0] + GROUPS)),
                pl.BlockSpec((1, STATE), lambda i, g: (0, g[0])),
                pl.BlockSpec((1, STATE), lambda i, g: (0, g[0] + GROUPS)),
                const((8, width), 0, 0),
                const((8, STATE), 0, width // STATE),
                const((8, STATE), 0, width // STATE + 1),
            ],
            out_specs=[
                span_x,
                span_bc,
                span_bc,
                pl.BlockSpec((1, STATE, width), lambda i, *_: (i, 0, 0)),
                const((STATE + EXTRA, width), 0, 0),
                const((STATE, width), 0, 0),
            ],
            scratch_shapes=[
                pltpu.VMEM((8, width), f32),
                pltpu.VMEM((8, STATE), f32),
                pltpu.VMEM((8, STATE), f32),
                pltpu.VMEM((STATE, width), f32),
                pltpu.VMEM((8, width), f32),
            ],
        ),
        out_shape=[
            jax.ShapeDtypeStruct((rows, width), bf16),
            jax.ShapeDtypeStruct((rows, STATE), bf16),
            jax.ShapeDtypeStruct((rows, STATE), bf16),
            jax.ShapeDtypeStruct((spans, STATE, width), bf16),
            jax.ShapeDtypeStruct((STATE + EXTRA, width), bf16),
            jax.ShapeDtypeStruct((STATE, width), f32),
        ],
        compiler_params=params(),
        name="conv_and_states",
    )(
        group[None],
        inner_input, bc_input, bc_input, dt_input, rate,
        conv_weight_x, conv_bias_x[None], conv_weight_bc, conv_weight_bc,
        conv_bias_bc[None], conv_bias_bc[None], halo, halo, halo,
    )

    chained = seq_count == 4 and width % (PARTS * 128) == 0
    local_specs = [
        span_x,
        span_bc,
        span_bc,
        span_dt,
        const((heads, 1), 0, 0),
        const((1, heads), 0, 0),
        pl.BlockSpec((1, STATE, width), lambda i: (i, 0, 0)),
    ]
    local_args = (conv_x, conv_b, conv_c, dt_input, rate, skip_weight[None], enter)
    y_shape = jax.ShapeDtypeStruct((rows, width), f32)
    if chained:
        slots = (PARTS, STATE + EXTRA, width // PARTS)
        y_local, prior = pl.pallas_call(
            chain_kernel,
            grid=(spans,),
            in_specs=local_specs
            + [const((STATE, width), 0, 0), const((STATE + EXTRA, width), 0, 0)],
            out_specs=[span_x, const((STATE + EXTRA, width), 0, 0)],
            out_shape=[y_shape, jax.ShapeDtypeStruct((STATE + EXTRA, width), bf16)],
            scratch_shapes=[
                pltpu.VMEM(slots, bf16),
                pltpu.VMEM(slots, bf16),
                pltpu.SemaphoreType.DMA((PARTS,)),
                pltpu.SemaphoreType.DMA((PARTS,)),
            ],
            compiler_params=pltpu.CompilerParams(
                vmem_limit_bytes=VMEM_LIMIT, collective_id=1, has_side_effects=True
            ),
            name="local_outputs_and_chain",
        )(*local_args, local, sent)
        gathered = prior[None]
    else:
        gathered = lax.all_gather(sent, "seq")
        y_local = pl.pallas_call(
            local_kernel,
            grid=(spans,),
            in_specs=local_specs,
            out_specs=span_x,
            out_shape=y_shape,
            compiler_params=params(),
            name="local_outputs",
        )(*local_args)

    bits = head_count.bit_length() - 1
    distance = jnp.arange(head_count, dtype=jnp.int32) ^ head_index
    slot = jnp.zeros_like(distance)
    for bit in range(bits):
        slot = slot + ((distance >> bit) & 1) * (head_count >> (bit + 1))
    meta = jnp.concatenate([seq_index[None].astype(jnp.int32), slot.astype(jnp.int32) * block])

    normed, boundary = pl.pallas_call(
        functools.partial(
            output_kernel, block=block, halves=1, whole_group=whole_group, chained=chained
        ),
        grid_spec=pltpu.PrefetchScalarGridSpec(
            num_scalar_prefetch=1,
            grid=(spans,),
            in_specs=[
                span_x,
                span_bc,
                span_x,
                span_dt,
                const((heads, 1), 0, 0),
                const((1, width), 0, 0),
                const((gathered.shape[0], STATE + EXTRA, width), 0, 0, 0),
                const((EXTRA, width), STATE // EXTRA, 0),
                const((width, STATE), 0, 0),
                const((STATE, width), 0, 0),
            ],
            out_specs=[const((rows, width), 0, 0), const((width, STATE), 0, 0)],
            scratch_shapes=[
                pltpu.VMEM((STATE, width), f32),
                pltpu.VMEM((STATE, width), bf16),
                pltpu.VMEM((SPAN, width), f32),
                pltpu.VMEM((8, heads), f32),
            ],
        ),
        out_shape=[
            jax.ShapeDtypeStruct((rows, width), bf16 if whole_group else f32),
            jax.ShapeDtypeStruct((width, STATE), f32),
        ],
        compiler_params=params(),
        name="gated_outputs",
    )(
        meta,
        y_local, conv_c, gate_input, dt_input, rate, norm_gain[None], gathered, sent,
        init_state.reshape(width, STATE), local,
    )
    boundary = boundary.reshape(1, heads, HEADDIM, STATE)

    if not whole_group:
        piece = min(width, group_width)
        pieces = normed.reshape(rows, width // piece, piece)
        squares = jnp.sum(pieces * pieces, axis=2).T
        blocks = squares.reshape(squares.shape[0], head_count, block)
        ordered = jnp.take(blocks, slot, axis=1).reshape(squares.shape)
        own = (head_index * (width // piece) + jnp.arange(width // piece)) * piece // group_width
        member = (own[:, None] == jnp.arange(GROUPS)[None, :]).astype(f32)
        totals = lax.psum(jnp.dot(member.T, ordered, precision=highest), "head")
        sums = jnp.dot(member, totals, precision=highest)
        inverse = lax.rsqrt(sums / group_width + norm_eps)
        back = jnp.zeros_like(slot).at[slot].set(jnp.arange(head_count, dtype=slot.dtype))
        inverse = jnp.take(inverse.reshape(blocks.shape), back, axis=1).reshape(squares.shape).T
        normed = (
            (pieces * inverse[:, :, None]).reshape(rows, width) * norm_gain[None, :]
        ).astype(bf16)

    chips = seq_count // 2

    def around(value, by):
        if by % chips == 0:
            return value
        return lax.ppermute(
            value, "seq", [(i, (i + 2 * by) % seq_count) for i in range(seq_count)]
        )

    def across(value, bit):
        return lax.ppermute(
            value, "head", [(i, i ^ (1 << bit)) for i in range(head_count)]
        )

    def reduced(act, weight):
        half = rows // 2
        give = jnp.dot(act[half:], weight, preferred_element_type=f32).astype(bf16)
        keep = jnp.dot(act[:half], weight, preferred_element_type=f32)
        keep = keep + across(give, 0).astype(f32)
        for bit in range(1, bits):
            half = half // 2
            got = across(keep[half:].astype(bf16), bit)
            keep = keep[:half] + got.astype(f32)
        return keep.astype(bf16)

    core = seq_index % 2
    columns = out_weight.shape[1]
    layer_out = jnp.zeros((block, seq_count, columns), bf16)
    acts = [around(normed, by) for by in range(chips)]
    done = [[reduced(act, w) for w in (out_weight, other_core)] for act in acts]
    for by in range(chips):
        mine, other = [around(d, -by) for d in done[by]]
        chip = (seq_index // 2 + by) % chips
        layer_out = lax.dynamic_update_slice(
            layer_out, mine[:, None], (0, chip * 2 + core, 0)
        )
        layer_out = lax.dynamic_update_slice(
            layer_out, other[:, None], (0, chip * 2 + 1 - core, 0)
        )
    return (layer_out.reshape(block, seq_count * columns), boundary)


def solution(mesh):
    in_specs = (
        P("seq", "head"),
        P("seq", "head"),
        P("seq", None),
        P("head", "seq"),
        P("head"),
        P("head"),
        P(None, "head"),
        P("head"),
        P(),
        P(),
        P(None, "head"),
        P(),
        P("head", None, None),
        P("head"),
        P("head", "seq"),
    )
    out_specs = (P(("seq", "head"), None), P("seq", "head", None, None))
    return jax.shard_map(body, mesh=mesh, in_specs=in_specs, out_specs=out_specs, check_vma=False)
```

```python
import functools

import jax
import jax.numpy as jnp
from jax import lax
from jax.experimental import pallas as pl
from jax.experimental.pallas import tpu as pltpu
from jax.sharding import PartitionSpec as P

MIXER_HEADS = 256
HEADDIM = 64
STATE = 256
GROUPS = 8
KERNEL = 4
SPAN = 128
DINNER = 16384
EXTRA = 16
VMEM_LIMIT = 48 * 1024 * 1024
LAYER_LIMIT = 62 * 1024 * 1024

highest = lax.Precision.HIGHEST
norm_eps = 1e-05
f32 = jnp.float32
bf16 = jnp.bfloat16
MESH = pl.DeviceIdType.MESH


def silu(v):
    return v * (1.0 / (1.0 + jnp.exp(-v)))


def shifted(cur, prev8, by):
    moved = pltpu.roll(cur, by, 0)
    before = pltpu.roll(prev8, by, 0)
    row = lax.broadcasted_iota(jnp.int32, before.shape, 0)
    first = jnp.where(row < by, before, moved[:8])
    return jnp.concatenate([first, moved[8:]], axis=0)


def conv_block(in_ref, prev_ref, w_ref, b_ref, out_ref, chunk):
    width = in_ref.shape[1]
    rows = in_ref.shape[0]
    for c in range(0, width, chunk):
        cols = slice(c, c + chunk)
        cur = in_ref[:, cols].astype(f32)
        prev8 = prev_ref[:, cols]
        total = b_ref[:, cols] + w_ref[KERNEL - 1 : KERNEL, cols] * cur
        for by in range(1, KERNEL):
            k = KERNEL - 1 - by
            total = total + w_ref[k : k + 1, cols] * shifted(cur, prev8, by)
        prev_ref[:, cols] = cur[rows - 8 :]
        out_ref[:, cols] = silu(total).astype(bf16)


def spread_matrix(heads):
    h = lax.broadcasted_iota(jnp.int32, (heads, heads * HEADDIM), 0)
    c = lax.broadcasted_iota(jnp.int32, (heads, heads * HEADDIM), 1)
    return jnp.where(c // HEADDIM == h, 1.0, 0.0).astype(f32)


def spread(values, matrix):
    return jnp.dot(values, matrix, precision=highest, preferred_element_type=f32)


def softplus(v):
    e = jnp.exp(-jnp.abs(v))
    u = 1.0 + e
    series = e * (1.0 - e * (0.5 - e * (1.0 / 3.0 - 0.25 * e)))
    return jnp.maximum(v, 0.0) + jnp.where(e < 0.015625, series, jnp.log(u))


def transposed_dot(lhs, rhs):
    return lax.dot_general(
        lhs, rhs, (((1,), (1,)), ((), ())), precision=highest, preferred_element_type=f32
    )


def decay_terms(dt_ref, rate_ref):
    step = softplus(dt_ref[...])
    log = -jnp.exp(rate_ref[...]) * step
    t = lax.broadcasted_iota(jnp.int32, (SPAN, SPAN), 0)
    s = lax.broadcasted_iota(jnp.int32, (SPAN, SPAN), 1)
    lower = jnp.where(t >= s, 1.0, 0.0).astype(f32)
    eye = jnp.where(t == s, 1.0, 0.0).astype(f32)
    cumul_row = transposed_dot(log, lower)
    cumul_col = transposed_dot(lower, log)
    step_col = transposed_dot(eye, step)
    return step, step_col, cumul_row, cumul_col, t >= s


def state_kernel(
    g_ref, inner, bin_, cin, dt, rate, wx, bx, wb, wc, bb, bc, halo_x, halo_b, halo_c,
    x_out, b_out, c_out, enter_out, send_out, local_out,
    prev_x, prev_b, prev_c, state, total,
):
    i = pl.program_id(0)
    heads = dt.shape[0]

    @pl.when(i == 0)
    def _():
        prev_x[...] = halo_x[...].astype(f32)
        prev_b[...] = halo_b[...].astype(f32)
        prev_c[...] = halo_c[...].astype(f32)
        state[...] = jnp.zeros_like(state)
        total[...] = jnp.zeros_like(total)

    conv_block(inner, prev_x, wx, bx, x_out, 256)
    conv_block(bin_, prev_b, wb, bb, b_out, 256)
    conv_block(cin, prev_c, wc, bc, c_out, 256)
    step, step_col, cumul_row, cumul_col, causal = decay_terms(dt, rate)
    last = cumul_col[SPAN - 1 :]
    matrix = spread_matrix(heads)
    weights = spread(jnp.exp(last - cumul_col) * step_col, matrix)
    last8 = spread(jnp.broadcast_to(last, (8, heads)), matrix)
    enter_out[0] = state[...].astype(bf16)
    weighted = (x_out[...].astype(f32) * weights).astype(bf16)
    b_t = b_out[...].astype(f32).T.astype(bf16)
    written = jnp.dot(b_t, weighted, preferred_element_type=f32)
    state[...] = jnp.exp(last8[:1]) * state[...] + written
    total[...] += last8

    @pl.when(i == pl.num_programs(0) - 1)
    def _():
        local_out[...] = state[...]
        send_out[:STATE] = state[...].astype(bf16)
        tl = total[:1]
        high = tl.astype(bf16).astype(f32)
        row = lax.broadcasted_iota(jnp.int32, (EXTRA, tl.shape[1]), 0)
        send_out[STATE:] = jnp.where(row == 0, high, jnp.where(row == 1, tl - high, 0.0)).astype(bf16)


PARTS = 4


def chain_kernel(
    x, b, c, dt, rate, skip, enter, local, sent, y_out, prior_out,
    land, hop, send_sem, recv_sem,
):
    i = pl.program_id(0)
    seq = lax.axis_index("seq")
    last = 3
    wide = land.shape[2]

    def copy(k):
        return pltpu.make_async_remote_copy(
            src_ref=hop.at[k], dst_ref=land.at[k],
            send_sem=send_sem.at[k], recv_sem=recv_sem.at[k],
            device_id={"seq": (seq + 1) % 4}, device_id_type=MESH,
        )

    def joined(k):
        cols = slice(k * wide, (k + 1) * wide)
        own = sent[STATE : STATE + 1, cols].astype(f32) + sent[STATE + 1 : STATE + 2, cols].astype(f32)
        tail = land[k, STATE:].astype(f32)
        hop[k, :STATE] = (
            jnp.exp(own) * land[k, :STATE].astype(f32) + local[:, cols]
        ).astype(bf16)
        log = tail[0:1] + tail[1:2] + own
        high = log.astype(bf16).astype(f32)
        row = lax.broadcasted_iota(jnp.int32, (EXTRA, wide), 0)
        hop[k, STATE:] = jnp.where(row == 0, high, jnp.where(row == 1, log - high, 0.0)).astype(bf16)

    @pl.when(i == 0)
    def _():
        barrier = pltpu.get_barrier_semaphore()

        for by in (1, 3):
            pl.semaphore_signal(
                barrier, inc=1, device_id={"seq": (seq + by) % 4}, device_id_type=MESH
            )
        pl.semaphore_wait(barrier, 2)

        @pl.when(seq == 0)
        def _():
            for k in range(PARTS):
                hop[k] = sent[:, k * wide : (k + 1) * wide]
                copy(k).start()

        @pl.when(seq == 1)
        def _():
            for k in range(PARTS):
                copy(k).wait_recv()
                joined(k)
                copy(k).start()

    local_kernel(x, b, c, dt, rate, skip, enter, y_out)

    @pl.when(i == pl.num_programs(0) - 1)
    def _():
        @pl.when(seq == 2)
        def _():
            for k in range(PARTS):
                copy(k).wait_recv()
                joined(k)
                copy(k).start()

        @pl.when(seq == 3)
        def _():
            for k in range(PARTS):
                copy(k).wait_recv()

        @pl.when(seq > 0)
        def _():
            for k in range(PARTS):
                prior_out[:, k * wide : (k + 1) * wide] = land[k]

        @pl.when(seq == 0)
        def _():
            prior_out[...] = jnp.zeros_like(prior_out)

        @pl.when(seq < last)
        def _():
            for k in range(PARTS):
                copy(k).wait_send()


def local_kernel(x, b, c, dt, rate, skip, enter, y_out):
    heads = dt.shape[0]
    step, step_col, cumul_row, cumul_col, causal = decay_terms(dt, rate)
    matrix = spread_matrix(heads)
    scores = lax.dot_general(
        c[...], b[...], (((1,), (1,)), ((), ())), preferred_element_type=f32
    )
    row_term = jnp.log(step) - cumul_row
    growth = spread(jnp.exp(cumul_col), matrix)
    skip_row = spread(jnp.broadcast_to(skip[...], (8, heads)), matrix)[:1]
    lane = lax.broadcasted_iota(jnp.int32, (SPAN, 2 * HEADDIM), 1)
    zero = jnp.zeros((SPAN, 2 * HEADDIM), bf16)
    for pair in range(heads // 2):
        cols = slice(pair * 2 * HEADDIM, (pair + 1) * 2 * HEADDIM)
        mixers = []
        for h in (2 * pair, 2 * pair + 1):
            power = jnp.where(causal, cumul_col[:, h : h + 1] + row_term[h : h + 1], -1e30)
            mixers.append((scores * jnp.exp(power)).astype(bf16))
        xp = x[:, cols]
        both = jnp.concatenate(
            [jnp.where(lane < HEADDIM, xp, zero), jnp.where(lane >= HEADDIM, xp, zero)], axis=0
        )
        inside = jnp.dot(
            jnp.concatenate(mixers, axis=1), both, preferred_element_type=f32
        )
        carried = jnp.dot(c[...], enter[0, :, cols], preferred_element_type=f32)
        y_out[:, cols] = (
            inside + growth[:, cols] * carried + skip_row[:, cols] * xp.astype(f32)
        )


def output_kernel(
    meta, y, c, gate, dt, rate, gain, gathered, own_tail, init, local, normed_out, boundary_out,
    incoming, entering, mixed, offset, *, block, halves, whole_group, chained,
):
    i = pl.program_id(0)
    heads = dt.shape[0]
    width = y.shape[1]
    count = gathered.shape[0]

    @pl.when(i == 0)
    def _():
        place = meta[0]
        rate_sum = jnp.zeros((1, width), f32)
        incoming[...] = jnp.zeros_like(incoming)
        if chained:
            tail = gathered[0, STATE:].astype(f32)
            incoming[...] = gathered[0, :STATE].astype(f32)
            rate_sum = tail[0:1] + tail[1:2]
        for k in range(-1 if chained else count - 2, -1, -1):
            live = k < place
            tail = gathered[k, STATE:].astype(f32)
            factor = jnp.where(live, jnp.exp(rate_sum), 0.0)
            incoming[...] += factor * gathered[k, :STATE].astype(f32)
            rate_sum = rate_sum + jnp.where(live, tail[0:1] + tail[1:2], 0.0)
        tail = (own_tail[...] if chained else gathered[place, STATE:]).astype(f32)
        own = jnp.exp(tail[0:1] + tail[1:2])
        for k in range(0, width, 256):
            cols = slice(k, k + 256)
            value = incoming[:, cols] + jnp.exp(rate_sum[:, cols]) * init[cols, :].T
            entering[:, cols] = value.astype(bf16)
            boundary_out[cols, :] = (own[:, cols] * value + local[:, cols]).T
        offset[...] = jnp.zeros_like(offset)

    step, step_col, cumul_row, cumul_col, causal = decay_terms(dt, rate)
    cumul_col = cumul_col + offset[:1]
    offset[...] = jnp.broadcast_to(cumul_col[SPAN - 1 :], offset.shape)
    growth = spread(jnp.exp(cumul_col), spread_matrix(heads))
    squares = jnp.zeros((SPAN, 1), f32)
    for k in range(0, width, 256):
        cols = slice(k, k + 256)
        carried = jnp.dot(c[...], entering[:, cols], preferred_element_type=f32)
        value = (y[:, cols] + growth[:, cols] * carried) * silu(gate[:, cols].astype(f32))
        mixed[:, cols] = value
        squares = squares + jnp.sum(value * value, axis=1, keepdims=True)
    if whole_group:
        inverse = lax.rsqrt(squares / width + norm_eps)
    piece = block // halves
    for q in range(SPAN // piece):
        rows = slice(q * piece, (q + 1) * piece)
        first = meta[1 + i * (SPAN // block) + q // halves]
        first = first + (q % halves) * (normed_out.shape[0] // halves)
        value = mixed[rows, :]
        if whole_group:
            value = value * inverse[rows] * gain[...]
        normed_out[pl.ds(pl.multiple_of(first, piece), piece), :] = value.astype(normed_out.dtype)


def partner_of(place, bit):
    size = 1 << bit
    return place + (1 - 2 * ((place // size) % 2)) * size


HALVES = 2
QUARTERS = 4
WIDES = 3
NARROWS = 4
NARROW = 256
ARRIVED = 8
WIDE_Z = (2, 3, 7)
NARROW_Z = (1, 3, 7)
ORDER = (
    130, 131, 1, 129, 2, 5, 33, 3, 34, 163, 0, 161, 37, 65, 66, 4, 32, 256,
    162, 6, 193, 7, 195, 8, 69, 36, 128, 64, 39, 97, 38, 194, 68, 257, 132, 40,
    70, 96, 11, 135, 226, 160, 72, 225, 227, 9, 10, 164, 134, 71, 43, 196, 133, 104,
    192, 41, 167, 75, 228, 98, 35, 42, 103, 73, 224, 166, 74, 102, 100, 107, 165, 101,
    198, 199, 105, 197, 106, 230, 67, 231, 229, 99,
)


def tanh_silu(v):
    half = 0.5 * v
    return half + half * jnp.tanh(half)


def two_terms(values):
    high = values.astype(bf16)
    low = (values - high.astype(f32)).astype(bf16)
    return jnp.concatenate([high, low], axis=1)


def fill_matrix(matrix):
    heads = matrix.shape[0] // 2
    h = lax.broadcasted_iota(jnp.int32, matrix.shape, 0) % heads
    c = lax.broadcasted_iota(jnp.int32, matrix.shape, 1) // HEADDIM
    matrix[...] = jnp.where(c == h, 1.0, 0.0).astype(bf16)


def token_decays(dt, rate):
    step = softplus(dt).T
    log = -jnp.exp(rate) * step
    t = lax.broadcasted_iota(jnp.int32, (SPAN, SPAN), 0)
    s = lax.broadcasted_iota(jnp.int32, (SPAN, SPAN), 1)
    lower = jnp.where(t >= s, 1.0, 0.0).astype(f32)
    cumul = [
        jnp.dot(lower, log[k : k + SPAN], precision=highest, preferred_element_type=f32)
        for k in range(0, log.shape[0], SPAN)
    ]
    return step, cumul, t >= s


def conv_tile(cur, prev8, weight, bias):
    total = bias + weight[KERNEL - 1 : KERNEL] * cur
    for by in range(1, KERNEL):
        k = KERNEL - 1 - by
        total = total + weight[k : k + 1] * shifted(cur, prev8, by)
    return tanh_silu(total).astype(bf16)


def layer_kernel(
    inner, gate_all, bc_all, dt, rate, skip, wx, bx, wbc, bbc, tail_x, tail_bc, init_all, gain, w_own,
    out, state_out,
    x, gate, bc, halo_x, halo_bc, prev, b_t, weight, factors, matrix, scaled, total, state,
    land, hop, left, squares, w, w_last, acts,
    keep, y_send, y_recv, a_send, a_recv, b_send, b_recv, out_held, x_send, x_recv,
    n_keep, ny_send, ny_recv, na_send, na_recv, nb_send, nb_recv, n_held, nx_send, nx_recv,
    in_sem, load_sem, init_sem, halo_send, halo_recv, hop_send, hop_recv, w_sem, w_send, w_recv,
    act_send_sem, act_recv_sem,
    send_sem, recv_sem, out_sem, x_send_sem, x_recv_sem,
    n_send_sem, n_recv_sem, n_out_sem, nx_send_sem, nx_recv_sem,
):
    seq = lax.axis_index("seq")
    head = lax.axis_index("head")
    rows, width = x.shape
    heads = dt.shape[0]
    spans = rows // SPAN
    strip = width // QUARTERS
    wide = w.shape[2]
    columns = w_own.shape[1]
    piece = out.shape[0] // HALVES
    wides = keep.shape[0] // 2
    narrows = n_keep.shape[0] // 2
    other_chip = (seq + 2) % 4
    near = [partner_of(head, bit) for bit in range(3)]
    across = [{"head": place} for place in near]
    over_x = {"seq": other_chip}
    after = {"seq": (seq + 1) % 4}
    other_core = {"seq": partner_of(seq, 0)}
    firsts = [pl.multiple_of((head + g) * STATE, STATE) for g in (0, GROUPS)]
    chunk = 256

    def remote(source, dest, send, recv, target):
        return pltpu.make_async_remote_copy(
            src_ref=source, dst_ref=dest, send_sem=send, recv_sem=recv,
            device_id=target, device_id_type=MESH,
        )

    def strip_of(k):
        return pl.ds(pl.multiple_of(k * strip, strip), strip)

    def inner_copy(k):
        cols = slice(k * strip, (k + 1) * strip)
        return pltpu.make_async_copy(inner.at[:, cols], x.at[:, cols], in_sem.at[k])

    def bc_copy(k):
        return pltpu.make_async_copy(
            bc_all.at[:, pl.ds(firsts[k], STATE)], bc.at[k], load_sem.at[k]
        )

    def gate_copy():
        return pltpu.make_async_copy(gate_all, gate, load_sem.at[2])

    def init_copies():
        place = [(k, r) for k in range(QUARTERS) for r in range(strip // SPAN)]
        return [
            pltpu.make_async_copy(
                init_all.at[k * strip + r * SPAN : k * strip + (r + 1) * SPAN],
                keep.at[k, 0, :, r * STATE : (r + 1) * STATE],
                init_sem.at[k, r],
            )
            for k, r in place
        ]

    def state_copy():
        return pltpu.make_async_copy(state, state_out, load_sem.at[3])

    def own_first():
        return pltpu.make_async_copy(w_own.at[:, :wide], w.at[0], w_sem.at[0])

    def own_second():
        return pltpu.make_async_copy(w_own.at[:, wide:], w_last, w_sem.at[1])

    def other_weights(k):
        narrow = wide // 2
        place = slice(k % 2 * narrow, (k % 2 + 1) * narrow)
        source = w.at[0, :, place] if k < 2 else w_last.at[:, place]
        return remote(
            source, w.at[1 + k // 2, :, place], w_send.at[k], w_recv.at[k], other_core
        )

    def halo_copies():
        last = pl.ds(rows - 16, 16)
        pairs = [(inner.at[last], halo_x)] + [
            (bc_all.at[last, pl.ds(firsts[k], STATE)], halo_bc.at[k]) for k in range(2)
        ]
        return [
            remote(source, dest, halo_send.at[k], halo_recv.at[k], after)
            for k, (source, dest) in enumerate(pairs)
        ]

    def hop_copy(k):
        return remote(hop.at[k], land.at[k], hop_send.at[k], hop_recv.at[k], after)

    def act_copy(half):
        return remote(
            acts.at[0, half], acts.at[1, half], act_send_sem.at[half], act_recv_sem.at[half], over_x
        )

    def chip_copy(k):
        return remote(x_send.at[k], x_recv.at[k], x_send_sem.at[k], x_recv_sem.at[k], over_x)

    def chip_copy_narrow(k):
        return remote(nx_send.at[k], nx_recv.at[k], nx_send_sem.at[k], nx_recv_sem.at[k], over_x)

    def chosen(t, those):
        value = 0
        for k in those:
            value = value + jnp.where(t == k, 1, 0)
        return value

    broad = (
        keep, ((y_send, y_recv), (a_send, a_recv), (b_send, b_recv)), send_sem, recv_sem, WIDE_Z
    )
    slim = (
        n_keep, ((ny_send, ny_recv), (na_send, na_recv), (nb_send, nb_recv)),
        n_send_sem, n_recv_sem, NARROW_Z,
    )

    def head_copy(family, stage, t):
        _, buffers, sent, received, those = family
        source, dest = buffers[stage]
        target = across[2]
        if stage < 2:
            target = {"head": near[stage] + chosen(t, those) * (near[1 - stage] - near[stage])}
        return remote(source.at[t], dest.at[t], sent.at[stage, t], received.at[stage, t], target)

    for k in range(2):
        bc_copy(k).start()
    for k in range(QUARTERS):
        inner_copy(k).start()

    barrier = pltpu.get_barrier_semaphore()
    greeted = across + [over_x, after, {"seq": (seq + 3) % 4}]
    for target in greeted:
        pl.semaphore_signal(barrier, inc=1, device_id=target, device_id_type=MESH)

    own_first().start()
    own_second().start()
    for copy in init_copies():
        copy.start()
    gate_copy().start()

    fill_matrix(matrix)
    step, cumul, causal = token_decays(dt[...], rate[...])
    ends = [value[SPAN - 1 :] for value in cumul]
    later = jnp.zeros_like(ends[0])
    for k in range(spans - 1, -1, -1):
        span = slice(k * SPAN, (k + 1) * SPAN)
        later = later + ends[k]
        weight[span] = two_terms(jnp.exp(later - cumul[k]) * step[span])
    row = lax.broadcasted_iota(jnp.int32, (16, heads), 0)
    high = later.astype(bf16).astype(f32)
    total[...] = two_terms(jnp.where(row < 8, high, later - high))

    pl.semaphore_wait(barrier, len(greeted))

    @pl.when(seq < 3)
    def _():
        for copy in halo_copies():
            copy.start()

    def conv_rows(source, k, cols, before, kernel, bias):
        span = slice(k * SPAN, (k + 1) * SPAN)
        if k:
            before = source[k * SPAN - 16 : k * SPAN, cols].astype(f32)[8:]
        value = conv_tile(source[span, cols].astype(f32), before, kernel, bias)
        source[span, cols] = value
        return value

    def conv_bc(g, k):
        at = pl.ds(firsts[g], STATE)
        before = None if k else prev[:, strip + g * STATE : strip + (g + 1) * STATE]
        return conv_rows(bc.at[g], k, slice(0, STATE), before, wbc[:, at], bbc[:, at])

    def conv_b(k):
        value = conv_bc(0, k)
        b_t[:, k * SPAN : (k + 1) * SPAN] = value.astype(f32).T.astype(bf16)

    for k in range(2):
        bc_copy(k).wait()
    for k in range(spans - 1, 0, -1):
        conv_b(k)

    @pl.when(seq > 0)
    def _():
        for copy in halo_copies():
            copy.wait_recv()
        for g in range(2):
            prev[:, strip + g * STATE : strip + (g + 1) * STATE] = halo_bc[g].astype(f32)[8:]

    @pl.when(seq == 0)
    def _():
        for g in range(2):
            prev[8 - KERNEL + 1 :, strip + g * STATE : strip + (g + 1) * STATE] = tail_bc[
                :, pl.ds(firsts[g], STATE)
            ].astype(f32)
        land[...] = jnp.zeros_like(land)

    conv_b(0)

    def totals(k):
        spread_log = jnp.dot(total[...], matrix[:, strip_of(k)], preferred_element_type=f32)
        return spread_log[0:1] + spread_log[8:9]

    def fill_hop(k, value, log):
        hop[k, :STATE] = value.astype(bf16)
        top = log.astype(bf16).astype(f32)
        line = lax.broadcasted_iota(jnp.int32, (EXTRA, strip), 0)
        hop[k, STATE:] = jnp.where(line == 0, top, jnp.where(line == 1, log - top, 0.0)).astype(bf16)
        hop_copy(k).start()

    def pass_on(k):
        hop_copy(k).wait_recv()
        own = totals(k)
        tail = land[k, STATE:].astype(f32)
        fill_hop(
            k,
            jnp.exp(own) * land[k, :STATE].astype(f32) + state[:, strip_of(k)],
            tail[0:1] + tail[1:2] + own,
        )

    for k in range(QUARTERS):
        inner_copy(k).wait()

    def quarter(q, carry):
        @pl.when(seq > 0)
        def _():
            prev[:, :strip] = halo_x[:, strip_of(q)].astype(f32)[8:]

        @pl.when(seq == 0)
        def _():
            prev[8 - KERNEL + 1 :, :strip] = tail_x[:, strip_of(q)].astype(f32)

        for k in range(spans - 1, -1, -1):
            span = slice(k * SPAN, (k + 1) * SPAN)
            for c in range(0, strip, chunk):
                at = pl.ds(pl.multiple_of(q * strip + c, chunk), chunk)
                value = conv_rows(x, k, at, prev[:, c : c + chunk], wx[:, at], bx[:, at])
                factor = jnp.dot(weight[span], matrix[:, at], preferred_element_type=f32)
                scaled[span, c : c + chunk] = (value.astype(f32) * factor).astype(bf16)
        state[:, strip_of(q)] = jnp.dot(b_t[...], scaled[...], preferred_element_type=f32)

        @pl.when(seq == 0)
        def _():
            fill_hop(q, state[:, strip_of(q)], totals(q))

        @pl.when((seq == 1) & (q > 0))
        def _():
            pass_on(q - 1)

        @pl.when(q == 0)
        def _():
            own_first().wait()

        @pl.when(q == 2)
        def _():
            own_second().wait()

        for k in range(QUARTERS):
            @pl.when(q == k)
            def _():
                other_weights(k).start()

        return carry

    lax.fori_loop(0, QUARTERS, quarter, 0)

    @pl.when(seq == 1)
    def _():
        pass_on(QUARTERS - 1)

    for k in range(spans - 1, -1, -1):
        conv_bc(1, k)

    for k in range(spans):
        middle = 0.5 * ends[k]
        factors[k] = two_terms(
            jnp.concatenate(
                [
                    jnp.exp(cumul[k] - middle),
                    jnp.exp(middle - cumul[k]) * step[k * SPAN : (k + 1) * SPAN],
                    jnp.broadcast_to(jnp.exp(middle), (8, heads)),
                    jnp.broadcast_to(skip[...], (8, heads)),
                ],
                axis=0,
            )
        )

    for i in range(spans):
        span = slice(i * SPAN, (i + 1) * SPAN)
        scores = lax.dot_general(
            bc[1, span], bc[0, span], (((1,), (1,)), ((), ())), preferred_element_type=f32
        )
        left[i, :, :SPAN] = jnp.where(causal, scores, 0.0).astype(bf16)
        left[i, :, SPAN:] = bc[1, span]
    squares[...] = jnp.zeros_like(squares)
    for copy in init_copies():
        copy.wait()
    gate_copy().wait()

    def gated(q, carry):
        @pl.when(seq == 2)
        def _():
            pass_on(q)

        @pl.when(seq == 3)
        def _():
            hop_copy(q).wait_recv()

        tail = land[q, STATE:].astype(f32)
        factor = jnp.exp(tail[0:1] + tail[1:2])
        for r in range(strip // SPAN):
            lanes = slice(r * SPAN, (r + 1) * SPAN)
            at = pl.ds(pl.multiple_of(q * strip + r * SPAN, SPAN), SPAN)
            state[:, at] = (
                land[q, :STATE, lanes].astype(f32)
                + factor[:, lanes] * keep[q, 0, :, r * STATE : (r + 1) * STATE].T
            )
        cols = strip_of(q)
        spot = pl.ds(pl.multiple_of(q % 2 * strip, strip), strip)
        for i in range(spans):
            span = slice(i * SPAN, (i + 1) * SPAN)
            spread_all = jnp.dot(factors[i], matrix[:, cols], preferred_element_type=f32)
            half_decay = spread_all[2 * SPAN : 2 * SPAN + 1]
            value = x[span, cols].astype(f32)
            weighted = (value * spread_all[SPAN : 2 * SPAN]).astype(bf16)
            before = half_decay * state[:, cols]
            inside = jnp.dot(
                left[i], jnp.concatenate([weighted, before.astype(bf16)], axis=0),
                preferred_element_type=f32,
            )
            written = jnp.dot(b_t[:, span], weighted, preferred_element_type=f32)
            state[:, cols] = half_decay * (before + written)
            value = spread_all[:SPAN] * inside + spread_all[2 * SPAN + 8 : 2 * SPAN + 9] * value
            value = value * tanh_silu(gate[span, cols].astype(f32))
            keep[QUARTERS + 2 * i + q // 2, 0, :, spot] = value
            square = value * value
            for c in range(0, strip, 128):
                squares[i] = squares[i] + square[:, c : c + 128]
        return carry

    lax.fori_loop(0, QUARTERS, gated, 0)

    def normalized(half):
        block = HALVES * piece
        for i in range(spans):
            for p in range(SPAN // block):
                first = p * block + half * piece
                lines = slice(first, first + piece)
                inverse = lax.rsqrt(
                    jnp.sum(squares[i, lines], axis=1, keepdims=True) / width + norm_eps
                )
                owner = i * (SPAN // block) + p
                slot = 0
                for bit in range(3):
                    differs = (owner // (1 << bit) + head // (1 << bit)) % 2
                    slot = slot + differs * (4 >> bit)
                place = pl.ds(pl.multiple_of(slot * piece, piece), piece)
                for c in range(width // wide):
                    cols = slice(c * wide, (c + 1) * wide)
                    acts[0, half, place, cols] = (
                        keep[QUARTERS + 2 * i + c, 0, lines, :] * inverse * gain[:, cols]
                    ).astype(bf16)

    for half in range(HALVES):
        normalized(half)
        act_copy(half).start()
    state_copy().start()

    two = 2 * piece

    def send_product(family, t, product):
        held, buffers, _, _, those = family
        near_z = chosen(t, those) == 1
        sending = buffers[0][0]
        middle = [product[:, two : 2 * two], product[:, 2 * two : 3 * two]]
        sending[t, :, :two] = jnp.where(near_z, middle[0], middle[1]).astype(bf16)
        sending[t, :, two:] = product[:, 3 * two :].astype(bf16)
        head_copy(family, 0, t).start()
        held[t, :, :two] = product[:, :two]
        held[t, :, two:] = jnp.where(near_z, middle[1], middle[0])

    def first_stage(family, t):
        held, buffers = family[:2]
        arrived, sending = buffers[0][1], buffers[1][0]
        head_copy(family, 0, t).wait_recv()
        sending[t] = (held[t, :, two:] + arrived[t, :, two:].astype(f32)).astype(bf16)
        head_copy(family, 1, t).start()
        held[t, :, :two] = held[t, :, :two] + arrived[t, :, :two].astype(f32)

    def second_stage(family, t):
        held, buffers = family[:2]
        arrived, sending = buffers[1][1], buffers[2][0]
        head_copy(family, 1, t).wait_recv()
        sending[t] = (held[t, :, piece:two] + arrived[t, :, piece:].astype(f32)).astype(bf16)
        head_copy(family, 2, t).start()
        held[t, :, :piece] = held[t, :, :piece] + arrived[t, :, :piece].astype(f32)

    def third_stage(family, t):
        held, buffers = family[:2]
        head_copy(family, 2, t).wait_recv()
        return (held[t, :, :piece] + buffers[2][1][t].astype(f32)).astype(bf16)

    def wide_out(source, slot, home, t):
        group, half = t % WIDES, (t % wides) // WIDES
        partner = partner_of(home, 0)
        column = jnp.where(group == 0, home, partner) * columns + (group // 2) * wide
        place = pl.ds(pl.multiple_of(half * piece, piece), piece)
        return pltpu.make_async_copy(
            source.at[t], out.at[place, pl.ds(pl.multiple_of(column, wide), wide)], out_sem.at[slot]
        )

    def narrow_out(source, slot, home, t):
        column = home * columns + wide + t * NARROW
        return pltpu.make_async_copy(
            source.at[t], out.at[:, pl.ds(pl.multiple_of(column, NARROW), NARROW)],
            n_out_sem.at[slot],
        )

    def wide_multiply(t):
        place, half, group = t // wides, (t % wides) // WIDES, t % WIDES
        product = jnp.dot(acts[place, half], w[group], preferred_element_type=f32)
        send_product(broad, t, product[None])

    def narrow_multiply(t):
        lines = acts[t // NARROWS].reshape(rows, width)
        cols = pl.ds(pl.multiple_of(t % NARROWS * NARROW, NARROW), NARROW)
        product = jnp.dot(lines, w_last[:, cols], preferred_element_type=f32)
        send_product(slim, t, product.reshape(HALVES, rows // HALVES, NARROW))

    def wide_third(t):
        value = third_stage(broad, t)[0]

        @pl.when(t < wides)
        def _():
            out_held[t] = value
            wide_out(out_held, t, seq, t).start()

        @pl.when(t >= wides)
        def _():
            x_send[t - wides] = value
            chip_copy(t - wides).start()

    def narrow_third(t):
        value = third_stage(slim, t)

        @pl.when(t < NARROWS)
        def _():
            for half in range(HALVES):
                n_held[t, half * piece : (half + 1) * piece] = value[half]
            narrow_out(n_held, t, seq, t).start()

        @pl.when(t >= NARROWS)
        def _():
            for half in range(HALVES):
                nx_send[t - NARROWS, half * piece : (half + 1) * piece] = value[half]
            chip_copy_narrow(t - NARROWS).start()

    handlers = [
        wide_multiply,
        lambda t: first_stage(broad, t),
        lambda t: second_stage(broad, t),
        wide_third,
        narrow_multiply,
        lambda t: first_stage(slim, t),
        lambda t: second_stage(slim, t),
        narrow_third,
        lambda t: act_copy(t).wait_recv(),
    ]
    words = [
        sum(code << (9 * j) for j, code in enumerate(ORDER[k : k + 3]))
        for k in range(0, len(ORDER), 3)
    ]

    def event(i, carry):
        word = 0
        for k, value in enumerate(words):
            word = word + jnp.where(i // 3 == k, value, 0)
        low, mid, top = word % 512, word // 512 % 512, word // 262144
        code = jnp.where(i % 3 == 0, low, jnp.where(i % 3 == 1, mid, top))
        kind, t = code // 32, code % 32
        for k, handler in enumerate(handlers):
            @pl.when(kind == k)
            def _():
                handler(t)

        return carry

    for k in range(QUARTERS):
        other_weights(k).wait_recv()
    lax.fori_loop(0, len(ORDER), event, 0)

    def collect(k, carry):
        chip_copy(k).wait_recv()
        wide_out(x_recv, wides + k, other_chip, k).start()
        return carry

    def collect_narrow(k, carry):
        chip_copy_narrow(k).wait_recv()
        narrow_out(nx_recv, NARROWS + k, other_chip, k).start()
        return carry

    lax.fori_loop(0, wides, collect, 0)
    lax.fori_loop(0, NARROWS, collect_narrow, 0)

    for half in range(HALVES):
        act_copy(half).wait_send()
    for k in range(QUARTERS):
        other_weights(k).wait_send()
    state_copy().wait()

    @pl.when(seq < 3)
    def _():
        for k in range(QUARTERS):
            hop_copy(k).wait_send()
        for copy in halo_copies():
            copy.wait_send()

    def drain(t, carry):
        for stage in range(3):
            head_copy(broad, stage, t).wait_send()
        return carry

    def drain_narrow(t, carry):
        for stage in range(3):
            head_copy(slim, stage, t).wait_send()
        return carry

    def drain_out(k, carry):
        wide_out(out_held, k, seq, k).wait()
        wide_out(x_recv, wides + k, other_chip, k).wait()
        chip_copy(k).wait_send()
        return carry

    def drain_narrow_out(k, carry):
        narrow_out(n_held, k, seq, k).wait()
        narrow_out(nx_recv, NARROWS + k, other_chip, k).wait()
        chip_copy_narrow(k).wait_send()
        return carry

    lax.fori_loop(0, 2 * wides, drain, 0)
    lax.fori_loop(0, 2 * NARROWS, drain_narrow, 0)
    lax.fori_loop(0, wides, drain_out, 0)
    lax.fori_loop(0, NARROWS, drain_narrow_out, 0)


FINISH = 4


def finish_kernel(summed, state, out, boundary_out, sums, columns, rows, sem):
    wide, strip = sums.shape[1] // FINISH, columns.shape[1] // FINISH

    def part(k, step):
        return slice(k * step, (k + 1) * step)

    def copies(k):
        return [
            pltpu.make_async_copy(state.at[:, part(k, strip)], columns.at[:, part(k, strip)], sem.at[0, k]),
            pltpu.make_async_copy(summed.at[:, part(k, wide)], sums.at[:, part(k, wide)], sem.at[1, k]),
            pltpu.make_async_copy(rows.at[part(k, strip)], boundary_out.at[part(k, strip)], sem.at[2, k]),
            pltpu.make_async_copy(sums.at[:, part(k, wide)], out.at[:, part(k, wide)], sem.at[3, k]),
        ]

    for k in range(FINISH):
        for copy in copies(k)[:2]:
            copy.start()
    for k in range(FINISH):
        state_in, sum_in, state_back, sum_back = copies(k)
        state_in.wait()
        rows[part(k, strip)] = columns[:, part(k, strip)].T
        state_back.start()
        sum_in.wait()
        sum_back.start()
    for k in range(FINISH):
        for copy in copies(k)[2:]:
            copy.wait()


def layer(inner, gate, bc, dt, rate, skip, wx, bx, wbc, bbc, tail_x, tail_bc, init, gain, own):
    rows, width = inner.shape
    heads = dt.shape[0]
    columns = own.shape[1]
    strip = width // QUARTERS
    block = rows // 8
    piece = block // HALVES
    wide = columns // 2
    wides = HALVES * WIDES
    half_rows = rows // HALVES
    spans = rows // SPAN
    anywhere = pl.BlockSpec(memory_space=pl.ANY)
    vmem = pl.BlockSpec(memory_space=pltpu.VMEM)
    slots = (QUARTERS, STATE + EXTRA, strip)
    dma = pltpu.SemaphoreType.DMA
    summed, state = pl.pallas_call(
        layer_kernel,
        in_specs=[anywhere] * 3 + [vmem] * 9 + [anywhere, vmem, anywhere],
        out_specs=[anywhere, anywhere],
        out_shape=[
            jax.ShapeDtypeStruct((block, 4 * columns), bf16),
            jax.ShapeDtypeStruct((STATE, width), f32),
        ],
        scratch_shapes=[
            pltpu.VMEM((rows, width), bf16),
            pltpu.VMEM((rows, width), bf16),
            pltpu.VMEM((2, rows, STATE), bf16),
            pltpu.VMEM((16, width), bf16),
            pltpu.VMEM((2, 16, STATE), bf16),
            pltpu.VMEM((8, strip + 2 * STATE), f32),
            pltpu.VMEM((STATE, rows), bf16),
            pltpu.VMEM((rows, 2 * heads), bf16),
            pltpu.VMEM((spans, 2 * SPAN + 16, 2 * heads), bf16),
            pltpu.VMEM((2 * heads, width), bf16),
            pltpu.VMEM((rows, strip), bf16),
            pltpu.VMEM((16, 2 * heads), bf16),
            pltpu.VMEM((STATE, width), f32),
            pltpu.VMEM(slots, bf16),
            pltpu.VMEM(slots, bf16),
            pltpu.VMEM((spans, SPAN, SPAN + STATE), bf16),
            pltpu.VMEM((spans, SPAN, 128), f32),
            pltpu.VMEM((WIDES, width, wide), bf16),
            pltpu.VMEM((width, wide), bf16),
            pltpu.VMEM((2, HALVES, half_rows, width), bf16),
            pltpu.VMEM((2 * wides, 1, 4 * piece, wide), f32),
            pltpu.VMEM((2 * wides, 1, 4 * piece, wide), bf16),
            pltpu.VMEM((2 * wides, 1, 4 * piece, wide), bf16),
            pltpu.VMEM((2 * wides, 1, 2 * piece, wide), bf16),
            pltpu.VMEM((2 * wides, 1, 2 * piece, wide), bf16),
            pltpu.VMEM((2 * wides, 1, piece, wide), bf16),
            pltpu.VMEM((2 * wides, 1, piece, wide), bf16),
            pltpu.VMEM((wides, piece, wide), bf16),
            pltpu.VMEM((wides, piece, wide), bf16),
            pltpu.VMEM((wides, piece, wide), bf16),
            pltpu.VMEM((2 * NARROWS, HALVES, 4 * piece, NARROW), f32),
            pltpu.VMEM((2 * NARROWS, HALVES, 4 * piece, NARROW), bf16),
            pltpu.VMEM((2 * NARROWS, HALVES, 4 * piece, NARROW), bf16),
            pltpu.VMEM((2 * NARROWS, HALVES, 2 * piece, NARROW), bf16),
            pltpu.VMEM((2 * NARROWS, HALVES, 2 * piece, NARROW), bf16),
            pltpu.VMEM((2 * NARROWS, HALVES, piece, NARROW), bf16),
            pltpu.VMEM((2 * NARROWS, HALVES, piece, NARROW), bf16),
            pltpu.VMEM((NARROWS, block, NARROW), bf16),
            pltpu.VMEM((NARROWS, block, NARROW), bf16),
            pltpu.VMEM((NARROWS, block, NARROW), bf16),
            dma((QUARTERS,)),
            dma((4,)),
            dma((QUARTERS, strip // SPAN)),
            dma((3,)),
            dma((3,)),
            dma((QUARTERS,)),
            dma((QUARTERS,)),
            dma((2,)),
            dma((QUARTERS,)),
            dma((QUARTERS,)),
            dma((HALVES,)),
            dma((HALVES,)),
            dma((3, 2 * wides)),
            dma((3, 2 * wides)),
            dma((2 * wides,)),
            dma((wides,)),
            dma((wides,)),
            dma((3, 2 * NARROWS)),
            dma((3, 2 * NARROWS)),
            dma((2 * NARROWS,)),
            dma((NARROWS,)),
            dma((NARROWS,)),
        ],
        compiler_params=pltpu.CompilerParams(
            vmem_limit_bytes=LAYER_LIMIT, collective_id=0, has_side_effects=True
        ),
        name="layer",
    )(
        inner, gate, bc, dt, rate[None], skip[None], wx, bx[None], wbc, bbc[None], tail_x, tail_bc,
        init.reshape(width, STATE), gain[None], own,
    )
    return pl.pallas_call(
        finish_kernel,
        in_specs=[anywhere, anywhere],
        out_specs=[anywhere, anywhere],
        out_shape=[
            jax.ShapeDtypeStruct((block, 4 * columns), bf16),
            jax.ShapeDtypeStruct((width, STATE), f32),
        ],
        scratch_shapes=[
            pltpu.VMEM((block, 4 * columns), bf16),
            pltpu.VMEM((STATE, width), f32),
            pltpu.VMEM((width, STATE), f32),
            dma((4, FINISH)),
        ],
        compiler_params=pltpu.CompilerParams(vmem_limit_bytes=LAYER_LIMIT),
        name="finish",
    )(summed, state)


def params():
    return pltpu.CompilerParams(vmem_limit_bytes=VMEM_LIMIT)


def body(
    inner_input,
    gate_input,
    bc_input,
    dt_input,
    log_rate,
    skip_weight,
    conv_weight_x,
    conv_bias_x,
    conv_weight_bc,
    conv_bias_bc,
    conv_tail_x,
    conv_tail_bc,
    init_state,
    norm_gain,
    out_weight,
):
    seq_count = lax.axis_size("seq")
    head_count = lax.axis_size("head")
    seq_index = lax.axis_index("seq")
    head_index = lax.axis_index("head")
    rows, width = inner_input.shape
    heads = dt_input.shape[0]
    per_group = MIXER_HEADS // GROUPS
    group = (head_index * heads // per_group).astype(jnp.int32)
    spans = rows // SPAN
    block = rows // head_count
    group_width = DINNER // GROUPS
    whole_group = width == group_width

    projected = (
        seq_count == 4 and head_count == 8 and whole_group and rows == 512 and width == 2048
        and out_weight.shape[1] % 512 == 0
    )
    if projected:
        out, boundary = layer(
            inner_input, gate_input, bc_input, dt_input, log_rate, skip_weight, conv_weight_x,
            conv_bias_x, conv_weight_bc, conv_bias_bc, conv_tail_x, conv_tail_bc, init_state,
            norm_gain, out_weight,
        )
        return (out, boundary.reshape(1, heads, HEADDIM, STATE))

    other_core = lax.ppermute(out_weight, "seq", [(i, i ^ 1) for i in range(seq_count)])

    def pair_columns(table, axis):
        return [
            lax.dynamic_slice_in_dim(table, (g + group) * STATE, STATE, axis) for g in (0, GROUPS)
        ]

    tail_rows = rows - KERNEL + 1
    last_rows = jnp.concatenate(
        [inner_input[tail_rows:]] + pair_columns(bc_input[tail_rows:], 1), axis=1
    )
    arrived = lax.ppermute(last_rows, "seq", [(i, i + 1) for i in range(seq_count - 1)])
    first_rows = jnp.concatenate([conv_tail_x] + pair_columns(conv_tail_bc, 1), axis=1)
    halo = jnp.where(seq_index == 0, first_rows, arrived)
    halo = jnp.pad(halo, ((8 - KERNEL + 1, 0), (0, 0)))
    rate = log_rate[:, None]

    def const(shape, *index):
        return pl.BlockSpec(shape, lambda i, *_: index)

    span_x = pl.BlockSpec((SPAN, width), lambda i, *_: (i, 0))
    span_bc = pl.BlockSpec((SPAN, STATE), lambda i, *_: (i, 0))
    span_dt = pl.BlockSpec((heads, SPAN), lambda i, *_: (0, i))

    conv_x, conv_b, conv_c, enter, sent, local = pl.pallas_call(
        state_kernel,
        grid_spec=pltpu.PrefetchScalarGridSpec(
            num_scalar_prefetch=1,
            grid=(spans,),
            in_specs=[
                span_x,
                pl.BlockSpec((SPAN, STATE), lambda i, g: (i, g[0])),
                pl.BlockSpec((SPAN, STATE), lambda i, g: (i, g[0] + GROUPS)),
                span_dt,
                const((heads, 1), 0, 0),
                const((KERNEL, width), 0, 0),
                const((1, width), 0, 0),
                pl.BlockSpec((KERNEL, STATE), lambda i, g: (0, g[0])),
                pl.BlockSpec((KERNEL, STATE), lambda i, g: (0, g[0] + GROUPS)),
                pl.BlockSpec((1, STATE), lambda i, g: (0, g[0])),
                pl.BlockSpec((1, STATE), lambda i, g: (0, g[0] + GROUPS)),
                const((8, width), 0, 0),
                const((8, STATE), 0, width // STATE),
                const((8, STATE), 0, width // STATE + 1),
            ],
            out_specs=[
                span_x,
                span_bc,
                span_bc,
                pl.BlockSpec((1, STATE, width), lambda i, *_: (i, 0, 0)),
                const((STATE + EXTRA, width), 0, 0),
                const((STATE, width), 0, 0),
            ],
            scratch_shapes=[
                pltpu.VMEM((8, width), f32),
                pltpu.VMEM((8, STATE), f32),
                pltpu.VMEM((8, STATE), f32),
                pltpu.VMEM((STATE, width), f32),
                pltpu.VMEM((8, width), f32),
            ],
        ),
        out_shape=[
            jax.ShapeDtypeStruct((rows, width), bf16),
            jax.ShapeDtypeStruct((rows, STATE), bf16),
            jax.ShapeDtypeStruct((rows, STATE), bf16),
            jax.ShapeDtypeStruct((spans, STATE, width), bf16),
            jax.ShapeDtypeStruct((STATE + EXTRA, width), bf16),
            jax.ShapeDtypeStruct((STATE, width), f32),
        ],
        compiler_params=params(),
        name="conv_and_states",
    )(
        group[None],
        inner_input, bc_input, bc_input, dt_input, rate,
        conv_weight_x, conv_bias_x[None], conv_weight_bc, conv_weight_bc,
        conv_bias_bc[None], conv_bias_bc[None], halo, halo, halo,
    )

    chained = seq_count == 4 and width % (PARTS * 128) == 0
    local_specs = [
        span_x,
        span_bc,
        span_bc,
        span_dt,
        const((heads, 1), 0, 0),
        const((1, heads), 0, 0),
        pl.BlockSpec((1, STATE, width), lambda i: (i, 0, 0)),
    ]
    local_args = (conv_x, conv_b, conv_c, dt_input, rate, skip_weight[None], enter)
    y_shape = jax.ShapeDtypeStruct((rows, width), f32)
    if chained:
        slots = (PARTS, STATE + EXTRA, width // PARTS)
        y_local, prior = pl.pallas_call(
            chain_kernel,
            grid=(spans,),
            in_specs=local_specs
            + [const((STATE, width), 0, 0), const((STATE + EXTRA, width), 0, 0)],
            out_specs=[span_x, const((STATE + EXTRA, width), 0, 0)],
            out_shape=[y_shape, jax.ShapeDtypeStruct((STATE + EXTRA, width), bf16)],
            scratch_shapes=[
                pltpu.VMEM(slots, bf16),
                pltpu.VMEM(slots, bf16),
                pltpu.SemaphoreType.DMA((PARTS,)),
                pltpu.SemaphoreType.DMA((PARTS,)),
            ],
            compiler_params=pltpu.CompilerParams(
                vmem_limit_bytes=VMEM_LIMIT, collective_id=1, has_side_effects=True
            ),
            name="local_outputs_and_chain",
        )(*local_args, local, sent)
        gathered = prior[None]
    else:
        gathered = lax.all_gather(sent, "seq")
        y_local = pl.pallas_call(
            local_kernel,
            grid=(spans,),
            in_specs=local_specs,
            out_specs=span_x,
            out_shape=y_shape,
            compiler_params=params(),
            name="local_outputs",
        )(*local_args)

    bits = head_count.bit_length() - 1
    distance = jnp.arange(head_count, dtype=jnp.int32) ^ head_index
    slot = jnp.zeros_like(distance)
    for bit in range(bits):
        slot = slot + ((distance >> bit) & 1) * (head_count >> (bit + 1))
    meta = jnp.concatenate([seq_index[None].astype(jnp.int32), slot.astype(jnp.int32) * block])

    normed, boundary = pl.pallas_call(
        functools.partial(
            output_kernel, block=block, halves=1, whole_group=whole_group, chained=chained
        ),
        grid_spec=pltpu.PrefetchScalarGridSpec(
            num_scalar_prefetch=1,
            grid=(spans,),
            in_specs=[
                span_x,
                span_bc,
                span_x,
                span_dt,
                const((heads, 1), 0, 0),
                const((1, width), 0, 0),
                const((gathered.shape[0], STATE + EXTRA, width), 0, 0, 0),
                const((EXTRA, width), STATE // EXTRA, 0),
                const((width, STATE), 0, 0),
                const((STATE, width), 0, 0),
            ],
            out_specs=[const((rows, width), 0, 0), const((width, STATE), 0, 0)],
            scratch_shapes=[
                pltpu.VMEM((STATE, width), f32),
                pltpu.VMEM((STATE, width), bf16),
                pltpu.VMEM((SPAN, width), f32),
                pltpu.VMEM((8, heads), f32),
            ],
        ),
        out_shape=[
            jax.ShapeDtypeStruct((rows, width), bf16 if whole_group else f32),
            jax.ShapeDtypeStruct((width, STATE), f32),
        ],
        compiler_params=params(),
        name="gated_outputs",
    )(
        meta,
        y_local, conv_c, gate_input, dt_input, rate, norm_gain[None], gathered, sent,
        init_state.reshape(width, STATE), local,
    )
    boundary = boundary.reshape(1, heads, HEADDIM, STATE)

    if not whole_group:
        piece = min(width, group_width)
        pieces = normed.reshape(rows, width // piece, piece)
        squares = jnp.sum(pieces * pieces, axis=2).T
        blocks = squares.reshape(squares.shape[0], head_count, block)
        ordered = jnp.take(blocks, slot, axis=1).reshape(squares.shape)
        own = (head_index * (width // piece) + jnp.arange(width // piece)) * piece // group_width
        member = (own[:, None] == jnp.arange(GROUPS)[None, :]).astype(f32)
        totals = lax.psum(jnp.dot(member.T, ordered, precision=highest), "head")
        sums = jnp.dot(member, totals, precision=highest)
        inverse = lax.rsqrt(sums / group_width + norm_eps)
        back = jnp.zeros_like(slot).at[slot].set(jnp.arange(head_count, dtype=slot.dtype))
        inverse = jnp.take(inverse.reshape(blocks.shape), back, axis=1).reshape(squares.shape).T
        normed = (
            (pieces * inverse[:, :, None]).reshape(rows, width) * norm_gain[None, :]
        ).astype(bf16)

    chips = seq_count // 2

    def around(value, by):
        if by % chips == 0:
            return value
        return lax.ppermute(
            value, "seq", [(i, (i + 2 * by) % seq_count) for i in range(seq_count)]
        )

    def across(value, bit):
        return lax.ppermute(
            value, "head", [(i, i ^ (1 << bit)) for i in range(head_count)]
        )

    def reduced(act, weight):
        half = rows // 2
        give = jnp.dot(act[half:], weight, preferred_element_type=f32).astype(bf16)
        keep = jnp.dot(act[:half], weight, preferred_element_type=f32)
        keep = keep + across(give, 0).astype(f32)
        for bit in range(1, bits):
            half = half // 2
            got = across(keep[half:].astype(bf16), bit)
            keep = keep[:half] + got.astype(f32)
        return keep.astype(bf16)

    core = seq_index % 2
    columns = out_weight.shape[1]
    layer_out = jnp.zeros((block, seq_count, columns), bf16)
    acts = [around(normed, by) for by in range(chips)]
    done = [[reduced(act, w) for w in (out_weight, other_core)] for act in acts]
    for by in range(chips):
        mine, other = [around(d, -by) for d in done[by]]
        chip = (seq_index // 2 + by) % chips
        layer_out = lax.dynamic_update_slice(
            layer_out, mine[:, None], (0, chip * 2 + core, 0)
        )
        layer_out = lax.dynamic_update_slice(
            layer_out, other[:, None], (0, chip * 2 + 1 - core, 0)
        )
    return (layer_out.reshape(block, seq_count * columns), boundary)


def solution(mesh):
    in_specs = (
        P("seq", "head"),
        P("seq", "head"),
        P("seq", None),
        P("head", "seq"),
        P("head"),
        P("head"),
        P(None, "head"),
        P("head"),
        P(),
        P(),
        P(None, "head"),
        P(),
        P("head", None, None),
        P("head"),
        P("head", "seq"),
    )
    out_specs = (P(("seq", "head"), None), P("seq", "head", None, None))
    return jax.shard_map(body, mesh=mesh, in_specs=in_specs, out_specs=out_specs, check_vma=False)
```

```python
import functools

import jax
import jax.numpy as jnp
from jax import lax
from jax.experimental import pallas as pl
from jax.experimental.pallas import tpu as pltpu
from jax.sharding import PartitionSpec as P

MIXER_HEADS = 256
HEADDIM = 64
STATE = 256
GROUPS = 8
KERNEL = 4
SPAN = 128
DINNER = 16384
EXTRA = 16
VMEM_LIMIT = 48 * 1024 * 1024
LAYER_LIMIT = 62 * 1024 * 1024

highest = lax.Precision.HIGHEST
norm_eps = 1e-05
f32 = jnp.float32
bf16 = jnp.bfloat16
MESH = pl.DeviceIdType.MESH


def silu(v):
    return v * (1.0 / (1.0 + jnp.exp(-v)))


def shifted(cur, prev8, by):
    moved = pltpu.roll(cur, by, 0)
    before = pltpu.roll(prev8, by, 0)
    row = lax.broadcasted_iota(jnp.int32, before.shape, 0)
    first = jnp.where(row < by, before, moved[:8])
    return jnp.concatenate([first, moved[8:]], axis=0)


def conv_block(in_ref, prev_ref, w_ref, b_ref, out_ref, chunk):
    width = in_ref.shape[1]
    rows = in_ref.shape[0]
    for c in range(0, width, chunk):
        cols = slice(c, c + chunk)
        cur = in_ref[:, cols].astype(f32)
        prev8 = prev_ref[:, cols]
        total = b_ref[:, cols] + w_ref[KERNEL - 1 : KERNEL, cols] * cur
        for by in range(1, KERNEL):
            k = KERNEL - 1 - by
            total = total + w_ref[k : k + 1, cols] * shifted(cur, prev8, by)
        prev_ref[:, cols] = cur[rows - 8 :]
        out_ref[:, cols] = silu(total).astype(bf16)


def spread_matrix(heads):
    h = lax.broadcasted_iota(jnp.int32, (heads, heads * HEADDIM), 0)
    c = lax.broadcasted_iota(jnp.int32, (heads, heads * HEADDIM), 1)
    return jnp.where(c // HEADDIM == h, 1.0, 0.0).astype(f32)


def spread(values, matrix):
    return jnp.dot(values, matrix, precision=highest, preferred_element_type=f32)


def softplus(v):
    e = jnp.exp(-jnp.abs(v))
    u = 1.0 + e
    series = e * (1.0 - e * (0.5 - e * (1.0 / 3.0 - 0.25 * e)))
    return jnp.maximum(v, 0.0) + jnp.where(e < 0.015625, series, jnp.log(u))


def transposed_dot(lhs, rhs):
    return lax.dot_general(
        lhs, rhs, (((1,), (1,)), ((), ())), precision=highest, preferred_element_type=f32
    )


def decay_terms(dt_ref, rate_ref):
    step = softplus(dt_ref[...])
    log = -jnp.exp(rate_ref[...]) * step
    t = lax.broadcasted_iota(jnp.int32, (SPAN, SPAN), 0)
    s = lax.broadcasted_iota(jnp.int32, (SPAN, SPAN), 1)
    lower = jnp.where(t >= s, 1.0, 0.0).astype(f32)
    eye = jnp.where(t == s, 1.0, 0.0).astype(f32)
    cumul_row = transposed_dot(log, lower)
    cumul_col = transposed_dot(lower, log)
    step_col = transposed_dot(eye, step)
    return step, step_col, cumul_row, cumul_col, t >= s


def state_kernel(
    g_ref, inner, bin_, cin, dt, rate, wx, bx, wb, wc, bb, bc, halo_x, halo_b, halo_c,
    x_out, b_out, c_out, enter_out, send_out, local_out,
    prev_x, prev_b, prev_c, state, total,
):
    i = pl.program_id(0)
    heads = dt.shape[0]

    @pl.when(i == 0)
    def _():
        prev_x[...] = halo_x[...].astype(f32)
        prev_b[...] = halo_b[...].astype(f32)
        prev_c[...] = halo_c[...].astype(f32)
        state[...] = jnp.zeros_like(state)
        total[...] = jnp.zeros_like(total)

    conv_block(inner, prev_x, wx, bx, x_out, 256)
    conv_block(bin_, prev_b, wb, bb, b_out, 256)
    conv_block(cin, prev_c, wc, bc, c_out, 256)
    step, step_col, cumul_row, cumul_col, causal = decay_terms(dt, rate)
    last = cumul_col[SPAN - 1 :]
    matrix = spread_matrix(heads)
    weights = spread(jnp.exp(last - cumul_col) * step_col, matrix)
    last8 = spread(jnp.broadcast_to(last, (8, heads)), matrix)
    enter_out[0] = state[...].astype(bf16)
    weighted = (x_out[...].astype(f32) * weights).astype(bf16)
    b_t = b_out[...].astype(f32).T.astype(bf16)
    written = jnp.dot(b_t, weighted, preferred_element_type=f32)
    state[...] = jnp.exp(last8[:1]) * state[...] + written
    total[...] += last8

    @pl.when(i == pl.num_programs(0) - 1)
    def _():
        local_out[...] = state[...]
        send_out[:STATE] = state[...].astype(bf16)
        tl = total[:1]
        high = tl.astype(bf16).astype(f32)
        row = lax.broadcasted_iota(jnp.int32, (EXTRA, tl.shape[1]), 0)
        send_out[STATE:] = jnp.where(row == 0, high, jnp.where(row == 1, tl - high, 0.0)).astype(bf16)


PARTS = 4


def chain_kernel(
    x, b, c, dt, rate, skip, enter, local, sent, y_out, prior_out,
    land, hop, send_sem, recv_sem,
):
    i = pl.program_id(0)
    seq = lax.axis_index("seq")
    last = 3
    wide = land.shape[2]

    def copy(k):
        return pltpu.make_async_remote_copy(
            src_ref=hop.at[k], dst_ref=land.at[k],
            send_sem=send_sem.at[k], recv_sem=recv_sem.at[k],
            device_id={"seq": (seq + 1) % 4}, device_id_type=MESH,
        )

    def joined(k):
        cols = slice(k * wide, (k + 1) * wide)
        own = sent[STATE : STATE + 1, cols].astype(f32) + sent[STATE + 1 : STATE + 2, cols].astype(f32)
        tail = land[k, STATE:].astype(f32)
        hop[k, :STATE] = (
            jnp.exp(own) * land[k, :STATE].astype(f32) + local[:, cols]
        ).astype(bf16)
        log = tail[0:1] + tail[1:2] + own
        high = log.astype(bf16).astype(f32)
        row = lax.broadcasted_iota(jnp.int32, (EXTRA, wide), 0)
        hop[k, STATE:] = jnp.where(row == 0, high, jnp.where(row == 1, log - high, 0.0)).astype(bf16)

    @pl.when(i == 0)
    def _():
        barrier = pltpu.get_barrier_semaphore()

        for by in (1, 3):
            pl.semaphore_signal(
                barrier, inc=1, device_id={"seq": (seq + by) % 4}, device_id_type=MESH
            )
        pl.semaphore_wait(barrier, 2)

        @pl.when(seq == 0)
        def _():
            for k in range(PARTS):
                hop[k] = sent[:, k * wide : (k + 1) * wide]
                copy(k).start()

        @pl.when(seq == 1)
        def _():
            for k in range(PARTS):
                copy(k).wait_recv()
                joined(k)
                copy(k).start()

    local_kernel(x, b, c, dt, rate, skip, enter, y_out)

    @pl.when(i == pl.num_programs(0) - 1)
    def _():
        @pl.when(seq == 2)
        def _():
            for k in range(PARTS):
                copy(k).wait_recv()
                joined(k)
                copy(k).start()

        @pl.when(seq == 3)
        def _():
            for k in range(PARTS):
                copy(k).wait_recv()

        @pl.when(seq > 0)
        def _():
            for k in range(PARTS):
                prior_out[:, k * wide : (k + 1) * wide] = land[k]

        @pl.when(seq == 0)
        def _():
            prior_out[...] = jnp.zeros_like(prior_out)

        @pl.when(seq < last)
        def _():
            for k in range(PARTS):
                copy(k).wait_send()


def local_kernel(x, b, c, dt, rate, skip, enter, y_out):
    heads = dt.shape[0]
    step, step_col, cumul_row, cumul_col, causal = decay_terms(dt, rate)
    matrix = spread_matrix(heads)
    scores = lax.dot_general(
        c[...], b[...], (((1,), (1,)), ((), ())), preferred_element_type=f32
    )
    row_term = jnp.log(step) - cumul_row
    growth = spread(jnp.exp(cumul_col), matrix)
    skip_row = spread(jnp.broadcast_to(skip[...], (8, heads)), matrix)[:1]
    lane = lax.broadcasted_iota(jnp.int32, (SPAN, 2 * HEADDIM), 1)
    zero = jnp.zeros((SPAN, 2 * HEADDIM), bf16)
    for pair in range(heads // 2):
        cols = slice(pair * 2 * HEADDIM, (pair + 1) * 2 * HEADDIM)
        mixers = []
        for h in (2 * pair, 2 * pair + 1):
            power = jnp.where(causal, cumul_col[:, h : h + 1] + row_term[h : h + 1], -1e30)
            mixers.append((scores * jnp.exp(power)).astype(bf16))
        xp = x[:, cols]
        both = jnp.concatenate(
            [jnp.where(lane < HEADDIM, xp, zero), jnp.where(lane >= HEADDIM, xp, zero)], axis=0
        )
        inside = jnp.dot(
            jnp.concatenate(mixers, axis=1), both, preferred_element_type=f32
        )
        carried = jnp.dot(c[...], enter[0, :, cols], preferred_element_type=f32)
        y_out[:, cols] = (
            inside + growth[:, cols] * carried + skip_row[:, cols] * xp.astype(f32)
        )


def output_kernel(
    meta, y, c, gate, dt, rate, gain, gathered, own_tail, init, local, normed_out, boundary_out,
    incoming, entering, mixed, offset, *, block, halves, whole_group, chained,
):
    i = pl.program_id(0)
    heads = dt.shape[0]
    width = y.shape[1]
    count = gathered.shape[0]

    @pl.when(i == 0)
    def _():
        place = meta[0]
        rate_sum = jnp.zeros((1, width), f32)
        incoming[...] = jnp.zeros_like(incoming)
        if chained:
            tail = gathered[0, STATE:].astype(f32)
            incoming[...] = gathered[0, :STATE].astype(f32)
            rate_sum = tail[0:1] + tail[1:2]
        for k in range(-1 if chained else count - 2, -1, -1):
            live = k < place
            tail = gathered[k, STATE:].astype(f32)
            factor = jnp.where(live, jnp.exp(rate_sum), 0.0)
            incoming[...] += factor * gathered[k, :STATE].astype(f32)
            rate_sum = rate_sum + jnp.where(live, tail[0:1] + tail[1:2], 0.0)
        tail = (own_tail[...] if chained else gathered[place, STATE:]).astype(f32)
        own = jnp.exp(tail[0:1] + tail[1:2])
        for k in range(0, width, 256):
            cols = slice(k, k + 256)
            value = incoming[:, cols] + jnp.exp(rate_sum[:, cols]) * init[cols, :].T
            entering[:, cols] = value.astype(bf16)
            boundary_out[cols, :] = (own[:, cols] * value + local[:, cols]).T
        offset[...] = jnp.zeros_like(offset)

    step, step_col, cumul_row, cumul_col, causal = decay_terms(dt, rate)
    cumul_col = cumul_col + offset[:1]
    offset[...] = jnp.broadcast_to(cumul_col[SPAN - 1 :], offset.shape)
    growth = spread(jnp.exp(cumul_col), spread_matrix(heads))
    squares = jnp.zeros((SPAN, 1), f32)
    for k in range(0, width, 256):
        cols = slice(k, k + 256)
        carried = jnp.dot(c[...], entering[:, cols], preferred_element_type=f32)
        value = (y[:, cols] + growth[:, cols] * carried) * silu(gate[:, cols].astype(f32))
        mixed[:, cols] = value
        squares = squares + jnp.sum(value * value, axis=1, keepdims=True)
    if whole_group:
        inverse = lax.rsqrt(squares / width + norm_eps)
    piece = block // halves
    for q in range(SPAN // piece):
        rows = slice(q * piece, (q + 1) * piece)
        first = meta[1 + i * (SPAN // block) + q // halves]
        first = first + (q % halves) * (normed_out.shape[0] // halves)
        value = mixed[rows, :]
        if whole_group:
            value = value * inverse[rows] * gain[...]
        normed_out[pl.ds(pl.multiple_of(first, piece), piece), :] = value.astype(normed_out.dtype)


def partner_of(place, bit):
    size = 1 << bit
    return place + (1 - 2 * ((place // size) % 2)) * size


HALVES = 2
QUARTERS = 4
WIDES = 3
NARROWS = 4
NARROW = 256
ARRIVED = 8
WIDE_Z = (2, 3, 7)
NARROW_Z = (1, 3, 7)
ORDER = (
    130, 131, 1, 129, 2, 5, 33, 3, 34, 163, 0, 161, 37, 65, 66, 4, 32, 256,
    162, 6, 193, 7, 195, 8, 69, 36, 128, 64, 39, 97, 38, 194, 68, 257, 132, 40,
    70, 96, 11, 135, 226, 160, 72, 225, 227, 9, 10, 164, 134, 71, 43, 196, 133, 104,
    192, 41, 167, 75, 228, 98, 35, 42, 103, 73, 224, 166, 74, 102, 100, 107, 165, 101,
    198, 199, 105, 197, 106, 230, 67, 231, 229, 99,
)


def tanh_silu(v):
    half = 0.5 * v
    return half + half * jnp.tanh(half)


def two_terms(values):
    high = values.astype(bf16)
    low = (values - high.astype(f32)).astype(bf16)
    return jnp.concatenate([high, low], axis=1)


def fill_matrix(matrix):
    heads = matrix.shape[0] // 2
    h = lax.broadcasted_iota(jnp.int32, matrix.shape, 0) % heads
    c = lax.broadcasted_iota(jnp.int32, matrix.shape, 1) // HEADDIM
    matrix[...] = jnp.where(c == h, 1.0, 0.0).astype(bf16)


def token_decays(dt, rate):
    step = softplus(dt).T
    log = -jnp.exp(rate) * step
    t = lax.broadcasted_iota(jnp.int32, (SPAN, SPAN), 0)
    s = lax.broadcasted_iota(jnp.int32, (SPAN, SPAN), 1)
    lower = jnp.where(t >= s, 1.0, 0.0).astype(f32)
    cumul = [
        jnp.dot(lower, log[k : k + SPAN], precision=highest, preferred_element_type=f32)
        for k in range(0, log.shape[0], SPAN)
    ]
    return step, cumul, t >= s


def conv_tile(cur, prev8, weight, bias):
    total = bias + weight[KERNEL - 1 : KERNEL] * cur
    for by in range(1, KERNEL):
        k = KERNEL - 1 - by
        total = total + weight[k : k + 1] * shifted(cur, prev8, by)
    return tanh_silu(total).astype(bf16)


def layer_kernel(
    inner, gate_all, bc_all, dt, rate, skip, wx, bx, wbc, bbc, tail_x, tail_bc, init_all, gain, w_own,
    out, state_out,
    x, gate, bc, halo_x, halo_bc, prev, b_t, weight, factors, matrix, scaled, total, state,
    land, hop, left, squares, spread_ahead, weighted_ahead, written_ahead, w, w_last, acts,
    keep, y_send, y_recv, a_send, a_recv, b_send, b_recv, out_held, x_send, x_recv,
    n_keep, ny_send, ny_recv, na_send, na_recv, nb_send, nb_recv, n_held, nx_send, nx_recv,
    in_sem, load_sem, init_sem, halo_send, halo_recv, hop_send, hop_recv, w_sem, w_send, w_recv,
    act_send_sem, act_recv_sem,
    send_sem, recv_sem, out_sem, x_send_sem, x_recv_sem,
    n_send_sem, n_recv_sem, n_out_sem, nx_send_sem, nx_recv_sem,
):
    seq = lax.axis_index("seq")
    head = lax.axis_index("head")
    rows, width = x.shape
    heads = dt.shape[0]
    spans = rows // SPAN
    strip = width // QUARTERS
    wide = w.shape[2]
    columns = w_own.shape[1]
    piece = out.shape[0] // HALVES
    wides = keep.shape[0] // 2
    narrows = n_keep.shape[0] // 2
    other_chip = (seq + 2) % 4
    near = [partner_of(head, bit) for bit in range(3)]
    across = [{"head": place} for place in near]
    over_x = {"seq": other_chip}
    after = {"seq": (seq + 1) % 4}
    other_core = {"seq": partner_of(seq, 0)}
    firsts = [pl.multiple_of((head + g) * STATE, STATE) for g in (0, GROUPS)]
    chunk = 256

    def remote(source, dest, send, recv, target):
        return pltpu.make_async_remote_copy(
            src_ref=source, dst_ref=dest, send_sem=send, recv_sem=recv,
            device_id=target, device_id_type=MESH,
        )

    def strip_of(k):
        return pl.ds(pl.multiple_of(k * strip, strip), strip)

    def inner_copy(k):
        cols = slice(k * strip, (k + 1) * strip)
        return pltpu.make_async_copy(inner.at[:, cols], x.at[:, cols], in_sem.at[k])

    def bc_copy(k):
        return pltpu.make_async_copy(
            bc_all.at[:, pl.ds(firsts[k], STATE)], bc.at[k], load_sem.at[k]
        )

    def gate_copy():
        return pltpu.make_async_copy(gate_all, gate, load_sem.at[2])

    def init_copies():
        place = [(k, r) for k in range(QUARTERS) for r in range(strip // SPAN)]
        return [
            pltpu.make_async_copy(
                init_all.at[k * strip + r * SPAN : k * strip + (r + 1) * SPAN],
                keep.at[k, 0, :, r * STATE : (r + 1) * STATE],
                init_sem.at[k, r],
            )
            for k, r in place
        ]

    def state_copy():
        return pltpu.make_async_copy(state, state_out, load_sem.at[3])

    def own_first():
        return pltpu.make_async_copy(w_own.at[:, :wide], w.at[0], w_sem.at[0])

    def own_second():
        return pltpu.make_async_copy(w_own.at[:, wide:], w_last, w_sem.at[1])

    def other_weights(k):
        narrow = wide // 2
        place = slice(k % 2 * narrow, (k % 2 + 1) * narrow)
        source = w.at[0, :, place] if k < 2 else w_last.at[:, place]
        return remote(
            source, w.at[1 + k // 2, :, place], w_send.at[k], w_recv.at[k], other_core
        )

    def halo_copies():
        last = pl.ds(rows - 16, 16)
        pairs = [(inner.at[last], halo_x)] + [
            (bc_all.at[last, pl.ds(firsts[k], STATE)], halo_bc.at[k]) for k in range(2)
        ]
        return [
            remote(source, dest, halo_send.at[k], halo_recv.at[k], after)
            for k, (source, dest) in enumerate(pairs)
        ]

    def hop_copy(k):
        return remote(hop.at[k], land.at[k], hop_send.at[k], hop_recv.at[k], after)

    def act_copy(half):
        return remote(
            acts.at[0, half], acts.at[1, half], act_send_sem.at[half], act_recv_sem.at[half], over_x
        )

    def chip_copy(k):
        return remote(x_send.at[k], x_recv.at[k], x_send_sem.at[k], x_recv_sem.at[k], over_x)

    def chip_copy_narrow(k):
        return remote(nx_send.at[k], nx_recv.at[k], nx_send_sem.at[k], nx_recv_sem.at[k], over_x)

    def chosen(t, those):
        value = 0
        for k in those:
            value = value + jnp.where(t == k, 1, 0)
        return value

    broad = (
        keep, ((y_send, y_recv), (a_send, a_recv), (b_send, b_recv)), send_sem, recv_sem, WIDE_Z
    )
    slim = (
        n_keep, ((ny_send, ny_recv), (na_send, na_recv), (nb_send, nb_recv)),
        n_send_sem, n_recv_sem, NARROW_Z,
    )

    def head_copy(family, stage, t):
        _, buffers, sent, received, those = family
        source, dest = buffers[stage]
        target = across[2]
        if stage < 2:
            target = {"head": near[stage] + chosen(t, those) * (near[1 - stage] - near[stage])}
        return remote(source.at[t], dest.at[t], sent.at[stage, t], received.at[stage, t], target)

    for k in range(2):
        bc_copy(k).start()
    for k in range(QUARTERS):
        inner_copy(k).start()

    barrier = pltpu.get_barrier_semaphore()
    greeted = across + [over_x, after, {"seq": (seq + 3) % 4}]
    for target in greeted:
        pl.semaphore_signal(barrier, inc=1, device_id=target, device_id_type=MESH)

    own_first().start()
    own_second().start()
    for copy in init_copies():
        copy.start()
    gate_copy().start()

    fill_matrix(matrix)
    step, cumul, causal = token_decays(dt[...], rate[...])
    ends = [value[SPAN - 1 :] for value in cumul]
    later = jnp.zeros_like(ends[0])
    for k in range(spans - 1, -1, -1):
        span = slice(k * SPAN, (k + 1) * SPAN)
        later = later + ends[k]
        weight[span] = two_terms(jnp.exp(later - cumul[k]) * step[span])
    row = lax.broadcasted_iota(jnp.int32, (16, heads), 0)
    high = later.astype(bf16).astype(f32)
    total[...] = two_terms(jnp.where(row < 8, high, later - high))

    pl.semaphore_wait(barrier, len(greeted))

    @pl.when(seq < 3)
    def _():
        for copy in halo_copies():
            copy.start()

    def conv_rows(source, k, cols, before, kernel, bias):
        span = slice(k * SPAN, (k + 1) * SPAN)
        if k:
            before = source[k * SPAN - 16 : k * SPAN, cols].astype(f32)[8:]
        value = conv_tile(source[span, cols].astype(f32), before, kernel, bias)
        source[span, cols] = value
        return value

    def conv_bc(g, k):
        at = pl.ds(firsts[g], STATE)
        before = None if k else prev[:, strip + g * STATE : strip + (g + 1) * STATE]
        return conv_rows(bc.at[g], k, slice(0, STATE), before, wbc[:, at], bbc[:, at])

    def conv_b(k):
        value = conv_bc(0, k)
        b_t[:, k * SPAN : (k + 1) * SPAN] = value.astype(f32).T.astype(bf16)

    for k in range(2):
        bc_copy(k).wait()
    for k in range(spans - 1, 0, -1):
        conv_b(k)

    @pl.when(seq > 0)
    def _():
        for copy in halo_copies():
            copy.wait_recv()
        for g in range(2):
            prev[:, strip + g * STATE : strip + (g + 1) * STATE] = halo_bc[g].astype(f32)[8:]

    @pl.when(seq == 0)
    def _():
        for g in range(2):
            prev[8 - KERNEL + 1 :, strip + g * STATE : strip + (g + 1) * STATE] = tail_bc[
                :, pl.ds(firsts[g], STATE)
            ].astype(f32)
        land[...] = jnp.zeros_like(land)

    conv_b(0)

    def totals(k):
        spread_log = jnp.dot(total[...], matrix[:, strip_of(k)], preferred_element_type=f32)
        return spread_log[0:1] + spread_log[8:9]

    def fill_hop(k, value, log):
        hop[k, :STATE] = value.astype(bf16)
        top = log.astype(bf16).astype(f32)
        line = lax.broadcasted_iota(jnp.int32, (EXTRA, strip), 0)
        hop[k, STATE:] = jnp.where(line == 0, top, jnp.where(line == 1, log - top, 0.0)).astype(bf16)
        hop_copy(k).start()

    def pass_on(k):
        hop_copy(k).wait_recv()
        own = totals(k)
        tail = land[k, STATE:].astype(f32)
        fill_hop(
            k,
            jnp.exp(own) * land[k, :STATE].astype(f32) + state[:, strip_of(k)],
            tail[0:1] + tail[1:2] + own,
        )

    for k in range(QUARTERS):
        inner_copy(k).wait()

    def quarter(q, carry):
        @pl.when(seq > 0)
        def _():
            prev[:, :strip] = halo_x[:, strip_of(q)].astype(f32)[8:]

        @pl.when(seq == 0)
        def _():
            prev[8 - KERNEL + 1 :, :strip] = tail_x[:, strip_of(q)].astype(f32)

        for k in range(spans - 1, -1, -1):
            span = slice(k * SPAN, (k + 1) * SPAN)
            for c in range(0, strip, chunk):
                at = pl.ds(pl.multiple_of(q * strip + c, chunk), chunk)
                value = conv_rows(x, k, at, prev[:, c : c + chunk], wx[:, at], bx[:, at])
                factor = jnp.dot(weight[span], matrix[:, at], preferred_element_type=f32)
                scaled[span, c : c + chunk] = (value.astype(f32) * factor).astype(bf16)
        state[:, strip_of(q)] = jnp.dot(b_t[...], scaled[...], preferred_element_type=f32)

        @pl.when(seq == 0)
        def _():
            fill_hop(q, state[:, strip_of(q)], totals(q))

        @pl.when((seq == 1) & (q > 0))
        def _():
            pass_on(q - 1)

        @pl.when(q == 0)
        def _():
            own_first().wait()

        @pl.when(q == 2)
        def _():
            own_second().wait()

        for k in range(QUARTERS):
            @pl.when(q == k)
            def _():
                other_weights(k).start()

        return carry

    lax.fori_loop(0, QUARTERS, quarter, 0)

    @pl.when(seq == 1)
    def _():
        pass_on(QUARTERS - 1)

    for k in range(spans - 1, -1, -1):
        conv_bc(1, k)

    for k in range(spans):
        middle = 0.5 * ends[k]
        factors[k] = two_terms(
            jnp.concatenate(
                [
                    jnp.exp(cumul[k] - middle),
                    jnp.exp(middle - cumul[k]) * step[k * SPAN : (k + 1) * SPAN],
                    jnp.broadcast_to(jnp.exp(middle), (8, heads)),
                    jnp.broadcast_to(skip[...], (8, heads)),
                ],
                axis=0,
            )
        )

    for i in range(spans):
        span = slice(i * SPAN, (i + 1) * SPAN)
        scores = lax.dot_general(
            bc[1, span], bc[0, span], (((1,), (1,)), ((), ())), preferred_element_type=f32
        )
        left[i, :, :SPAN] = jnp.where(causal, scores, 0.0).astype(bf16)
        left[i, :, SPAN:] = bc[1, span]
    squares[...] = jnp.zeros_like(squares)
    for copy in init_copies():
        copy.wait()
    gate_copy().wait()

    def gated(q, carry):
        cols = strip_of(q)
        for i in range(spans):
            span = slice(i * SPAN, (i + 1) * SPAN)
            spread_ahead[i] = jnp.dot(factors[i], matrix[:, cols], preferred_element_type=f32)
            ahead = (x[span, cols].astype(f32) * spread_ahead[i, SPAN : 2 * SPAN]).astype(bf16)
            weighted_ahead[i] = ahead
            written_ahead[i] = jnp.dot(b_t[:, span], ahead, preferred_element_type=f32)

        @pl.when(seq == 2)
        def _():
            pass_on(q)

        @pl.when(seq == 3)
        def _():
            hop_copy(q).wait_recv()

        tail = land[q, STATE:].astype(f32)
        factor = jnp.exp(tail[0:1] + tail[1:2])
        for r in range(strip // SPAN):
            lanes = slice(r * SPAN, (r + 1) * SPAN)
            at = pl.ds(pl.multiple_of(q * strip + r * SPAN, SPAN), SPAN)
            state[:, at] = (
                land[q, :STATE, lanes].astype(f32)
                + factor[:, lanes] * keep[q, 0, :, r * STATE : (r + 1) * STATE].T
            )
        spot = pl.ds(pl.multiple_of(q % 2 * strip, strip), strip)
        for i in range(spans):
            span = slice(i * SPAN, (i + 1) * SPAN)
            spread_all = spread_ahead[i]
            half_decay = spread_all[2 * SPAN : 2 * SPAN + 1]
            value = x[span, cols].astype(f32)
            before = half_decay * state[:, cols]
            inside = jnp.dot(
                left[i], jnp.concatenate([weighted_ahead[i], before.astype(bf16)], axis=0),
                preferred_element_type=f32,
            )
            state[:, cols] = half_decay * (before + written_ahead[i])
            value = spread_all[:SPAN] * inside + spread_all[2 * SPAN + 8 : 2 * SPAN + 9] * value
            value = value * tanh_silu(gate[span, cols].astype(f32))
            keep[QUARTERS + 2 * i + q // 2, 0, :, spot] = value
            square = value * value
            for c in range(0, strip, 128):
                squares[i] = squares[i] + square[:, c : c + 128]
        return carry

    lax.fori_loop(0, QUARTERS, gated, 0)

    def normalized(half):
        block = HALVES * piece
        for i in range(spans):
            for p in range(SPAN // block):
                first = p * block + half * piece
                lines = slice(first, first + piece)
                inverse = lax.rsqrt(
                    jnp.sum(squares[i, lines], axis=1, keepdims=True) / width + norm_eps
                )
                owner = i * (SPAN // block) + p
                slot = 0
                for bit in range(3):
                    differs = (owner // (1 << bit) + head // (1 << bit)) % 2
                    slot = slot + differs * (4 >> bit)
                place = pl.ds(pl.multiple_of(slot * piece, piece), piece)
                for c in range(width // wide):
                    cols = slice(c * wide, (c + 1) * wide)
                    acts[0, half, place, cols] = (
                        keep[QUARTERS + 2 * i + c, 0, lines, :] * inverse * gain[:, cols]
                    ).astype(bf16)

    for half in range(HALVES):
        normalized(half)
        act_copy(half).start()
    state_copy().start()

    two = 2 * piece

    def send_product(family, t, product):
        held, buffers, _, _, those = family
        near_z = chosen(t, those) == 1
        sending = buffers[0][0]
        middle = [product[:, two : 2 * two], product[:, 2 * two : 3 * two]]
        sending[t, :, :two] = jnp.where(near_z, middle[0], middle[1]).astype(bf16)
        sending[t, :, two:] = product[:, 3 * two :].astype(bf16)
        head_copy(family, 0, t).start()
        held[t, :, :two] = product[:, :two]
        held[t, :, two:] = jnp.where(near_z, middle[1], middle[0])

    def first_stage(family, t):
        held, buffers = family[:2]
        arrived, sending = buffers[0][1], buffers[1][0]
        head_copy(family, 0, t).wait_recv()
        sending[t] = (held[t, :, two:] + arrived[t, :, two:].astype(f32)).astype(bf16)
        head_copy(family, 1, t).start()
        held[t, :, :two] = held[t, :, :two] + arrived[t, :, :two].astype(f32)

    def second_stage(family, t):
        held, buffers = family[:2]
        arrived, sending = buffers[1][1], buffers[2][0]
        head_copy(family, 1, t).wait_recv()
        sending[t] = (held[t, :, piece:two] + arrived[t, :, piece:].astype(f32)).astype(bf16)
        head_copy(family, 2, t).start()
        held[t, :, :piece] = held[t, :, :piece] + arrived[t, :, :piece].astype(f32)

    def third_stage(family, t):
        held, buffers = family[:2]
        head_copy(family, 2, t).wait_recv()
        return (held[t, :, :piece] + buffers[2][1][t].astype(f32)).astype(bf16)

    def wide_out(source, slot, home, t):
        group, half = t % WIDES, (t % wides) // WIDES
        partner = partner_of(home, 0)
        column = jnp.where(group == 0, home, partner) * columns + (group // 2) * wide
        place = pl.ds(pl.multiple_of(half * piece, piece), piece)
        return pltpu.make_async_copy(
            source.at[t], out.at[place, pl.ds(pl.multiple_of(column, wide), wide)], out_sem.at[slot]
        )

    def narrow_out(source, slot, home, t):
        column = home * columns + wide + t * NARROW
        return pltpu.make_async_copy(
            source.at[t], out.at[:, pl.ds(pl.multiple_of(column, NARROW), NARROW)],
            n_out_sem.at[slot],
        )

    def wide_multiply(t):
        place, half, group = t // wides, (t % wides) // WIDES, t % WIDES
        product = jnp.dot(acts[place, half], w[group], preferred_element_type=f32)
        send_product(broad, t, product[None])

    def narrow_multiply(t):
        lines = acts[t // NARROWS].reshape(rows, width)
        cols = pl.ds(pl.multiple_of(t % NARROWS * NARROW, NARROW), NARROW)
        product = jnp.dot(lines, w_last[:, cols], preferred_element_type=f32)
        send_product(slim, t, product.reshape(HALVES, rows // HALVES, NARROW))

    def wide_third(t):
        value = third_stage(broad, t)[0]

        @pl.when(t < wides)
        def _():
            out_held[t] = value
            wide_out(out_held, t, seq, t).start()

        @pl.when(t >= wides)
        def _():
            x_send[t - wides] = value
            chip_copy(t - wides).start()

    def narrow_third(t):
        value = third_stage(slim, t)

        @pl.when(t < NARROWS)
        def _():
            for half in range(HALVES):
                n_held[t, half * piece : (half + 1) * piece] = value[half]
            narrow_out(n_held, t, seq, t).start()

        @pl.when(t >= NARROWS)
        def _():
            for half in range(HALVES):
                nx_send[t - NARROWS, half * piece : (half + 1) * piece] = value[half]
            chip_copy_narrow(t - NARROWS).start()

    handlers = [
        wide_multiply,
        lambda t: first_stage(broad, t),
        lambda t: second_stage(broad, t),
        wide_third,
        narrow_multiply,
        lambda t: first_stage(slim, t),
        lambda t: second_stage(slim, t),
        narrow_third,
        lambda t: act_copy(t).wait_recv(),
    ]
    words = [
        sum(code << (9 * j) for j, code in enumerate(ORDER[k : k + 3]))
        for k in range(0, len(ORDER), 3)
    ]

    def event(i, carry):
        word = 0
        for k, value in enumerate(words):
            word = word + jnp.where(i // 3 == k, value, 0)
        low, mid, top = word % 512, word // 512 % 512, word // 262144
        code = jnp.where(i % 3 == 0, low, jnp.where(i % 3 == 1, mid, top))
        kind, t = code // 32, code % 32
        for k, handler in enumerate(handlers):
            @pl.when(kind == k)
            def _():
                handler(t)

        return carry

    for k in range(QUARTERS):
        other_weights(k).wait_recv()
    lax.fori_loop(0, len(ORDER), event, 0)

    def collect(k, carry):
        chip_copy(k).wait_recv()
        wide_out(x_recv, wides + k, other_chip, k).start()
        return carry

    def collect_narrow(k, carry):
        chip_copy_narrow(k).wait_recv()
        narrow_out(nx_recv, NARROWS + k, other_chip, k).start()
        return carry

    lax.fori_loop(0, wides, collect, 0)
    lax.fori_loop(0, NARROWS, collect_narrow, 0)

    for half in range(HALVES):
        act_copy(half).wait_send()
    for k in range(QUARTERS):
        other_weights(k).wait_send()
    state_copy().wait()

    @pl.when(seq < 3)
    def _():
        for k in range(QUARTERS):
            hop_copy(k).wait_send()
        for copy in halo_copies():
            copy.wait_send()

    def drain(t, carry):
        for stage in range(3):
            head_copy(broad, stage, t).wait_send()
        return carry

    def drain_narrow(t, carry):
        for stage in range(3):
            head_copy(slim, stage, t).wait_send()
        return carry

    def drain_out(k, carry):
        wide_out(out_held, k, seq, k).wait()
        wide_out(x_recv, wides + k, other_chip, k).wait()
        chip_copy(k).wait_send()
        return carry

    def drain_narrow_out(k, carry):
        narrow_out(n_held, k, seq, k).wait()
        narrow_out(nx_recv, NARROWS + k, other_chip, k).wait()
        chip_copy_narrow(k).wait_send()
        return carry

    lax.fori_loop(0, 2 * wides, drain, 0)
    lax.fori_loop(0, 2 * NARROWS, drain_narrow, 0)
    lax.fori_loop(0, wides, drain_out, 0)
    lax.fori_loop(0, NARROWS, drain_narrow_out, 0)


FINISH = 4


def finish_kernel(summed, state, out, boundary_out, sums, columns, rows, sem):
    wide, strip = sums.shape[1] // FINISH, columns.shape[1] // FINISH

    def part(k, step):
        return slice(k * step, (k + 1) * step)

    def copies(k):
        return [
            pltpu.make_async_copy(state.at[:, part(k, strip)], columns.at[:, part(k, strip)], sem.at[0, k]),
            pltpu.make_async_copy(summed.at[:, part(k, wide)], sums.at[:, part(k, wide)], sem.at[1, k]),
            pltpu.make_async_copy(rows.at[part(k, strip)], boundary_out.at[part(k, strip)], sem.at[2, k]),
            pltpu.make_async_copy(sums.at[:, part(k, wide)], out.at[:, part(k, wide)], sem.at[3, k]),
        ]

    for k in range(FINISH):
        for copy in copies(k)[:2]:
            copy.start()
    for k in range(FINISH):
        state_in, sum_in, state_back, sum_back = copies(k)
        state_in.wait()
        rows[part(k, strip)] = columns[:, part(k, strip)].T
        state_back.start()
        sum_in.wait()
        sum_back.start()
    for k in range(FINISH):
        for copy in copies(k)[2:]:
            copy.wait()


def layer(inner, gate, bc, dt, rate, skip, wx, bx, wbc, bbc, tail_x, tail_bc, init, gain, own):
    rows, width = inner.shape
    heads = dt.shape[0]
    columns = own.shape[1]
    strip = width // QUARTERS
    block = rows // 8
    piece = block // HALVES
    wide = columns // 2
    wides = HALVES * WIDES
    half_rows = rows // HALVES
    spans = rows // SPAN
    anywhere = pl.BlockSpec(memory_space=pl.ANY)
    vmem = pl.BlockSpec(memory_space=pltpu.VMEM)
    slots = (QUARTERS, STATE + EXTRA, strip)
    dma = pltpu.SemaphoreType.DMA
    summed, state = pl.pallas_call(
        layer_kernel,
        in_specs=[anywhere] * 3 + [vmem] * 9 + [anywhere, vmem, anywhere],
        out_specs=[anywhere, anywhere],
        out_shape=[
            jax.ShapeDtypeStruct((block, 4 * columns), bf16),
            jax.ShapeDtypeStruct((STATE, width), f32),
        ],
        scratch_shapes=[
            pltpu.VMEM((rows, width), bf16),
            pltpu.VMEM((rows, width), bf16),
            pltpu.VMEM((2, rows, STATE), bf16),
            pltpu.VMEM((16, width), bf16),
            pltpu.VMEM((2, 16, STATE), bf16),
            pltpu.VMEM((8, strip + 2 * STATE), f32),
            pltpu.VMEM((STATE, rows), bf16),
            pltpu.VMEM((rows, 2 * heads), bf16),
            pltpu.VMEM((spans, 2 * SPAN + 16, 2 * heads), bf16),
            pltpu.VMEM((2 * heads, width), bf16),
            pltpu.VMEM((rows, strip), bf16),
            pltpu.VMEM((16, 2 * heads), bf16),
            pltpu.VMEM((STATE, width), f32),
            pltpu.VMEM(slots, bf16),
            pltpu.VMEM(slots, bf16),
            pltpu.VMEM((spans, SPAN, SPAN + STATE), bf16),
            pltpu.VMEM((spans, SPAN, 128), f32),
            pltpu.VMEM((spans, 2 * SPAN + 16, strip), f32),
            pltpu.VMEM((spans, SPAN, strip), bf16),
            pltpu.VMEM((spans, STATE, strip), f32),
            pltpu.VMEM((WIDES, width, wide), bf16),
            pltpu.VMEM((width, wide), bf16),
            pltpu.VMEM((2, HALVES, half_rows, width), bf16),
            pltpu.VMEM((2 * wides, 1, 4 * piece, wide), f32),
            pltpu.VMEM((2 * wides, 1, 4 * piece, wide), bf16),
            pltpu.VMEM((2 * wides, 1, 4 * piece, wide), bf16),
            pltpu.VMEM((2 * wides, 1, 2 * piece, wide), bf16),
            pltpu.VMEM((2 * wides, 1, 2 * piece, wide), bf16),
            pltpu.VMEM((2 * wides, 1, piece, wide), bf16),
            pltpu.VMEM((2 * wides, 1, piece, wide), bf16),
            pltpu.VMEM((wides, piece, wide), bf16),
            pltpu.VMEM((wides, piece, wide), bf16),
            pltpu.VMEM((wides, piece, wide), bf16),
            pltpu.VMEM((2 * NARROWS, HALVES, 4 * piece, NARROW), f32),
            pltpu.VMEM((2 * NARROWS, HALVES, 4 * piece, NARROW), bf16),
            pltpu.VMEM((2 * NARROWS, HALVES, 4 * piece, NARROW), bf16),
            pltpu.VMEM((2 * NARROWS, HALVES, 2 * piece, NARROW), bf16),
            pltpu.VMEM((2 * NARROWS, HALVES, 2 * piece, NARROW), bf16),
            pltpu.VMEM((2 * NARROWS, HALVES, piece, NARROW), bf16),
            pltpu.VMEM((2 * NARROWS, HALVES, piece, NARROW), bf16),
            pltpu.VMEM((NARROWS, block, NARROW), bf16),
            pltpu.VMEM((NARROWS, block, NARROW), bf16),
            pltpu.VMEM((NARROWS, block, NARROW), bf16),
            dma((QUARTERS,)),
            dma((4,)),
            dma((QUARTERS, strip // SPAN)),
            dma((3,)),
            dma((3,)),
            dma((QUARTERS,)),
            dma((QUARTERS,)),
            dma((2,)),
            dma((QUARTERS,)),
            dma((QUARTERS,)),
            dma((HALVES,)),
            dma((HALVES,)),
            dma((3, 2 * wides)),
            dma((3, 2 * wides)),
            dma((2 * wides,)),
            dma((wides,)),
            dma((wides,)),
            dma((3, 2 * NARROWS)),
            dma((3, 2 * NARROWS)),
            dma((2 * NARROWS,)),
            dma((NARROWS,)),
            dma((NARROWS,)),
        ],
        compiler_params=pltpu.CompilerParams(
            vmem_limit_bytes=LAYER_LIMIT, collective_id=0, has_side_effects=True
        ),
        name="layer",
    )(
        inner, gate, bc, dt, rate[None], skip[None], wx, bx[None], wbc, bbc[None], tail_x, tail_bc,
        init.reshape(width, STATE), gain[None], own,
    )
    return pl.pallas_call(
        finish_kernel,
        in_specs=[anywhere, anywhere],
        out_specs=[anywhere, anywhere],
        out_shape=[
            jax.ShapeDtypeStruct((block, 4 * columns), bf16),
            jax.ShapeDtypeStruct((width, STATE), f32),
        ],
        scratch_shapes=[
            pltpu.VMEM((block, 4 * columns), bf16),
            pltpu.VMEM((STATE, width), f32),
            pltpu.VMEM((width, STATE), f32),
            dma((4, FINISH)),
        ],
        compiler_params=pltpu.CompilerParams(vmem_limit_bytes=LAYER_LIMIT),
        name="finish",
    )(summed, state)


def params():
    return pltpu.CompilerParams(vmem_limit_bytes=VMEM_LIMIT)


def body(
    inner_input,
    gate_input,
    bc_input,
    dt_input,
    log_rate,
    skip_weight,
    conv_weight_x,
    conv_bias_x,
    conv_weight_bc,
    conv_bias_bc,
    conv_tail_x,
    conv_tail_bc,
    init_state,
    norm_gain,
    out_weight,
):
    seq_count = lax.axis_size("seq")
    head_count = lax.axis_size("head")
    seq_index = lax.axis_index("seq")
    head_index = lax.axis_index("head")
    rows, width = inner_input.shape
    heads = dt_input.shape[0]
    per_group = MIXER_HEADS // GROUPS
    group = (head_index * heads // per_group).astype(jnp.int32)
    spans = rows // SPAN
    block = rows // head_count
    group_width = DINNER // GROUPS
    whole_group = width == group_width

    projected = (
        seq_count == 4 and head_count == 8 and whole_group and rows == 512 and width == 2048
        and out_weight.shape[1] % 512 == 0
    )
    if projected:
        out, boundary = layer(
            inner_input, gate_input, bc_input, dt_input, log_rate, skip_weight, conv_weight_x,
            conv_bias_x, conv_weight_bc, conv_bias_bc, conv_tail_x, conv_tail_bc, init_state,
            norm_gain, out_weight,
        )
        return (out, boundary.reshape(1, heads, HEADDIM, STATE))

    other_core = lax.ppermute(out_weight, "seq", [(i, i ^ 1) for i in range(seq_count)])

    def pair_columns(table, axis):
        return [
            lax.dynamic_slice_in_dim(table, (g + group) * STATE, STATE, axis) for g in (0, GROUPS)
        ]

    tail_rows = rows - KERNEL + 1
    last_rows = jnp.concatenate(
        [inner_input[tail_rows:]] + pair_columns(bc_input[tail_rows:], 1), axis=1
    )
    arrived = lax.ppermute(last_rows, "seq", [(i, i + 1) for i in range(seq_count - 1)])
    first_rows = jnp.concatenate([conv_tail_x] + pair_columns(conv_tail_bc, 1), axis=1)
    halo = jnp.where(seq_index == 0, first_rows, arrived)
    halo = jnp.pad(halo, ((8 - KERNEL + 1, 0), (0, 0)))
    rate = log_rate[:, None]

    def const(shape, *index):
        return pl.BlockSpec(shape, lambda i, *_: index)

    span_x = pl.BlockSpec((SPAN, width), lambda i, *_: (i, 0))
    span_bc = pl.BlockSpec((SPAN, STATE), lambda i, *_: (i, 0))
    span_dt = pl.BlockSpec((heads, SPAN), lambda i, *_: (0, i))

    conv_x, conv_b, conv_c, enter, sent, local = pl.pallas_call(
        state_kernel,
        grid_spec=pltpu.PrefetchScalarGridSpec(
            num_scalar_prefetch=1,
            grid=(spans,),
            in_specs=[
                span_x,
                pl.BlockSpec((SPAN, STATE), lambda i, g: (i, g[0])),
                pl.BlockSpec((SPAN, STATE), lambda i, g: (i, g[0] + GROUPS)),
                span_dt,
                const((heads, 1), 0, 0),
                const((KERNEL, width), 0, 0),
                const((1, width), 0, 0),
                pl.BlockSpec((KERNEL, STATE), lambda i, g: (0, g[0])),
                pl.BlockSpec((KERNEL, STATE), lambda i, g: (0, g[0] + GROUPS)),
                pl.BlockSpec((1, STATE), lambda i, g: (0, g[0])),
                pl.BlockSpec((1, STATE), lambda i, g: (0, g[0] + GROUPS)),
                const((8, width), 0, 0),
                const((8, STATE), 0, width // STATE),
                const((8, STATE), 0, width // STATE + 1),
            ],
            out_specs=[
                span_x,
                span_bc,
                span_bc,
                pl.BlockSpec((1, STATE, width), lambda i, *_: (i, 0, 0)),
                const((STATE + EXTRA, width), 0, 0),
                const((STATE, width), 0, 0),
            ],
            scratch_shapes=[
                pltpu.VMEM((8, width), f32),
                pltpu.VMEM((8, STATE), f32),
                pltpu.VMEM((8, STATE), f32),
                pltpu.VMEM((STATE, width), f32),
                pltpu.VMEM((8, width), f32),
            ],
        ),
        out_shape=[
            jax.ShapeDtypeStruct((rows, width), bf16),
            jax.ShapeDtypeStruct((rows, STATE), bf16),
            jax.ShapeDtypeStruct((rows, STATE), bf16),
            jax.ShapeDtypeStruct((spans, STATE, width), bf16),
            jax.ShapeDtypeStruct((STATE + EXTRA, width), bf16),
            jax.ShapeDtypeStruct((STATE, width), f32),
        ],
        compiler_params=params(),
        name="conv_and_states",
    )(
        group[None],
        inner_input, bc_input, bc_input, dt_input, rate,
        conv_weight_x, conv_bias_x[None], conv_weight_bc, conv_weight_bc,
        conv_bias_bc[None], conv_bias_bc[None], halo, halo, halo,
    )

    chained = seq_count == 4 and width % (PARTS * 128) == 0
    local_specs = [
        span_x,
        span_bc,
        span_bc,
        span_dt,
        const((heads, 1), 0, 0),
        const((1, heads), 0, 0),
        pl.BlockSpec((1, STATE, width), lambda i: (i, 0, 0)),
    ]
    local_args = (conv_x, conv_b, conv_c, dt_input, rate, skip_weight[None], enter)
    y_shape = jax.ShapeDtypeStruct((rows, width), f32)
    if chained:
        slots = (PARTS, STATE + EXTRA, width // PARTS)
        y_local, prior = pl.pallas_call(
            chain_kernel,
            grid=(spans,),
            in_specs=local_specs
            + [const((STATE, width), 0, 0), const((STATE + EXTRA, width), 0, 0)],
            out_specs=[span_x, const((STATE + EXTRA, width), 0, 0)],
            out_shape=[y_shape, jax.ShapeDtypeStruct((STATE + EXTRA, width), bf16)],
            scratch_shapes=[
                pltpu.VMEM(slots, bf16),
                pltpu.VMEM(slots, bf16),
                pltpu.SemaphoreType.DMA((PARTS,)),
                pltpu.SemaphoreType.DMA((PARTS,)),
            ],
            compiler_params=pltpu.CompilerParams(
                vmem_limit_bytes=VMEM_LIMIT, collective_id=1, has_side_effects=True
            ),
            name="local_outputs_and_chain",
        )(*local_args, local, sent)
        gathered = prior[None]
    else:
        gathered = lax.all_gather(sent, "seq")
        y_local = pl.pallas_call(
            local_kernel,
            grid=(spans,),
            in_specs=local_specs,
            out_specs=span_x,
            out_shape=y_shape,
            compiler_params=params(),
            name="local_outputs",
        )(*local_args)

    bits = head_count.bit_length() - 1
    distance = jnp.arange(head_count, dtype=jnp.int32) ^ head_index
    slot = jnp.zeros_like(distance)
    for bit in range(bits):
        slot = slot + ((distance >> bit) & 1) * (head_count >> (bit + 1))
    meta = jnp.concatenate([seq_index[None].astype(jnp.int32), slot.astype(jnp.int32) * block])

    normed, boundary = pl.pallas_call(
        functools.partial(
            output_kernel, block=block, halves=1, whole_group=whole_group, chained=chained
        ),
        grid_spec=pltpu.PrefetchScalarGridSpec(
            num_scalar_prefetch=1,
            grid=(spans,),
            in_specs=[
                span_x,
                span_bc,
                span_x,
                span_dt,
                const((heads, 1), 0, 0),
                const((1, width), 0, 0),
                const((gathered.shape[0], STATE + EXTRA, width), 0, 0, 0),
                const((EXTRA, width), STATE // EXTRA, 0),
                const((width, STATE), 0, 0),
                const((STATE, width), 0, 0),
            ],
            out_specs=[const((rows, width), 0, 0), const((width, STATE), 0, 0)],
            scratch_shapes=[
                pltpu.VMEM((STATE, width), f32),
                pltpu.VMEM((STATE, width), bf16),
                pltpu.VMEM((SPAN, width), f32),
                pltpu.VMEM((8, heads), f32),
            ],
        ),
        out_shape=[
            jax.ShapeDtypeStruct((rows, width), bf16 if whole_group else f32),
            jax.ShapeDtypeStruct((width, STATE), f32),
        ],
        compiler_params=params(),
        name="gated_outputs",
    )(
        meta,
        y_local, conv_c, gate_input, dt_input, rate, norm_gain[None], gathered, sent,
        init_state.reshape(width, STATE), local,
    )
    boundary = boundary.reshape(1, heads, HEADDIM, STATE)

    if not whole_group:
        piece = min(width, group_width)
        pieces = normed.reshape(rows, width // piece, piece)
        squares = jnp.sum(pieces * pieces, axis=2).T
        blocks = squares.reshape(squares.shape[0], head_count, block)
        ordered = jnp.take(blocks, slot, axis=1).reshape(squares.shape)
        own = (head_index * (width // piece) + jnp.arange(width // piece)) * piece // group_width
        member = (own[:, None] == jnp.arange(GROUPS)[None, :]).astype(f32)
        totals = lax.psum(jnp.dot(member.T, ordered, precision=highest), "head")
        sums = jnp.dot(member, totals, precision=highest)
        inverse = lax.rsqrt(sums / group_width + norm_eps)
        back = jnp.zeros_like(slot).at[slot].set(jnp.arange(head_count, dtype=slot.dtype))
        inverse = jnp.take(inverse.reshape(blocks.shape), back, axis=1).reshape(squares.shape).T
        normed = (
            (pieces * inverse[:, :, None]).reshape(rows, width) * norm_gain[None, :]
        ).astype(bf16)

    chips = seq_count // 2

    def around(value, by):
        if by % chips == 0:
            return value
        return lax.ppermute(
            value, "seq", [(i, (i + 2 * by) % seq_count) for i in range(seq_count)]
        )

    def across(value, bit):
        return lax.ppermute(
            value, "head", [(i, i ^ (1 << bit)) for i in range(head_count)]
        )

    def reduced(act, weight):
        half = rows // 2
        give = jnp.dot(act[half:], weight, preferred_element_type=f32).astype(bf16)
        keep = jnp.dot(act[:half], weight, preferred_element_type=f32)
        keep = keep + across(give, 0).astype(f32)
        for bit in range(1, bits):
            half = half // 2
            got = across(keep[half:].astype(bf16), bit)
            keep = keep[:half] + got.astype(f32)
        return keep.astype(bf16)

    core = seq_index % 2
    columns = out_weight.shape[1]
    layer_out = jnp.zeros((block, seq_count, columns), bf16)
    acts = [around(normed, by) for by in range(chips)]
    done = [[reduced(act, w) for w in (out_weight, other_core)] for act in acts]
    for by in range(chips):
        mine, other = [around(d, -by) for d in done[by]]
        chip = (seq_index // 2 + by) % chips
        layer_out = lax.dynamic_update_slice(
            layer_out, mine[:, None], (0, chip * 2 + core, 0)
        )
        layer_out = lax.dynamic_update_slice(
            layer_out, other[:, None], (0, chip * 2 + 1 - core, 0)
        )
    return (layer_out.reshape(block, seq_count * columns), boundary)


def solution(mesh):
    in_specs = (
        P("seq", "head"),
        P("seq", "head"),
        P("seq", None),
        P("head", "seq"),
        P("head"),
        P("head"),
        P(None, "head"),
        P("head"),
        P(),
        P(),
        P(None, "head"),
        P(),
        P("head", None, None),
        P("head"),
        P("head", "seq"),
    )
    out_specs = (P(("seq", "head"), None), P("seq", "head", None, None))
    return jax.shard_map(body, mesh=mesh, in_specs=in_specs, out_specs=out_specs, check_vma=False)
```
